256 devices in a mesh: ma: 64 (over y, z, core), vert: 4 (over x).
Axes of the slice: x: 4, y: 4, z: 8, core: 2. Of those that a mesh axis runs over, the one named last changes fastest.
Arguments:
- trial_block: bfloat16 [128, 512, 4, 1024], P('vert', 'ma'), may hold values from -6 to 6
- legendre: bfloat16 [512, 2, 256, 1024], P('ma'), may hold values from -0.1875 to 0.1875
- order_slot: int32 [512], replicated, may hold values from 0 to 511, each once
- cycle_start: int32 [256], replicated, may hold values from 0 to 1023
- cycle_count: int32 [256], replicated, may hold values from 0 to 1024, as said below
- cycle_weight: float32 [256], replicated, may hold values from 4 to 32
Outputs:
- new_basis: bfloat16 [128, 512, 4, 1024], P('vert', 'ma')
- ritz_matrix: float32 [128, 128], replicated
The draws below stay inside these ranges and needn't reach their ends.
Inputs may be any that keep to these rules, and one draw needn't show every extreme that they name: `cycle_count`: exactly 64 consecutive cycles have a nonzero count, and one of them has 1024.
All inputs are finite; a program needn't handle non-finite values.
Results may differ from the reference program's by a relative error of at most 0.0073.
The reference program's roundings to bfloat16 on the way (of `fields`, `weighted`, `returned`, `adjoint`, `applied` and `mixing`) count: a program that leaves them out, or rounds other values in their place, can miss the bound.
Values may be sent and summed in bfloat16 or wider, within the bound.
No kernel may reach another device: no remote copies, remote signals or barrier semaphores. Data moves between devices by JAX's collectives and lax.ppermute only.
A program may use at most 192 MiB of HBM per device.

```python
import math
import jax
import jax.numpy as jnp
from jax import lax

LDEG = 1024
ORDERS = 512
CYCLES = 256
LIVE = 64
NLON = 1024
K = 128
NC = 2097152


def draw_cycle_count(key, part):
    keys = jax.random.split(jax.random.fold_in(key, 11), 3)
    band_start = jax.random.randint(keys[0], (), 0, CYCLES - LIVE + 1)
    counts = jax.random.randint(keys[1], (CYCLES,), 1, NLON + 1)
    full_cycle = jax.random.randint(keys[2], (), 0, LIVE)
    cycle_index = jnp.arange(CYCLES)
    inside = (cycle_index >= band_start) & (cycle_index < band_start + LIVE)
    counts = jnp.where(cycle_index == band_start + full_cycle, NLON, counts)
    return jnp.where(inside, counts, 0).astype(jnp.int32)


def set_ends(values, rng, smallest, high):
    index_at = [jax.random.randint(jax.random.fold_in(rng, axis), (), 0, length) for axis, length in enumerate(values.shape)]
    main_axis = values.shape.index(max(values.shape))
    next_to = index_at[:main_axis] + [(index_at[main_axis] + 1) % values.shape[main_axis]] + index_at[main_axis + 1:]
    return values.at[tuple(index_at)].set(smallest).at[tuple(next_to)].set(high)


def block_scale(key, shape, cuts, smallest, largest):
    loudness, own = 1.0, jax.random.fold_in(key, 6)
    for axis_at, parts in cuts:
        draws = jnp.exp(jax.random.uniform(jax.random.fold_in(own, axis_at), (parts,), jnp.float32, smallest / len(cuts), largest / len(cuts)))
        loudness = loudness * jnp.repeat(draws, shape[axis_at] // parts).reshape([-1 if axis == axis_at else 1 for axis in range(len(shape))])
    return loudness


def bell_draw(key, extent, width, limit, cuts=(), kind=jnp.bfloat16):
    array = width * jax.random.normal(key, extent, jnp.float32)
    if cuts:
        array = array * block_scale(key, extent, cuts, -0.22, 0.18)
    return jnp.clip(array, -limit, limit).astype(kind)


def setup_inputs(seed: int = 0) -> dict:
    key_list = jax.random.split(jax.random.key(seed), 7)
    return {
        "trial_block": bell_draw(key_list[0], (K, ORDERS, 4, LDEG), 1.0, 6.0, ((0, 4), (1, 64))),
        "legendre": bell_draw(key_list[1], (ORDERS, 2, CYCLES, LDEG), LDEG ** -0.5, 0.1875, ((0, 64),)),
        "order_slot": jax.random.permutation(key_list[2], ORDERS).astype(jnp.int32),
        "cycle_start": set_ends(jax.random.randint(key_list[3], (CYCLES,), 0, NLON), jax.random.fold_in(key_list[3], 1), 0, NLON - 1).astype(jnp.int32),
        "cycle_count": draw_cycle_count(jax.random.fold_in(key_list[6], 71), 0),
        "cycle_weight": jnp.clip(jnp.exp(jax.random.uniform(key_list[5], (CYCLES,), jnp.float32, math.log(4.0), math.log(32.0))), 4.0, 32.0),
    }


def combine_fields(products):
    first_kind = products[:, 0]
    second_kind = products[:, 1]
    return jnp.stack([first_kind[..., 0] + second_kind[..., 3], first_kind[..., 1] - second_kind[..., 2], second_kind[..., 1] - first_kind[..., 2], -second_kind[..., 0] - first_kind[..., 3]], axis=-1)

def adjoint_terms(returned):
    gtc = returned[..., 0]
    gts = returned[..., 1]
    gpc = returned[..., 2]
    gps = returned[..., 3]
    first_kind = jnp.stack([gtc, gts, -gpc, -gps], axis=-1)
    second_kind = jnp.stack([-gps, gpc, -gts, gtc], axis=-1)
    return jnp.stack([first_kind, second_kind], axis=1)

def fourier_tables(order_slot, longitudes, orders_total):
    longitude = jnp.arange(longitudes, dtype=jnp.int32)
    phases = longitude[:, None] * order_slot[None, :].astype(jnp.int32) % longitudes
    angles = phases.astype(jnp.float32) * (2.0 * math.pi / longitudes)
    scale = 1.0 / math.sqrt(orders_total)
    return ((jnp.cos(angles) * scale).astype(jnp.bfloat16), (jnp.sin(angles) * scale).astype(jnp.bfloat16))

def finish_ritz(gram_trial, cross, gram_applied):
    factor_trial = jnp.linalg.cholesky(gram_trial)
    half_solved = lax.linalg.triangular_solve(factor_trial, cross, left_side=True, lower=True)
    ritz_matrix = lax.linalg.triangular_solve(factor_trial, half_solved.T, left_side=True, lower=True).T
    factor_applied = jnp.linalg.cholesky(gram_applied)
    identity = jnp.eye(gram_applied.shape[0], dtype=gram_applied.dtype)
    mixing = lax.linalg.triangular_solve(factor_applied, identity, left_side=True, lower=True)
    return (ritz_matrix, mixing.astype(jnp.bfloat16))

def reference(trial_block, legendre, order_slot, cycle_start, cycle_count, cycle_weight):
    highest = lax.Precision.HIGHEST
    block = trial_block.astype(jnp.float32)
    table = legendre.astype(jnp.float32)
    products = lax.dot_general(table, block, (((3,), (3,)), ((0,), (1,))), precision=highest)
    fields = combine_fields(products).astype(jnp.bfloat16)
    cosine, sines = fourier_tables(order_slot, NLON, ORDERS)
    cosine_wide = cosine.astype(jnp.float32)
    sines_wide = sines.astype(jnp.float32)
    pieces = fields.astype(jnp.float32)
    grid_values = jnp.einsum('jo,orkc->rckj', cosine_wide, pieces[..., 0::2], precision=highest)
    grid_values = grid_values + jnp.einsum('jo,orkc->rckj', sines_wide, pieces[..., 1::2], precision=highest)
    longitude = jnp.arange(NLON, dtype=jnp.int32)
    inside = ((longitude[None, :] - cycle_start[:, None]) % NLON < cycle_count[:, None]).astype(jnp.float32)
    factor = inside * cycle_weight[:, None].astype(jnp.float32)
    weighted = (grid_values * factor[:, None, None, :]).astype(jnp.bfloat16).astype(jnp.float32)
    back_cos = jnp.einsum('jo,rckj->orkc', cosine_wide, weighted, precision=highest)
    back_sin = jnp.einsum('jo,rckj->orkc', sines_wide, weighted, precision=highest)
    returned = jnp.stack([back_cos[..., 0], back_sin[..., 0], back_cos[..., 1], back_sin[..., 1]], axis=-1).astype(jnp.bfloat16)
    adjoint = adjoint_terms(returned).astype(jnp.float32)
    adjoint = adjoint.reshape(ORDERS, 2, CYCLES, K * 4)
    applied = lax.dot_general(adjoint, table, (((1, 2), (1, 2)), ((0,), (0,))), precision=highest)
    applied = applied.reshape(ORDERS, K, 4, LDEG).transpose(1, 0, 2, 3).astype(jnp.bfloat16)
    trial_flat = trial_block.reshape(K, NC)
    applied_flat = applied.reshape(K, NC)
    gram_trial = jnp.dot(trial_flat.astype(jnp.float32), trial_flat.T.astype(jnp.float32), preferred_element_type=jnp.float32) / NC
    cross = jnp.dot(trial_flat.astype(jnp.float32), applied_flat.T.astype(jnp.float32), preferred_element_type=jnp.float32) / NC
    gram_applied = jnp.dot(applied_flat.astype(jnp.float32), applied_flat.T.astype(jnp.float32), preferred_element_type=jnp.float32) / NC
    ritz_matrix, mixing = finish_ritz(gram_trial, cross, gram_applied)
    new_basis = jnp.dot(mixing.astype(jnp.float32), applied_flat.astype(jnp.float32), preferred_element_type=jnp.float32)
    new_basis = new_basis.reshape(K, ORDERS, 4, LDEG).astype(jnp.bfloat16)
    return (new_basis, ritz_matrix)
```

```python
import functools
import math

import jax
import jax.numpy as jnp
from jax import lax
from jax.experimental import pallas as pl
from jax.experimental.pallas import tpu as pltpu
from jax.sharding import Mesh
from jax.sharding import PartitionSpec as P

MA = ("ma_0", "ma_1", "ma_2")
ALL = MA + ("vert",)
F32 = jnp.float32
BF16 = jnp.bfloat16
WINDOW = 80
NT = (((1,), (1,)), ((), ()))
NN = (((1,), (0,)), ((), ()))


def ring(size, shift):
    return [(i, (i + shift) % size) for i in range(size)]


def dot(a, b, dims=NN):
    return lax.dot_general(a, b, dims, preferred_element_type=F32)


def dot_high(a, b, dims=NN):
    return lax.dot_general(
        a, b, dims, precision=lax.Precision.HIGHEST, preferred_element_type=F32
    )


def window_copy(legendre, leg_v, sem, s, start):
    return pltpu.make_async_copy(
        legendre.at[s, :, pl.ds(start, WINDOW), :], leg_v.at[s], sem.at[s]
    )


def synthesize_kernel(
    where, trial, legendre, fields, tt, tr_v, leg_v, tt_v, prod, sem_t, sem_l, sem_o
):
    orders = trial.shape[1]
    vectors = trial.shape[0]
    start = pl.multiple_of(where[0], 16)
    shift = where[1]
    for s in range(orders):
        pltpu.make_async_copy(trial.at[:, s], tr_v.at[s], sem_t.at[s]).start()
        window_copy(legendre, leg_v, sem_l, s, start).start()
    rows = 4 * vectors
    i = lax.broadcasted_iota(jnp.int32, (rows, rows), 0)
    j = lax.broadcasted_iota(jnp.int32, (rows, rows), 1)
    by_part = (j == (i % vectors) * 4 + i // vectors).astype(BF16)
    for s in range(orders):
        pltpu.make_async_copy(trial.at[:, s], tr_v.at[s], sem_t.at[s]).wait()
        x = tr_v[s].reshape(rows, tr_v.shape[3])
        t = dot(by_part, x).astype(BF16)
        t0, t1, t2, t3 = (t[c * vectors : (c + 1) * vectors] for c in range(4))
        for c, part in enumerate((t0, t1, t2, t3)):
            tt_v[s, c] = part
        pltpu.make_async_copy(tt_v.at[s], tt.at[s], sem_o.at[s]).start()
        first_kind = jnp.concatenate([t0, t1, -t3, -t2], axis=0)
        second_kind = jnp.concatenate([t3, -t2, -t0, t1], axis=0)
        window_copy(legendre, leg_v, sem_l, s, start).wait()
        prod[s * WINDOW : (s + 1) * WINDOW] = dot(leg_v[s, 0], first_kind, NT) + dot(
            leg_v[s, 1], second_kind, NT
        )
    for r in range(fields.shape[0]):
        fields[r] = prod[pl.ds(shift + r, orders, stride=WINDOW), :].astype(BF16)
    for s in range(orders):
        pltpu.make_async_copy(tt_v.at[s], tt.at[s], sem_o.at[s]).wait()


def synthesize(where, trial, legendre, cycles):
    vectors, orders, _, degrees = trial.shape
    return pl.pallas_call(
        synthesize_kernel,
        out_shape=(
            jax.ShapeDtypeStruct((cycles, orders, 4 * vectors), BF16),
            jax.ShapeDtypeStruct((orders, 4, vectors, degrees), BF16),
        ),
        in_specs=[
            pl.BlockSpec(memory_space=pltpu.SMEM),
            pl.BlockSpec(memory_space=pl.ANY),
            pl.BlockSpec(memory_space=pl.ANY),
        ],
        out_specs=(
            pl.BlockSpec(memory_space=pltpu.VMEM),
            pl.BlockSpec(memory_space=pl.ANY),
        ),
        scratch_shapes=[
            pltpu.VMEM((orders, vectors, 4, degrees), BF16),
            pltpu.VMEM((orders, 2, WINDOW, degrees), BF16),
            pltpu.VMEM((orders, 4, vectors, degrees), BF16),
            pltpu.VMEM((orders * WINDOW, 4 * vectors), F32),
            pltpu.SemaphoreType.DMA((orders,)),
            pltpu.SemaphoreType.DMA((orders,)),
            pltpu.SemaphoreType.DMA((orders,)),
        ],
        compiler_params=pltpu.CompilerParams(vmem_limit_bytes=40 << 20),
        cost_estimate=pl.CostEstimate(
            flops=600_000_000, bytes_accessed=8 << 20, transcendentals=0
        ),
        name="synthesize",
    )(where, trial, legendre)


def tables_kernel(slot, cosine, sines):
    orders, longitudes = cosine.shape
    lanes = 128
    scale = 1.0 / math.sqrt(orders)
    step = 2.0 * math.pi / longitudes
    m = slot[...]
    near = lax.broadcasted_iota(jnp.int32, (orders, lanes), 1)
    near = ((m * near) & (longitudes - 1)).astype(F32) * step
    near_cos = jnp.cos(near) * scale
    near_sin = jnp.sin(near) * scale
    blocks = longitudes // lanes
    eighth = lax.broadcasted_iota(jnp.int32, (orders, lanes), 1) & (blocks - 1)
    far = ((m * eighth * lanes) & (longitudes - 1)).astype(F32) * step
    far_cos = jnp.cos(far)
    far_sin = jnp.sin(far)
    for b in range(blocks):
        a = far_cos[:, b : b + 1]
        c = far_sin[:, b : b + 1]
        cosine[:, b * lanes : (b + 1) * lanes] = (a * near_cos - c * near_sin).astype(BF16)
        sines[:, b * lanes : (b + 1) * lanes] = (c * near_cos + a * near_sin).astype(BF16)


def fourier_tables(order_slot):
    orders = order_slot.shape[0]
    shape = jax.ShapeDtypeStruct((orders, 2 * orders), BF16)
    return pl.pallas_call(
        tables_kernel,
        out_shape=(shape, shape),
        compiler_params=pltpu.CompilerParams(vmem_limit_bytes=32 << 20),
        cost_estimate=pl.CostEstimate(
            flops=10_000_000, bytes_accessed=2 << 20, transcendentals=300_000
        ),
        name="tables",
    )(order_slot[:, None])


def transform_kernel(received, cosine, sines, factor, returned):
    columns = received.shape[1]
    part = columns // 4
    ft = received[...].astype(F32).T.astype(BF16)
    with_cos = jnp.concatenate([ft[:part], ft[3 * part :]], axis=0)
    with_sin = ft[part : 3 * part]
    grid = dot(with_cos, cosine[...]) + dot(with_sin, sines[...])
    weighted = (grid * factor[...]).astype(BF16)
    colat, azimuth = weighted[:part], weighted[part:]
    none = jnp.zeros_like(colat)
    back = dot(
        cosine[...], jnp.concatenate([colat, none, none, azimuth], axis=0), NT
    ) + dot(sines[...], jnp.concatenate([none, colat, azimuth, none], axis=0), NT)
    returned[...] = back.astype(BF16)


def cycle_transform(received, cosine, sines, factor):
    return pl.pallas_call(
        transform_kernel,
        out_shape=jax.ShapeDtypeStruct(received.shape, BF16),
        compiler_params=pltpu.CompilerParams(vmem_limit_bytes=40 << 20),
        cost_estimate=pl.CostEstimate(
            flops=600_000_000, bytes_accessed=3 << 20, transcendentals=0
        ),
        name="transform",
    )(received, cosine, sines, factor)


def analyse_kernel(
    where, got0, got1, got2, got3, legendre, tt, applied, gram,
    wide, adj, leg_v, tt_v, app_v, sem_l, sem_t, sem_o,
):
    orders, _, vectors, _ = tt.shape
    columns = 4 * vectors
    start = pl.multiple_of(where[0], 16)
    shift = where[1]
    for s in range(orders):
        window_copy(legendre, leg_v, sem_l, s, start).start()
        pltpu.make_async_copy(tt.at[s], tt_v.at[s], sem_t.at[s]).start()
    gots = (got0, got1, got2, got3)
    for e, got in enumerate(gots):
        wide[e] = got[...].astype(F32)
    adj[...] = jnp.zeros_like(adj)
    lane = lax.broadcasted_iota(jnp.int32, (1, columns), 1) // vectors
    one = jnp.ones((1, columns), F32)
    sign0 = jnp.where(lane < 2, one, -one)
    sign1 = jnp.where((lane == 0) | (lane == 3), -one, one)
    cycles = got0.shape[0] // orders
    block = {0: 0, 1: 1, 3: 2, 2: 3}
    total = jnp.zeros(gram.shape, F32)
    for s in range(orders):
        for e in range(4):
            x = wide[e, pl.ds(s, cycles, stride=orders), :]
            base = e * 2 * WINDOW + shift
            adj[pl.ds(base, cycles), :] = x * sign0
            adj[pl.ds(base + WINDOW, cycles), :] = pltpu.roll(x, columns // 2, 1) * sign1
        a = jnp.concatenate(
            [adj[e * 2 * WINDOW : (e + 1) * 2 * WINDOW].T for e in range(4)], axis=0
        ).astype(BF16)
        window_copy(legendre, leg_v, sem_l, s, start).wait()
        rows = dot(a, leg_v[s].reshape(2 * WINDOW, leg_v.shape[3])).astype(BF16)
        pltpu.make_async_copy(tt.at[s], tt_v.at[s], sem_t.at[s]).wait()
        for c in range(4):
            b = block[c] * vectors
            own = [rows[e * columns + b : e * columns + b + vectors] for e in range(4)]
            every = jnp.concatenate(own, axis=0)
            app_v[s, c] = every
            total = total + dot(jnp.concatenate([tt_v[s, c], own[0]], axis=0), every, NT)
        pltpu.make_async_copy(app_v.at[s], applied.at[s], sem_o.at[s]).start()
    gram[...] = total
    for s in range(orders):
        pltpu.make_async_copy(app_v.at[s], applied.at[s], sem_o.at[s]).wait()


def analyse(where, gots, legendre, tt):
    orders, _, vectors, degrees = tt.shape
    cycles_rows, columns = gots[0].shape
    vmem = pl.BlockSpec(memory_space=pltpu.VMEM)
    hbm = pl.BlockSpec(memory_space=pl.ANY)
    return pl.pallas_call(
        analyse_kernel,
        out_shape=(
            jax.ShapeDtypeStruct((orders, 4, 4 * vectors, degrees), BF16),
            jax.ShapeDtypeStruct((2 * vectors, 4 * vectors), F32),
        ),
        in_specs=[pl.BlockSpec(memory_space=pltpu.SMEM)] + [vmem] * 4 + [hbm] * 2,
        out_specs=(hbm, vmem),
        scratch_shapes=[
            pltpu.VMEM((4, cycles_rows, columns), F32),
            pltpu.VMEM((4 * 2 * WINDOW, columns), F32),
            pltpu.VMEM((orders, 2, WINDOW, degrees), BF16),
            pltpu.VMEM((orders, 4, vectors, degrees), BF16),
            pltpu.VMEM((orders, 4, 4 * vectors, degrees), BF16),
            pltpu.SemaphoreType.DMA((orders,)),
            pltpu.SemaphoreType.DMA((orders,)),
            pltpu.SemaphoreType.DMA((orders,)),
        ],
        compiler_params=pltpu.CompilerParams(vmem_limit_bytes=48 << 20),
        cost_estimate=pl.CostEstimate(
            flops=2_000_000_000, bytes_accessed=14 << 20, transcendentals=0
        ),
        name="analyse",
    )(where, *gots, legendre, tt)


def trial_gram(blocks):
    def body(b0, b1, b2, b3, out):
        total = jnp.zeros(out.shape, F32)
        for s in range(b0.shape[0]):
            for c in range(4):
                x = jnp.concatenate([b[s, c] for b in (b0, b1, b2, b3)], axis=0)
                total = total + dot(x, x, NT)
        out[...] = total

    rows = 4 * blocks[0].shape[2]
    return pl.pallas_call(
        body,
        out_shape=jax.ShapeDtypeStruct((rows, rows), F32),
        compiler_params=pltpu.CompilerParams(vmem_limit_bytes=32 << 20),
        cost_estimate=pl.CostEstimate(
            flops=300_000_000, bytes_accessed=2 << 20, transcendentals=0
        ),
        name="trial_gram",
    )(*blocks)


def inverse_factors_kernel(trial_gram_ref, cross, applied_gram_ref, ritz, mixing, work):
    n = cross.shape[0]
    row = lax.broadcasted_iota(jnp.int32, (n, 2 * n), 0)
    col = lax.broadcasted_iota(jnp.int32, (n, 2 * n), 1)
    identity = (col == row + n).astype(F32)
    for which, ref in enumerate((trial_gram_ref, applied_gram_ref)):
        work[which] = identity
        work[which, :, :n] = ref[...]
    column = lax.broadcasted_iota(jnp.int32, (1, 2 * n), 1)
    index = lax.broadcasted_iota(jnp.int32, (n, 1), 0)

    def step(j, _):
        for which in range(2):
            m = work[which]
            line = work[which, pl.ds(j, 1), :]
            pivot = jnp.sum(jnp.where(column == j, line, 0.0), axis=1, keepdims=True)
            scaled = line / pivot
            multiple = jnp.sum(jnp.where(col == j, m, 0.0), axis=1, keepdims=True)
            multiple = jnp.where(index > j, multiple, 0.0)
            work[which] = m - multiple * scaled
            work[which, pl.ds(j, 1), :] = line * lax.rsqrt(pivot)
        return 0

    lax.fori_loop(0, n, step, 0)
    inverse_trial = work[0, :, n:]
    half = dot_high(inverse_trial, cross[...])
    ritz[...] = dot_high(half, inverse_trial, NT)
    mixing[...] = work[1, :, n:].astype(BF16)


def finish_ritz(gram_trial, cross, gram_applied):
    n = cross.shape[0]
    return pl.pallas_call(
        inverse_factors_kernel,
        out_shape=(
            jax.ShapeDtypeStruct((n, n), F32),
            jax.ShapeDtypeStruct((n, n), BF16),
        ),
        scratch_shapes=[pltpu.VMEM((2, n, 2 * n), F32)],
        name="factors",
    )(gram_trial, cross, gram_applied)


def mix_kernel(weights, applied, out):
    vectors = out.shape[0]
    x = applied[0].reshape(applied.shape[1] * applied.shape[2], applied.shape[3])
    y = dot(weights[...], x).astype(BF16)
    out[:, 0] = y.reshape(vectors, 4, applied.shape[3])


def mix(weights, applied):
    orders, _, everyone, degrees = applied.shape
    vectors = everyone // 4
    return pl.pallas_call(
        mix_kernel,
        grid=(orders,),
        out_shape=jax.ShapeDtypeStruct((vectors, orders, 4, degrees), BF16),
        in_specs=[
            pl.BlockSpec(weights.shape, lambda s: (0, 0)),
            pl.BlockSpec((1, 4, everyone, degrees), lambda s: (s, 0, 0, 0)),
        ],
        out_specs=pl.BlockSpec((vectors, 1, 4, degrees), lambda s: (0, s, 0, 0)),
        compiler_params=pltpu.CompilerParams(vmem_limit_bytes=32 << 20),
        cost_estimate=pl.CostEstimate(
            flops=1_100_000_000, bytes_accessed=10 << 20, transcendentals=0
        ),
        name="mix",
    )(weights, applied)


def shards(trial_block, legendre, order_slot, cycle_start, cycle_count, cycle_weight):
    vectors, orders, _, degrees = trial_block.shape
    cycles_total = legendre.shape[2]
    live = cycles_total // 4
    groups = 4
    everyone = groups * vectors
    columns = 4 * vectors
    me = lax.axis_index("vert")
    home = lax.axis_index(MA)
    owners = live
    longitudes = 2 * order_slot.shape[0]

    cycle_index = jnp.arange(cycles_total, dtype=jnp.int32)
    first = jnp.min(jnp.where(cycle_count > 0, cycle_index, cycles_total - live))
    start = jnp.minimum(first // 16 * 16, cycles_total - WINDOW)
    where = jnp.stack([start, first - start])

    fields, tt = synthesize(where, trial_block, legendre, live)
    received = lax.all_to_all(fields, MA, split_axis=0, concat_axis=0, tiled=True)
    cosine, sines = fourier_tables(order_slot)

    pair = orders // groups

    def pair_of(d):
        return lax.dynamic_slice_in_dim(tt, (me + d) % groups * pair, pair, 0)

    blocks = [pair_of(0)] + [
        lax.ppermute(pair_of(d), "vert", ring(groups, d)) for d in range(1, groups)
    ]

    mine = cycle_index == first + home
    count, begin = (
        jnp.sum(jnp.where(mine, x, 0)) for x in (cycle_count, cycle_start)
    )
    weight = jnp.sum(jnp.where(mine, cycle_weight, 0.0))
    longitude = jnp.arange(longitudes, dtype=jnp.int32)
    inside = (longitude - begin) % longitudes < count
    factor = jnp.where(inside, weight, 0.0)[None, :]
    returned = cycle_transform(
        received.reshape(owners * orders, columns), cosine, sines, factor
    )
    order_fields = lax.all_to_all(
        returned.reshape(owners, orders, columns), MA, split_axis=0, concat_axis=0, tiled=True
    )
    order_fields = order_fields.reshape(owners * orders, columns)
    gots = [order_fields] + [
        lax.ppermute(order_fields, "vert", ring(groups, -d)) for d in range(1, groups)
    ]

    share = trial_gram(blocks)
    rows_home = []
    for d in range(groups):
        rows = share[d * vectors : (d + 1) * vectors]
        rows = jnp.concatenate(
            [
                rows[:, (d - e) % groups * vectors : ((d - e) % groups + 1) * vectors]
                for e in range(groups)
            ],
            axis=1,
        )
        rows_home.append(rows if d == 0 else lax.ppermute(rows, "vert", ring(groups, -d)))
    trial_rows = sum(rows_home[1:], rows_home[0])

    applied, gram = analyse(where, gots, legendre, tt)
    half = everyone // 2
    packed = jnp.concatenate(
        [gram, jnp.concatenate([trial_rows[:, :half], trial_rows[:, half:]], axis=0)], axis=1
    )
    chunks = lax.all_to_all(packed, MA, split_axis=0, concat_axis=0, tiled=True)
    summed = jnp.sum(chunks, axis=0, keepdims=True)
    everywhere = owners * groups
    summed = lax.all_to_all(
        jnp.broadcast_to(summed, (everywhere, packed.shape[1])),
        ALL,
        split_axis=0,
        concat_axis=0,
        tiled=True,
    )
    summed = summed.reshape(owners, groups, packed.shape[1]) / (owners * orders * 4 * degrees)
    crosses, applieds, trials = [], [], []
    for v in range(groups):
        s = summed[:, v]
        t = jnp.concatenate([s[:vectors, everyone:], s[vectors:, everyone:]], axis=1)
        for into, rows in (
            (crosses, s[:vectors, :everyone]),
            (applieds, s[vectors:, :everyone]),
            (trials, t),
        ):
            into.append(jnp.roll(rows, v * vectors, axis=1))
    ritz_matrix, mixing = finish_ritz(
        *(jnp.concatenate(x, axis=0) for x in (trials, crosses, applieds))
    )
    mine_rows = lax.dynamic_slice_in_dim(mixing, me * vectors, vectors, 0)
    twice = jnp.concatenate([mine_rows, mine_rows], axis=1)
    mine_rows = lax.dynamic_slice_in_dim(twice, me * vectors, everyone, 1)
    spread = jnp.where(
        jnp.arange(4)[None, :, None, None] == jnp.arange(4)[None, None, :, None],
        mine_rows[:, None, None, :],
        jnp.zeros((), BF16),
    ).reshape(4 * vectors, 4 * everyone)
    new_basis = mix(spread, applied)
    return (new_basis, ritz_matrix)


def solution(mesh):
    split = Mesh(
        mesh.devices.reshape(4, 8, 2, mesh.shape["vert"]), ("ma_0", "ma_1", "ma_2", "vert")
    )
    placed = (P("vert", MA, None, None), P(MA, None, None, None), P(), P(), P(), P())
    return jax.shard_map(
        shards,
        mesh=split,
        in_specs=placed,
        out_specs=(P("vert", MA, None, None), P()),
        check_vma=False,
    )
```

```python
import math

import jax
import jax.numpy as jnp
from jax import lax
from jax.experimental import pallas as pl
from jax.experimental.pallas import tpu as pltpu
from jax.sharding import Mesh
from jax.sharding import PartitionSpec as P

MA = ("ma_0", "ma_1", "ma_2")
F32 = jnp.float32
BF16 = jnp.bfloat16
WINDOW = 80
PANEL = 8
NT = (((1,), (1,)), ((), ()))
NN = (((1,), (0,)), ((), ()))


def ring(size, shift):
    return [(i, (i + shift) % size) for i in range(size)]


def dot(a, b, dims=NN):
    return lax.dot_general(a, b, dims, preferred_element_type=F32)


def dot_high(a, b, dims=NN):
    return lax.dot_general(
        a, b, dims, precision=lax.Precision.HIGHEST, preferred_element_type=F32
    )


def window_copy(legendre, leg_v, sem, s, slot, start):
    return pltpu.make_async_copy(
        legendre.at[s, :, pl.ds(start, WINDOW), :], leg_v.at[slot], sem.at[slot]
    )


def order_at(step, orders):
    return (lax.axis_index("vert") * (orders // 4) + step) & (orders - 1)


def synthesize_kernel(
    counts, trial, legendre, fields, pair0, pair1, pair2, pair3, where,
    tr_v, leg_v, tt_v, prod, sem_t, sem_l, sem_o,
):
    vectors, orders = trial.shape[:2]
    pairs = (pair0, pair1, pair2, pair3)
    pair = orders // 4
    for n in range(orders):
        pltpu.make_async_copy(trial.at[:, order_at(n, orders)], tr_v.at[n], sem_t.at[n]).start()
    live = counts[...] > 0
    cycle = lax.broadcasted_iota(jnp.int32, live.shape, 0) * live.shape[1]
    cycle = cycle + lax.broadcasted_iota(jnp.int32, live.shape, 1)
    last = legendre.shape[2] - fields.shape[0]
    first = jnp.min(jnp.where(live, cycle, last).astype(F32)).astype(jnp.int32)
    start = jnp.minimum((first // 16) * 16, legendre.shape[2] - WINDOW)
    start = pl.multiple_of(start, 16)
    shift = first - start
    where[0] = start
    where[1] = shift
    for n in range(orders):
        window_copy(legendre, leg_v, sem_l, order_at(n, orders), n, start).start()
    rows = 4 * vectors
    i = lax.broadcasted_iota(jnp.int32, (rows, rows), 0)
    j = lax.broadcasted_iota(jnp.int32, (rows, rows), 1)
    by_part = (j == (i % vectors) * 4 + i // vectors).astype(BF16)
    for n in range(orders):
        s = order_at(n, orders)
        pltpu.make_async_copy(trial.at[:, s], tr_v.at[n], sem_t.at[n]).wait()
        x = tr_v[n].reshape(rows, tr_v.shape[3])
        t = dot(by_part, x).astype(BF16)
        t0, t1, t2, t3 = (t[c * vectors : (c + 1) * vectors] for c in range(4))
        for c, part in enumerate((t0, t1, t2, t3)):
            tt_v[n, c] = part
        pltpu.make_async_copy(tt_v.at[n], pairs[n // pair].at[n % pair], sem_o.at[n]).start()
        first_kind = jnp.concatenate([t0, t1, -t3, -t2], axis=0)
        second_kind = jnp.concatenate([t3, -t2, -t0, t1], axis=0)
        window_copy(legendre, leg_v, sem_l, s, n, start).wait()
        prod[pl.ds(pl.multiple_of(s * WINDOW, 8), WINDOW), :] = dot(
            leg_v[n, 0], first_kind, NT
        ) + dot(leg_v[n, 1], second_kind, NT)
    for r in range(fields.shape[0]):
        fields[r] = prod[pl.ds(shift + r, orders, stride=WINDOW), :].astype(BF16)
    for n in range(orders):
        pltpu.make_async_copy(tt_v.at[n], pairs[n // pair].at[n % pair], sem_o.at[n]).wait()


def synthesize(counts, trial, legendre, cycles):
    vectors, orders, _, degrees = trial.shape
    hbm = pl.BlockSpec(memory_space=pltpu.HBM)
    vmem = pl.BlockSpec(memory_space=pltpu.VMEM)
    pair = jax.ShapeDtypeStruct((orders // 4, 4, vectors, degrees), BF16)
    return pl.pallas_call(
        synthesize_kernel,
        out_shape=(
            jax.ShapeDtypeStruct((cycles, orders, 4 * vectors), BF16),
            *([pair] * 4),
            jax.ShapeDtypeStruct((2,), jnp.int32),
        ),
        in_specs=[vmem, hbm, hbm],
        out_specs=(vmem, hbm, hbm, hbm, hbm, pl.BlockSpec(memory_space=pltpu.SMEM)),
        scratch_shapes=[
            pltpu.VMEM((orders, vectors, 4, degrees), BF16),
            pltpu.VMEM((orders, 2, WINDOW, degrees), BF16),
            pltpu.VMEM((orders, 4, vectors, degrees), BF16),
            pltpu.VMEM((orders * WINDOW, 4 * vectors), F32),
            pltpu.SemaphoreType.DMA((orders,)),
            pltpu.SemaphoreType.DMA((orders,)),
            pltpu.SemaphoreType.DMA((orders,)),
        ],
        compiler_params=pltpu.CompilerParams(vmem_limit_bytes=40 << 20),
        cost_estimate=pl.CostEstimate(
            flops=600_000_000, bytes_accessed=8 << 20, transcendentals=0
        ),
        name="synthesize",
    )(counts, trial, legendre)


def quarter_sine(x):
    y = x * x
    sine = 1.0 + y * (-1 / 6 + y * (1 / 120 + y * (-1 / 5040 + y * (1 / 362880 + y * (-1 / 39916800)))))
    cosine = 1.0 + y * (
        -1 / 2 + y * (1 / 24 + y * (-1 / 720 + y * (1 / 40320 + y * (-1 / 3628800 + y * (1 / 479001600)))))
    )
    return sine * x, cosine


def turn(phase, longitudes):
    quarter = longitudes // 4
    s, c = quarter_sine((phase & (quarter - 1)).astype(F32) * (2.0 * math.pi / longitudes))
    quadrant = phase // quarter
    swapped = (quadrant & 1) == 1
    sine = jnp.where(swapped, c, s)
    cosine = jnp.where(swapped, s, c)
    sine = jnp.where(quadrant >= 2, -sine, sine)
    cosine = jnp.where((quadrant == 1) | (quadrant == 2), -cosine, cosine)
    return sine, cosine


def transform_kernel(
    where, begins, counts, weights, slots, received, returned, cosine, sines
):
    orders, longitudes = cosine.shape
    lanes = slots.shape[1]
    columns = received.shape[1]
    part = columns // 4
    scale = 1.0 / math.sqrt(orders)
    near = lax.broadcasted_iota(jnp.int32, (lanes, lanes), 1)
    for g in range(slots.shape[0]):
        m = jnp.broadcast_to(slots[g : g + 1, :].astype(F32), (lanes, lanes)).T
        m = m.astype(jnp.int32)
        span = slice(g * lanes, (g + 1) * lanes)
        step_s, step_c = turn((m * lanes) & (longitudes - 1), longitudes)
        s, c = turn((m * near) & (longitudes - 1), longitudes)
        s, c = s * scale, c * scale
        for b in range(longitudes // lanes):
            cosine[span, b * lanes : (b + 1) * lanes] = c.astype(BF16)
            sines[span, b * lanes : (b + 1) * lanes] = s.astype(BF16)
            s, c = s * step_c + c * step_s, c * step_c - s * step_s

    home = (lax.axis_index("ma_0") * 8 + lax.axis_index("ma_1")) * 2 + lax.axis_index("ma_2")
    r = where[0] + where[1] + home
    j = lax.broadcasted_iota(jnp.int32, (1, longitudes), 1)
    inside = ((j - begins[r]) & (longitudes - 1)) < counts[r]
    factor = jnp.where(inside, weights[r], 0.0)

    ft = received[...].astype(F32).T.astype(BF16)
    with_cos = jnp.concatenate([ft[:part], ft[3 * part :]], axis=0)
    with_sin = ft[part : 3 * part]
    grid = dot(with_cos, cosine[...]) + dot(with_sin, sines[...])
    weighted = (grid * factor).astype(BF16)
    colat, azimuth = weighted[:part], weighted[part:]
    none = jnp.zeros_like(colat)
    back = dot(
        cosine[...], jnp.concatenate([colat, none, none, azimuth], axis=0), NT
    ) + dot(sines[...], jnp.concatenate([none, colat, azimuth, none], axis=0), NT)
    returned[...] = back.astype(BF16)


def cycle_transform(where, begins, counts, weights, slots, received):
    vmem = pl.BlockSpec(memory_space=pltpu.VMEM)
    smem = pl.BlockSpec(memory_space=pltpu.SMEM)
    orders = slots.size
    return pl.pallas_call(
        transform_kernel,
        out_shape=jax.ShapeDtypeStruct(received.shape, BF16),
        in_specs=[smem] * 4 + [vmem] * 2,
        out_specs=vmem,
        scratch_shapes=[pltpu.VMEM((orders, 2 * orders), BF16)] * 2,
        compiler_params=pltpu.CompilerParams(vmem_limit_bytes=40 << 20),
        cost_estimate=pl.CostEstimate(
            flops=600_000_000, bytes_accessed=3 << 20, transcendentals=0
        ),
        name="transform",
    )(where, begins, counts, weights, slots, received)


def trial_gram_kernel(b0, b1, b2, b3, own, home1, home2, home3):
    total = 0.0
    for s in range(b0.shape[0]):
        for c in range(4):
            x = jnp.concatenate([b[s, c] for b in (b0, b1, b2, b3)], axis=0)
            total = total + dot(x, x, NT)
    n = own.shape[0]
    for d, out in enumerate((own, home1, home2, home3)):
        rows = total[d * n : (d + 1) * n]
        out[...] = jnp.concatenate(
            [rows[:, (d - e) % 4 * n : ((d - e) % 4 + 1) * n] for e in range(4)], axis=1
        )


def trial_gram(blocks):
    vectors = blocks[0].shape[2]
    return pl.pallas_call(
        trial_gram_kernel,
        out_shape=[jax.ShapeDtypeStruct((vectors, 4 * vectors), F32)] * 4,
        compiler_params=pltpu.CompilerParams(vmem_limit_bytes=32 << 20),
        cost_estimate=pl.CostEstimate(
            flops=300_000_000, bytes_accessed=2 << 20, transcendentals=0
        ),
        name="trial_gram",
    )(*blocks)


def analyse_kernel(
    where, got0, got1, got2, got3, rows0, rows1, rows2, rows3, legendre,
    pair0, pair1, pair2, pair3, applied, gram,
    wide, adj, leg_v, tt_v, app_v, sem_l, sem_t, sem_o,
):
    pairs = (pair0, pair1, pair2, pair3)
    orders = applied.shape[0]
    pair = orders // 4
    vectors = pair0.shape[2]
    columns = 4 * vectors
    start = pl.multiple_of(where[0], 16)
    shift = where[1]

    def trial_copy(n):
        return pltpu.make_async_copy(
            pairs[n // pair].at[n % pair], tt_v.at[n], sem_t.at[n]
        )

    for n in range(orders):
        window_copy(legendre, leg_v, sem_l, order_at(n, orders), n, start).start()
        trial_copy(n).start()
    for e, got in enumerate((got0, got1, got2, got3)):
        wide[e] = got[...].astype(F32)
    adj[...] = jnp.zeros_like(adj)
    lane = lax.broadcasted_iota(jnp.int32, (1, columns), 1) // vectors
    one = jnp.ones((1, columns), F32)
    sign0 = jnp.where(lane < 2, one, -one)
    sign1 = jnp.where((lane == 0) | (lane == 3), -one, one)
    cycles = got0.shape[0] // orders
    block = {0: 0, 1: 1, 3: 2, 2: 3}
    total = 0.0
    for n in range(orders):
        s = order_at(n, orders)
        for e in range(4):
            x = wide[e, pl.ds(s, cycles, stride=orders), :]
            base = e * 2 * WINDOW + shift
            adj[pl.ds(base, cycles), :] = x * sign0
            adj[pl.ds(base + WINDOW, cycles), :] = pltpu.roll(x, columns // 2, 1) * sign1
        a = jnp.concatenate(
            [adj[e * 2 * WINDOW : (e + 1) * 2 * WINDOW].T for e in range(4)], axis=0
        ).astype(BF16)
        window_copy(legendre, leg_v, sem_l, s, n, start).wait()
        rows = dot(a, leg_v[n].reshape(2 * WINDOW, leg_v.shape[3])).astype(BF16)
        trial_copy(n).wait()
        for c in range(4):
            b = block[c] * vectors
            own = [rows[e * columns + b : e * columns + b + vectors] for e in range(4)]
            every = jnp.concatenate(own, axis=0)
            app_v[n, c] = every
            total = total + dot(every, jnp.concatenate([tt_v[n, c], own[0]], axis=0), NT)
        pltpu.make_async_copy(app_v.at[n], applied.at[n], sem_o.at[n]).start()
    gram[:vectors] = (rows0[...] + rows1[...]) + (rows2[...] + rows3[...])
    gram[vectors:] = total.T
    for n in range(orders):
        pltpu.make_async_copy(app_v.at[n], applied.at[n], sem_o.at[n]).wait()


def analyse(where, gots, trial_rows, legendre, pairs):
    _, _, vectors, degrees = pairs[0].shape
    orders = 4 * pairs[0].shape[0]
    cycles_rows, columns = gots[0].shape
    vmem = pl.BlockSpec(memory_space=pltpu.VMEM)
    hbm = pl.BlockSpec(memory_space=pltpu.HBM)
    return pl.pallas_call(
        analyse_kernel,
        out_shape=(
            jax.ShapeDtypeStruct((orders, 4, 4 * vectors, degrees), BF16),
            jax.ShapeDtypeStruct((3 * vectors, 4 * vectors), F32),
        ),
        in_specs=[pl.BlockSpec(memory_space=pltpu.SMEM)] + [vmem] * 8 + [hbm] * 5,
        out_specs=(hbm, vmem),
        scratch_shapes=[
            pltpu.VMEM((4, cycles_rows, columns), F32),
            pltpu.VMEM((4 * 2 * WINDOW, columns), F32),
            pltpu.VMEM((orders, 2, WINDOW, degrees), BF16),
            pltpu.VMEM((orders, 4, vectors, degrees), BF16),
            pltpu.VMEM((orders, 4, 4 * vectors, degrees), BF16),
            pltpu.SemaphoreType.DMA((orders,)),
            pltpu.SemaphoreType.DMA((orders,)),
            pltpu.SemaphoreType.DMA((orders,)),
        ],
        compiler_params=pltpu.CompilerParams(vmem_limit_bytes=48 << 20),
        cost_estimate=pl.CostEstimate(
            flops=2_000_000_000, bytes_accessed=14 << 20, transcendentals=0
        ),
        name="analyse",
    )(where, *gots, *trial_rows, legendre, *pairs)


def eliminate(work, n):
    shape = (PANEL, n)
    sub = lax.broadcasted_iota(jnp.int32, shape, 0)
    for j in range(0, n, PANEL):
        for which in range(work.shape[0]):
            top = work[which, j : j + PANEL, :n]
            value, low, inverse = {}, {}, []
            for m in range(PANEL):
                column = jnp.broadcast_to(top[:, j + m : j + m + 1], shape)
                for i in range(m, PANEL):
                    value[i, m] = jnp.broadcast_to(column[i : i + 1], shape)
            for m in range(PANEL):
                inverse.append(lax.rsqrt(value[m, m]))
                for i in range(m + 1, PANEL):
                    low[i, m] = value[i, m] * inverse[m]
                for i in range(m + 1, PANEL):
                    for k in range(m + 1, i + 1):
                        value[i, k] = value[i, k] - low[i, m] * low[k, m]

            def solved(base):
                rows = []
                for m in range(PANEL):
                    line = jnp.broadcast_to(
                        work[which, j + m : j + m + 1, base : base + n], shape
                    )
                    for k in range(m):
                        line = line - low[m, k] * rows[k]
                    rows.append(line * inverse[m])
                return rows

            left = solved(0) if j + PANEL < n else None
            right = solved(n)
            panel = right[0]
            for m in range(1, PANEL):
                panel = jnp.where(sub == m, right[m], panel)
            work[which, j : j + PANEL, n:] = panel
            for i in range(j + PANEL, n, PANEL):
                block = work[which, i : i + PANEL, :n]
                tail = work[which, i : i + PANEL, n:]
                factor = []
                for m in range(PANEL):
                    column = jnp.broadcast_to(block[:, j + m : j + m + 1], shape)
                    for k in range(m):
                        column = column - low[m, k] * factor[k]
                    factor.append(column * inverse[m])
                for m in range(PANEL):
                    block = block - factor[m] * left[m]
                    tail = tail - factor[m] * right[m]
                work[which, i : i + PANEL, :n] = block
                work[which, i : i + PANEL, n:] = tail


def finish_kernel(
    gram0, gram1, gram2, gram3, applied, new_basis, ritz,
    work, cross, app_v, out_v, sem_i, sem_o,
):
    n = cross.shape[0]
    vectors = n // 4
    orders, _, _, degrees = applied.shape
    coefficients = 512 * 4 * degrees
    for s in range(orders):
        pltpu.make_async_copy(applied.at[s], app_v.at[s], sem_i.at[s]).start()
    me = lax.axis_index("vert")
    unit = (
        lax.broadcasted_iota(jnp.int32, (n, n), 0)
        == lax.broadcasted_iota(jnp.int32, (n, n), 1)
    ).astype(F32)
    work[0, :, n:] = unit
    work[1, :, n:] = unit
    for d, gram in enumerate((gram0, gram1, gram2, gram3)):
        group = (me + d) & 3
        rows = pltpu.roll(gram[...] * (1.0 / coefficients), group * vectors, 1)
        span = pl.ds(pl.multiple_of(group * vectors, vectors), vectors)
        work[0, span, :n] = rows[:vectors]
        cross[span, :] = rows[vectors : 2 * vectors]
        work[1, span, :n] = rows[2 * vectors :]
    eliminate(work, n)
    inverse_trial = work[0, :, n:]
    ritz[...] = dot_high(dot_high(inverse_trial, cross[...]), inverse_trial, NT)
    mine = work[1, pl.ds(pl.multiple_of(me * vectors, vectors), vectors), n:]
    mine = pltpu.roll(mine, ((4 - me) & 3) * vectors, 1).astype(BF16)
    i = lax.broadcasted_iota(jnp.int32, (n, vectors), 0)
    repeat = (i // 4 == lax.broadcasted_iota(jnp.int32, (n, vectors), 1)).astype(BF16)
    mine = dot(repeat, mine)
    part = lax.broadcasted_iota(jnp.int32, (n, n), 0) & 3
    weights = jnp.concatenate(
        [jnp.where(part == c, mine, 0.0) for c in range(4)], axis=1
    ).astype(BF16)

    def out_copy(s):
        return pltpu.make_async_copy(
            out_v.at[s], new_basis.at[:, order_at(s, orders)], sem_o.at[s]
        )

    for s in range(orders):
        pltpu.make_async_copy(applied.at[s], app_v.at[s], sem_i.at[s]).wait()
        y = dot(weights, app_v[s].reshape(4 * n, degrees)).astype(BF16)
        out_v[s] = y.reshape(vectors, 4, degrees)
        out_copy(s).start()
    for s in range(orders):
        out_copy(s).wait()


def finish(grams, applied):
    orders, _, n, degrees = applied.shape
    vectors = n // 4
    vmem = pl.BlockSpec(memory_space=pltpu.VMEM)
    hbm = pl.BlockSpec(memory_space=pltpu.HBM)
    return pl.pallas_call(
        finish_kernel,
        out_shape=(
            jax.ShapeDtypeStruct((vectors, orders, 4, degrees), BF16),
            jax.ShapeDtypeStruct((n, n), F32),
        ),
        in_specs=[vmem] * 4 + [hbm],
        out_specs=(hbm, vmem),
        scratch_shapes=[
            pltpu.VMEM((2, n, 2 * n), F32),
            pltpu.VMEM((n, n), F32),
            pltpu.VMEM((orders, 4, n, degrees), BF16),
            pltpu.VMEM((orders, vectors, 4, degrees), BF16),
            pltpu.SemaphoreType.DMA((orders,)),
            pltpu.SemaphoreType.DMA((orders,)),
        ],
        compiler_params=pltpu.CompilerParams(vmem_limit_bytes=40 << 20),
        cost_estimate=pl.CostEstimate(
            flops=1_200_000_000, bytes_accessed=11 << 20, transcendentals=0
        ),
        name="finish",
    )(*grams, applied)


def swap(value, axis, size, bit):
    return lax.ppermute(value, axis, [(i, i ^ bit) for i in range(size)])


def sum_of_four(value, axis, size):
    one, two, three = (swap(value, axis, size, bit) for bit in (1, 2, 3))
    return (value + one) + (two + three)


def sum_over_ma(value):
    value = value + swap(value, "ma_2", 2, 1)
    value = sum_of_four(value, "ma_1", 8)
    value = value + swap(value, "ma_1", 8, 4)
    return sum_of_four(value, "ma_0", 4)


def from_groups(value):
    return [value] + [lax.ppermute(value, "vert", ring(4, -d)) for d in (1, 2, 3)]


def shards(trial_block, legendre, order_slot, cycle_start, cycle_count, cycle_weight):
    vectors, orders, _, _ = trial_block.shape
    live = legendre.shape[2] // 4
    columns = 4 * vectors

    fields, *pairs, where = synthesize(
        cycle_count.reshape(-1, 128), trial_block, legendre, live
    )
    received = lax.all_to_all(fields, MA, split_axis=0, concat_axis=0, tiled=True)
    blocks = [pairs[0]] + [lax.ppermute(pairs[d], "vert", ring(4, d)) for d in (1, 2, 3)]
    returned = cycle_transform(
        where, cycle_start, cycle_count, cycle_weight, order_slot.reshape(-1, 128),
        received.reshape(live * orders, columns),
    )
    order_fields = lax.all_to_all(
        returned.reshape(live, orders, columns), MA, split_axis=0, concat_axis=0, tiled=True
    )
    gots = from_groups(order_fields.reshape(live * orders, columns))
    shares = trial_gram(blocks)
    trial_rows = [shares[0]] + [
        lax.ppermute(shares[d], "vert", ring(4, -d)) for d in (1, 2, 3)
    ]
    applied, gram = analyse(where, gots, trial_rows, legendre, pairs)
    return tuple(finish(from_groups(sum_over_ma(gram)), applied))


def solution(mesh):
    split = Mesh(
        mesh.devices.reshape(4, 8, 2, mesh.shape["vert"]), ("ma_0", "ma_1", "ma_2", "vert")
    )
    placed = (P("vert", MA, None, None), P(MA, None, None, None), P(), P(), P(), P())
    return jax.shard_map(
        shards,
        mesh=split,
        in_specs=placed,
        out_specs=(P("vert", MA, None, None), P()),
        check_vma=False,
    )
```

```python
import math

import jax
import jax.numpy as jnp
from jax import lax
from jax.experimental import pallas as pl
from jax.experimental.pallas import tpu as pltpu
from jax.sharding import Mesh
from jax.sharding import PartitionSpec as P

MA = ("ma_0", "ma_1", "ma_2")
F32 = jnp.float32
BF16 = jnp.bfloat16
WINDOW = 80
PANEL = 8
NT = (((1,), (1,)), ((), ()))
NN = (((1,), (0,)), ((), ()))


def ring(size, shift):
    return [(i, (i + shift) % size) for i in range(size)]


def dot(a, b, dims=NN):
    return lax.dot_general(a, b, dims, preferred_element_type=F32)


def in_hbm(value):
    return pltpu.with_memory_space_constraint(value, pltpu.HBM)


def dot_high(a, b, dims=NN):
    return lax.dot_general(
        a, b, dims, precision=lax.Precision.HIGHEST, preferred_element_type=F32
    )


def window_copy(legendre, leg_v, sem, s, slot, start):
    return pltpu.make_async_copy(
        legendre.at[s, :, pl.ds(start, WINDOW), :], leg_v.at[slot], sem.at[slot]
    )


def by_part(vectors):
    shape = (4 * vectors, 4 * vectors)
    i = lax.broadcasted_iota(jnp.int32, shape, 0)
    j = lax.broadcasted_iota(jnp.int32, shape, 1)
    return (j == (i % vectors) * 4 + i // vectors).astype(BF16)


def synthesize_kernel(
    counts, trial, legendre, fields, up, down, where,
    tr_v, leg_v, one, two, prod, sem_t, sem_l, sem_o,
):
    vectors, orders = trial.shape[:2]
    me = lax.axis_index("vert")
    sent = up.shape[0]

    def send_copies():
        for n in range(sent):
            for k, (out, lead) in enumerate(((up, 2), (down, 5))):
                yield pltpu.make_async_copy(
                    tr_v.at[(2 * me + lead + n) & (orders - 1)], out.at[n], sem_o.at[k, n]
                )

    for s in range(orders):
        pltpu.make_async_copy(trial.at[:, s], tr_v.at[s], sem_t.at[s]).start()
    live = counts[...] > 0
    cycle = lax.broadcasted_iota(jnp.int32, live.shape, 0) * live.shape[1]
    cycle = cycle + lax.broadcasted_iota(jnp.int32, live.shape, 1)
    last = legendre.shape[2] - fields.shape[0]
    first = jnp.min(jnp.where(live, cycle, last).astype(F32)).astype(jnp.int32)
    start = jnp.minimum((first // 16) * 16, legendre.shape[2] - WINDOW)
    start = pl.multiple_of(start, 16)
    shift = first - start
    where[0] = start
    where[1] = shift
    for s in range(orders):
        window_copy(legendre, leg_v, sem_l, s, s, start).start()
    for s in range(orders):
        pltpu.make_async_copy(trial.at[:, s], tr_v.at[s], sem_t.at[s]).wait()
        x = tr_v[s].reshape(4 * vectors, tr_v.shape[3])
        window_copy(legendre, leg_v, sem_l, s, s, start).wait()
        slot = s % 2
        one[slot, :, :WINDOW] = dot(x, leg_v[s, 0], NT)
        two[slot, :, :WINDOW] = dot(x, leg_v[s, 1], NT)
        w, x = (
            [ref[slot, pl.ds(c, vectors, stride=4), :] for c in range(4)]
            for ref in (one, two)
        )
        f = jnp.concatenate([w[0] + x[3], w[1] - x[2], -x[0] - w[3], x[1] - w[2]], axis=0)
        prod[s * WINDOW : (s + 1) * WINDOW] = f.T[:WINDOW]
        if s == orders - 1:
            for copy in send_copies():
                copy.start()
    for r in range(fields.shape[0]):
        fields[r] = prod[pl.ds(shift + r, orders, stride=WINDOW), :].astype(BF16)
    for copy in send_copies():
        copy.wait()


def synthesize(counts, trial, legendre, cycles):
    vectors, orders, _, degrees = trial.shape
    columns = 4 * vectors
    hbm = pl.BlockSpec(memory_space=pltpu.HBM)
    vmem = pl.BlockSpec(memory_space=pltpu.VMEM)
    sent = pltpu.HBM((3 * orders // 8, vectors, 4, degrees), BF16)
    return pl.pallas_call(
        synthesize_kernel,
        out_shape=(
            jax.ShapeDtypeStruct((cycles, orders, columns), BF16),
            sent,
            sent,
            jax.ShapeDtypeStruct((2,), jnp.int32),
        ),
        in_specs=[vmem, hbm, hbm],
        out_specs=(vmem, hbm, hbm, pl.BlockSpec(memory_space=pltpu.SMEM)),
        scratch_shapes=[
            pltpu.VMEM((orders, vectors, 4, degrees), BF16),
            pltpu.VMEM((orders, 2, WINDOW, degrees), BF16),
            pltpu.VMEM((2, columns, 128), F32),
            pltpu.VMEM((2, columns, 128), F32),
            pltpu.VMEM((orders * WINDOW, columns), F32),
            pltpu.SemaphoreType.DMA((orders,)),
            pltpu.SemaphoreType.DMA((orders,)),
            pltpu.SemaphoreType.DMA((2, 3 * orders // 8)),
        ],
        compiler_params=pltpu.CompilerParams(vmem_limit_bytes=40 << 20),
        cost_estimate=pl.CostEstimate(
            flops=600_000_000, bytes_accessed=5 << 20, transcendentals=0
        ),
        name="synthesize",
    )(counts, in_hbm(trial), in_hbm(legendre))


def arrange_kernel(trial, tt, tr_v, tt_v, sem_t, sem_o):
    vectors, orders = trial.shape[:2]
    for s in range(orders):
        pltpu.make_async_copy(trial.at[:, s], tr_v.at[s], sem_t.at[s]).start()
    order = by_part(vectors)
    for s in range(orders):
        pltpu.make_async_copy(trial.at[:, s], tr_v.at[s], sem_t.at[s]).wait()
        t = dot(order, tr_v[s].reshape(4 * vectors, tr_v.shape[3])).astype(BF16)
        for c in range(4):
            tt_v[s, c] = t[c * vectors : (c + 1) * vectors]
        pltpu.make_async_copy(tt_v.at[s], tt.at[s], sem_o.at[s]).start()
    for s in range(orders):
        pltpu.make_async_copy(tt_v.at[s], tt.at[s], sem_o.at[s]).wait()


def arrange(trial):
    vectors, orders, _, degrees = trial.shape
    hbm = pl.BlockSpec(memory_space=pltpu.HBM)
    return pl.pallas_call(
        arrange_kernel,
        out_shape=pltpu.HBM((orders, 4, vectors, degrees), BF16),
        in_specs=[hbm],
        out_specs=hbm,
        scratch_shapes=[
            pltpu.VMEM((orders, vectors, 4, degrees), BF16),
            pltpu.VMEM((orders, 4, vectors, degrees), BF16),
            pltpu.SemaphoreType.DMA((orders,)),
            pltpu.SemaphoreType.DMA((orders,)),
        ],
        compiler_params=pltpu.CompilerParams(vmem_limit_bytes=40 << 20),
        cost_estimate=pl.CostEstimate(
            flops=300_000_000, bytes_accessed=4 << 20, transcendentals=0
        ),
        name="arrange",
    )(in_hbm(trial))


def quarter_sine(x):
    y = x * x
    sine = 1.0 + y * (-1 / 6 + y * (1 / 120 + y * (-1 / 5040 + y * (1 / 362880 + y * (-1 / 39916800)))))
    cosine = 1.0 + y * (
        -1 / 2 + y * (1 / 24 + y * (-1 / 720 + y * (1 / 40320 + y * (-1 / 3628800 + y * (1 / 479001600)))))
    )
    return sine * x, cosine


def turn(phase, longitudes):
    quarter = longitudes // 4
    s, c = quarter_sine((phase & (quarter - 1)).astype(F32) * (2.0 * math.pi / longitudes))
    quadrant = phase // quarter
    swapped = (quadrant & 1) == 1
    sine = jnp.where(swapped, c, s)
    cosine = jnp.where(swapped, s, c)
    sine = jnp.where(quadrant >= 2, -sine, sine)
    cosine = jnp.where((quadrant == 1) | (quadrant == 2), -cosine, cosine)
    return sine, cosine


def transform_kernel(
    where, begins, counts, weights, slots, received, returned, token, cosine, sines
):
    orders, longitudes = cosine.shape
    lanes = slots.shape[1]
    columns = received.shape[1]
    part = columns // 4
    scale = 1.0 / math.sqrt(orders)
    near = lax.broadcasted_iota(jnp.int32, (lanes, lanes), 1)
    for g in range(slots.shape[0]):
        m = jnp.broadcast_to(slots[g : g + 1, :].astype(F32), (lanes, lanes)).T
        m = m.astype(jnp.int32)
        span = slice(g * lanes, (g + 1) * lanes)
        step_s, step_c = turn((m * lanes) & (longitudes - 1), longitudes)
        s, c = turn((m * near) & (longitudes - 1), longitudes)
        s, c = s * scale, c * scale
        for b in range(longitudes // lanes):
            cosine[span, b * lanes : (b + 1) * lanes] = c.astype(BF16)
            sines[span, b * lanes : (b + 1) * lanes] = s.astype(BF16)
            s, c = s * step_c + c * step_s, c * step_c - s * step_s

    home = (lax.axis_index("ma_0") * 8 + lax.axis_index("ma_1")) * 2 + lax.axis_index("ma_2")
    r = where[0] + where[1] + home
    j = lax.broadcasted_iota(jnp.int32, (1, longitudes), 1)
    inside = ((j - begins[r]) & (longitudes - 1)) < counts[r]
    factor = jnp.where(inside, weights[r], 0.0)

    ft = received[...].astype(F32).T.astype(BF16)
    with_cos = jnp.concatenate([ft[:part], ft[3 * part :]], axis=0)
    with_sin = ft[part : 3 * part]
    grid = dot(with_cos, cosine[...]) + dot(with_sin, sines[...])
    weighted = (grid * factor).astype(BF16)
    colat, azimuth = weighted[:part], weighted[part:]
    none = jnp.zeros_like(colat)
    back = dot(
        cosine[...], jnp.concatenate([colat, none, none, azimuth], axis=0), NT
    ) + dot(sines[...], jnp.concatenate([none, colat, azimuth, none], axis=0), NT)
    returned[...] = back.astype(BF16)
    token[...] = jnp.zeros_like(token)


def cycle_transform(where, begins, counts, weights, slots, received):
    vmem = pl.BlockSpec(memory_space=pltpu.VMEM)
    smem = pl.BlockSpec(memory_space=pltpu.SMEM)
    orders = slots.size
    return pl.pallas_call(
        transform_kernel,
        out_shape=(
            jax.ShapeDtypeStruct(received.shape, BF16),
            jax.ShapeDtypeStruct((8, 128), F32),
        ),
        in_specs=[smem] * 4 + [vmem] * 2,
        out_specs=(vmem, vmem),
        scratch_shapes=[pltpu.VMEM((orders, 2 * orders), BF16)] * 2,
        compiler_params=pltpu.CompilerParams(vmem_limit_bytes=40 << 20),
        cost_estimate=pl.CostEstimate(
            flops=600_000_000, bytes_accessed=3 << 20, transcendentals=0
        ),
        name="transform",
    )(where, begins, counts, weights, slots, received)


def trial_gram_kernel(
    trial, below, above, two_below, two_above, _, own, home1, home2, home3, mine, sem
):
    n, _, _, degrees = trial.shape
    me = lax.axis_index("vert")
    copies = [
        pltpu.make_async_copy(trial.at[:, 2 * me + i], mine.at[i], sem.at[i]) for i in range(2)
    ]
    for copy in copies:
        copy.start()
    order = by_part(n)
    total = 0.0
    for i, second in enumerate((two_below[0], two_above[0])):
        copies[i].wait()
        parts = [
            dot(order, b.reshape(4 * n, degrees)).astype(BF16)
            for b in (mine[i], below[i], second, above[i + 1])
        ]
        for c in range(4):
            x = jnp.concatenate([p[c * n : (c + 1) * n] for p in parts], axis=0)
            total = total + dot(x, x, NT)
    for d, out in enumerate((own, home1, home2, home3)):
        rows = total[d * n : (d + 1) * n]
        out[...] = jnp.concatenate(
            [rows[:, (d - e) % 4 * n : ((d - e) % 4 + 1) * n] for e in range(4)], axis=1
        )


def trial_gram(trial, received, token):
    vectors, _, parts, degrees = trial.shape
    vmem = pl.BlockSpec(memory_space=pltpu.VMEM)
    return pl.pallas_call(
        trial_gram_kernel,
        out_shape=[jax.ShapeDtypeStruct((vectors, 4 * vectors), F32)] * 4,
        in_specs=[pl.BlockSpec(memory_space=pltpu.HBM)] + [vmem] * 5,
        scratch_shapes=[
            pltpu.VMEM((2, vectors, parts, degrees), BF16),
            pltpu.SemaphoreType.DMA((2,)),
        ],
        compiler_params=pltpu.CompilerParams(vmem_limit_bytes=32 << 20),
        cost_estimate=pl.CostEstimate(
            flops=600_000_000, bytes_accessed=2 << 20, transcendentals=0
        ),
        name="trial_gram",
    )(in_hbm(trial), *received, token)


def analyse_kernel(
    where, got0, got1, got2, got3, rows0, rows1, rows2, rows3, legendre,
    tt, applied, gram,
    got_v, rows_v, wide, adj, leg_v, tt_v, app_v, sem_g, sem_r, sem_l, sem_t, sem_o,
):
    orders, _, vectors, _ = tt.shape
    columns = 4 * vectors
    start = pl.multiple_of(where[0], 16)
    shift = where[1]

    def trial_copy(n):
        return pltpu.make_async_copy(tt.at[n], tt_v.at[n], sem_t.at[n])

    got_copies = [
        pltpu.make_async_copy(got, got_v.at[e], sem_g.at[e])
        for e, got in enumerate((got0, got1, got2, got3))
    ]
    row_copies = [
        pltpu.make_async_copy(rows, rows_v.at[e], sem_r.at[e])
        for e, rows in enumerate((rows0, rows1, rows2, rows3))
    ]
    for copy in got_copies:
        copy.start()
    for n in range(orders):
        window_copy(legendre, leg_v, sem_l, n, n, start).start()
        trial_copy(n).start()
    for copy in row_copies:
        copy.start()
    for e, copy in enumerate(got_copies):
        copy.wait()
        wide[e] = got_v[e].astype(F32)
    adj[...] = jnp.zeros_like(adj)
    lane = lax.broadcasted_iota(jnp.int32, (1, columns), 1) // vectors
    one = jnp.ones((1, columns), F32)
    sign0 = jnp.where(lane < 2, one, -one)
    sign1 = jnp.where((lane == 0) | (lane == 3), -one, one)
    cycles = got0.shape[0] // orders
    block = {0: 0, 1: 1, 3: 2, 2: 3}
    total = 0.0
    for n in range(orders):
        for e in range(4):
            x = wide[e, pl.ds(n, cycles, stride=orders), :]
            base = e * 2 * WINDOW + shift
            adj[pl.ds(base, cycles), :] = x * sign0
            adj[pl.ds(base + WINDOW, cycles), :] = pltpu.roll(x, columns // 2, 1) * sign1
        a = jnp.concatenate(
            [adj[e * 2 * WINDOW : (e + 1) * 2 * WINDOW].T for e in range(4)], axis=0
        ).astype(BF16)
        window_copy(legendre, leg_v, sem_l, n, n, start).wait()
        rows = dot(a, leg_v[n].reshape(2 * WINDOW, leg_v.shape[3])).astype(BF16)
        trial_copy(n).wait()
        for c in range(4):
            b = block[c] * vectors
            own = [rows[e * columns + b : e * columns + b + vectors] for e in range(4)]
            every = jnp.concatenate(own, axis=0)
            app_v[n, c] = every
            total = total + dot(every, jnp.concatenate([tt_v[n, c], own[0]], axis=0), NT)
        pltpu.make_async_copy(app_v.at[n], applied.at[n], sem_o.at[n]).start()
    for copy in row_copies:
        copy.wait()
    gram[:vectors] = (rows_v[0] + rows_v[1]) + (rows_v[2] + rows_v[3])
    gram[vectors:] = total.T
    for n in range(orders):
        pltpu.make_async_copy(app_v.at[n], applied.at[n], sem_o.at[n]).wait()


def analyse(where, gots, trial_rows, legendre, tt):
    orders, _, vectors, degrees = tt.shape
    cycles_rows, columns = gots[0].shape
    vmem = pl.BlockSpec(memory_space=pltpu.VMEM)
    hbm = pl.BlockSpec(memory_space=pltpu.HBM)
    return pl.pallas_call(
        analyse_kernel,
        out_shape=(
            pltpu.HBM((orders, 4, 4 * vectors, degrees), BF16),
            jax.ShapeDtypeStruct((3 * vectors, 4 * vectors), F32),
        ),
        in_specs=[pl.BlockSpec(memory_space=pltpu.SMEM)] + [hbm] * 10,
        out_specs=(hbm, vmem),
        scratch_shapes=[
            pltpu.VMEM((4, cycles_rows, columns), BF16),
            pltpu.VMEM((4, vectors, columns), F32),
            pltpu.VMEM((4, cycles_rows, columns), F32),
            pltpu.VMEM((4 * 2 * WINDOW, columns), F32),
            pltpu.VMEM((orders, 2, WINDOW, degrees), BF16),
            pltpu.VMEM((orders, 4, vectors, degrees), BF16),
            pltpu.VMEM((orders, 4, 4 * vectors, degrees), BF16),
            pltpu.SemaphoreType.DMA((4,)),
            pltpu.SemaphoreType.DMA((4,)),
            pltpu.SemaphoreType.DMA((orders,)),
            pltpu.SemaphoreType.DMA((orders,)),
            pltpu.SemaphoreType.DMA((orders,)),
        ],
        compiler_params=pltpu.CompilerParams(vmem_limit_bytes=40 << 20),
        cost_estimate=pl.CostEstimate(
            flops=2_000_000_000, bytes_accessed=14 << 20, transcendentals=0
        ),
        name="analyse",
    )(where, *gots, *trial_rows, in_hbm(legendre), in_hbm(tt))


def eliminate(work, n):
    shape = (PANEL, n)
    sub = lax.broadcasted_iota(jnp.int32, shape, 0)
    for j in range(0, n, PANEL):
        for which in range(work.shape[0]):
            top = work[which, j : j + PANEL, :n]
            value, low, inverse = {}, {}, []
            for m in range(PANEL):
                column = jnp.broadcast_to(top[:, j + m : j + m + 1], shape)
                for i in range(m, PANEL):
                    value[i, m] = jnp.broadcast_to(column[i : i + 1], shape)
            for m in range(PANEL):
                inverse.append(lax.rsqrt(value[m, m]))
                for i in range(m + 1, PANEL):
                    low[i, m] = value[i, m] * inverse[m]
                for i in range(m + 1, PANEL):
                    for k in range(m + 1, i + 1):
                        value[i, k] = value[i, k] - low[i, m] * low[k, m]

            def solved(base):
                rows = []
                for m in range(PANEL):
                    line = jnp.broadcast_to(
                        work[which, j + m : j + m + 1, base : base + n], shape
                    )
                    for k in range(m):
                        line = line - low[m, k] * rows[k]
                    rows.append(line * inverse[m])
                return rows

            left = solved(0) if j + PANEL < n else None
            right = solved(n)
            panel = right[0]
            for m in range(1, PANEL):
                panel = jnp.where(sub == m, right[m], panel)
            work[which, j : j + PANEL, n:] = panel
            for i in range(j + PANEL, n, PANEL):
                block = work[which, i : i + PANEL, :n]
                tail = work[which, i : i + PANEL, n:]
                factor = []
                for m in range(PANEL):
                    column = jnp.broadcast_to(block[:, j + m : j + m + 1], shape)
                    for k in range(m):
                        column = column - low[m, k] * factor[k]
                    factor.append(column * inverse[m])
                for m in range(PANEL):
                    block = block - factor[m] * left[m]
                    tail = tail - factor[m] * right[m]
                work[which, i : i + PANEL, :n] = block
                work[which, i : i + PANEL, n:] = tail


def finish_kernel(
    gram0, gram1, gram2, gram3, applied, new_basis, ritz,
    gram_v, work, cross, app_v, out_v, sem_g, sem_i, sem_o,
):
    n = cross.shape[0]
    vectors = n // 4
    orders, _, _, degrees = applied.shape
    coefficients = 512 * 4 * degrees
    gram_copies = [
        pltpu.make_async_copy(gram, gram_v.at[d], sem_g.at[d])
        for d, gram in enumerate((gram0, gram1, gram2, gram3))
    ]
    for copy in gram_copies:
        copy.start()
    for s in range(orders):
        pltpu.make_async_copy(applied.at[s], app_v.at[s], sem_i.at[s]).start()
    me = lax.axis_index("vert")
    unit = (
        lax.broadcasted_iota(jnp.int32, (n, n), 0)
        == lax.broadcasted_iota(jnp.int32, (n, n), 1)
    ).astype(F32)
    work[0, :, n:] = unit
    work[1, :, n:] = unit
    for d, copy in enumerate(gram_copies):
        copy.wait()
        group = (me + d) & 3
        rows = pltpu.roll(gram_v[d] * (1.0 / coefficients), group * vectors, 1)
        span = pl.ds(pl.multiple_of(group * vectors, vectors), vectors)
        work[0, span, :n] = rows[:vectors]
        cross[span, :] = rows[vectors : 2 * vectors]
        work[1, span, :n] = rows[2 * vectors :]
    eliminate(work, n)
    inverse_trial = work[0, :, n:]
    ritz[...] = dot_high(dot_high(inverse_trial, cross[...]), inverse_trial, NT)
    mine = work[1, pl.ds(pl.multiple_of(me * vectors, vectors), vectors), n:]
    mine = pltpu.roll(mine, ((4 - me) & 3) * vectors, 1).astype(BF16)
    i = lax.broadcasted_iota(jnp.int32, (n, vectors), 0)
    repeat = (i // 4 == lax.broadcasted_iota(jnp.int32, (n, vectors), 1)).astype(BF16)
    mine = dot(repeat, mine)
    part = lax.broadcasted_iota(jnp.int32, (n, n), 0) & 3
    weights = jnp.concatenate(
        [jnp.where(part == c, mine, 0.0) for c in range(4)], axis=1
    ).astype(BF16)

    def out_copy(s):
        return pltpu.make_async_copy(
            out_v.at[s], new_basis.at[:, s], sem_o.at[s]
        )

    for s in range(orders):
        pltpu.make_async_copy(applied.at[s], app_v.at[s], sem_i.at[s]).wait()
        y = dot(weights, app_v[s].reshape(4 * n, degrees)).astype(BF16)
        out_v[s] = y.reshape(vectors, 4, degrees)
        out_copy(s).start()
    for s in range(orders):
        out_copy(s).wait()


def finish(grams, applied):
    orders, _, n, degrees = applied.shape
    vectors = n // 4
    vmem = pl.BlockSpec(memory_space=pltpu.VMEM)
    hbm = pl.BlockSpec(memory_space=pltpu.HBM)
    return pl.pallas_call(
        finish_kernel,
        out_shape=(
            jax.ShapeDtypeStruct((vectors, orders, 4, degrees), BF16),
            jax.ShapeDtypeStruct((n, n), F32),
        ),
        in_specs=[hbm] * 5,
        out_specs=(hbm, vmem),
        scratch_shapes=[
            pltpu.VMEM((4, *grams[0].shape), F32),
            pltpu.VMEM((2, n, 2 * n), F32),
            pltpu.VMEM((n, n), F32),
            pltpu.VMEM((orders, 4, n, degrees), BF16),
            pltpu.VMEM((orders, vectors, 4, degrees), BF16),
            pltpu.SemaphoreType.DMA((4,)),
            pltpu.SemaphoreType.DMA((orders,)),
            pltpu.SemaphoreType.DMA((orders,)),
        ],
        compiler_params=pltpu.CompilerParams(vmem_limit_bytes=40 << 20),
        cost_estimate=pl.CostEstimate(
            flops=1_200_000_000, bytes_accessed=11 << 20, transcendentals=0
        ),
        name="finish",
    )(*grams, in_hbm(applied))


def swap(value, axis, size, bit):
    return lax.ppermute(value, axis, [(i, i ^ bit) for i in range(size)])


def sum_of_four(value, axis, size):
    one, two, three = (swap(value, axis, size, bit) for bit in (1, 2, 3))
    return (value + one) + (two + three)


def sum_over_ma(value):
    value = value + swap(value, "ma_2", 2, 1)
    value = sum_of_four(value, "ma_1", 8)
    value = value + swap(value, "ma_1", 8, 4)
    return sum_of_four(value, "ma_0", 4)


def from_groups(value):
    return [value] + [lax.ppermute(value, "vert", ring(4, -d)) for d in (1, 2, 3)]


def shards(trial_block, legendre, order_slot, cycle_start, cycle_count, cycle_weight):
    vectors, orders, _, _ = trial_block.shape
    live = legendre.shape[2] // 4
    columns = 4 * vectors

    fields, up, down, where = synthesize(
        cycle_count.reshape(-1, 128), trial_block, legendre, live
    )
    received = lax.all_to_all(fields, MA, split_axis=0, concat_axis=0, tiled=True)
    below = lax.ppermute(up, "vert", ring(4, 1))
    above = lax.ppermute(down, "vert", ring(4, -1))
    tt = arrange(trial_block)
    received, tt = lax.optimization_barrier((received, tt))
    returned, token = cycle_transform(
        where, cycle_start, cycle_count, cycle_weight, order_slot.reshape(-1, 128),
        received.reshape(live * orders, columns),
    )
    below_late, above_late, token = lax.optimization_barrier((below, above, token))
    two_below = lax.ppermute(below_late[2:], "vert", ring(4, 1))
    two_above = lax.ppermute(above_late[:1], "vert", ring(4, -1))
    order_fields = lax.all_to_all(
        returned.reshape(live, orders, columns), MA, split_axis=0, concat_axis=0, tiled=True
    )
    shares = list(
        trial_gram(trial_block, (below_late, above_late, two_below, two_above), token)
    )
    order_fields, shares[0] = lax.optimization_barrier((order_fields, shares[0]))
    trial_rows = [shares[0]] + [
        lax.ppermute(shares[d], "vert", ring(4, -d)) for d in (1, 2, 3)
    ]
    gots = from_groups(order_fields.reshape(live * orders, columns))
    applied, gram = analyse(where, gots, trial_rows, legendre, tt)
    return tuple(finish(from_groups(sum_over_ma(gram)), applied))


def solution(mesh):
    split = Mesh(
        mesh.devices.reshape(4, 8, 2, mesh.shape["vert"]), ("ma_0", "ma_1", "ma_2", "vert")
    )
    placed = (P("vert", MA, None, None), P(MA, None, None, None), P(), P(), P(), P())
    return jax.shard_map(
        shards,
        mesh=split,
        in_specs=placed,
        out_specs=(P("vert", MA, None, None), P()),
        check_vma=False,
    )
```

```python
import math

import jax
import jax.numpy as jnp
from jax import lax
from jax.experimental import pallas as pl
from jax.experimental.pallas import tpu as pltpu
from jax.sharding import Mesh
from jax.sharding import PartitionSpec as P

MA = ("ma_0", "ma_1", "ma_2")
F32 = jnp.float32
BF16 = jnp.bfloat16
WINDOW = 80
PANEL = 8
NT = (((1,), (1,)), ((), ()))
NN = (((1,), (0,)), ((), ()))


def ring(size, shift):
    return [(i, (i + shift) % size) for i in range(size)]


def dot(a, b, dims=NN):
    return lax.dot_general(a, b, dims, preferred_element_type=F32)


def in_hbm(value):
    return pltpu.with_memory_space_constraint(value, pltpu.HBM)


def dot_high(a, b, dims=NN):
    return lax.dot_general(
        a, b, dims, precision=lax.Precision.HIGHEST, preferred_element_type=F32
    )


def window_copy(legendre, leg_v, sem, s, slot, start):
    return pltpu.make_async_copy(
        legendre.at[s, :, pl.ds(start, WINDOW), :], leg_v.at[slot], sem.at[slot]
    )


def by_part(vectors):
    shape = (4 * vectors, 4 * vectors)
    i = lax.broadcasted_iota(jnp.int32, shape, 0)
    j = lax.broadcasted_iota(jnp.int32, shape, 1)
    return (j == (i % vectors) * 4 + i // vectors).astype(BF16)


def synthesize_kernel(
    counts, trial, legendre, fields, sent1, sent2, sent3, where,
    tr_v, leg_v, one, two, prod, sem_t, sem_l, sem_o,
):
    vectors, orders = trial.shape[:2]
    me = lax.axis_index("vert")
    pair = orders // 4

    def send_copies():
        for d, out in enumerate((sent1, sent2, sent3)):
            yield pltpu.make_async_copy(
                tr_v.at[pl.ds((me + d + 1) % 4 * pair, pair)], out, sem_o.at[d]
            )

    for s in range(orders):
        pltpu.make_async_copy(trial.at[:, s], tr_v.at[s], sem_t.at[s]).start()
    live = counts[...] > 0
    cycle = lax.broadcasted_iota(jnp.int32, live.shape, 0) * live.shape[1]
    cycle = cycle + lax.broadcasted_iota(jnp.int32, live.shape, 1)
    last = legendre.shape[2] - fields.shape[0]
    first = jnp.min(jnp.where(live, cycle, last).astype(F32)).astype(jnp.int32)
    start = jnp.minimum((first // 16) * 16, legendre.shape[2] - WINDOW)
    start = pl.multiple_of(start, 16)
    shift = first - start
    where[0] = start
    where[1] = shift
    for s in range(orders):
        window_copy(legendre, leg_v, sem_l, s, s, start).start()
    for s in range(orders):
        pltpu.make_async_copy(trial.at[:, s], tr_v.at[s], sem_t.at[s]).wait()
        x = tr_v[s].reshape(4 * vectors, tr_v.shape[3])
        window_copy(legendre, leg_v, sem_l, s, s, start).wait()
        slot = s % 2
        one[slot, :, :WINDOW] = dot(x, leg_v[s, 0], NT)
        two[slot, :, :WINDOW] = dot(x, leg_v[s, 1], NT)
        w, x = (
            [ref[slot, pl.ds(c, vectors, stride=4), :] for c in range(4)]
            for ref in (one, two)
        )
        f = jnp.concatenate([w[0] + x[3], w[1] - x[2], -x[0] - w[3], x[1] - w[2]], axis=0)
        prod[s * WINDOW : (s + 1) * WINDOW] = f.T[:WINDOW]
        if s == orders - 1:
            for copy in send_copies():
                copy.start()
    for r in range(fields.shape[0]):
        fields[r] = prod[pl.ds(shift + r, orders, stride=WINDOW), :].astype(BF16)
    for copy in send_copies():
        copy.wait()


def synthesize(counts, trial, legendre, cycles):
    vectors, orders, _, degrees = trial.shape
    columns = 4 * vectors
    hbm = pl.BlockSpec(memory_space=pltpu.HBM)
    vmem = pl.BlockSpec(memory_space=pltpu.VMEM)
    sent = pltpu.HBM((orders // 4, vectors, 4, degrees), BF16)
    return pl.pallas_call(
        synthesize_kernel,
        out_shape=(
            jax.ShapeDtypeStruct((cycles, orders, columns), BF16),
            sent,
            sent,
            sent,
            jax.ShapeDtypeStruct((2,), jnp.int32),
        ),
        in_specs=[vmem, hbm, hbm],
        out_specs=(vmem, hbm, hbm, hbm, pl.BlockSpec(memory_space=pltpu.SMEM)),
        scratch_shapes=[
            pltpu.VMEM((orders, vectors, 4, degrees), BF16),
            pltpu.VMEM((orders, 2, WINDOW, degrees), BF16),
            pltpu.VMEM((2, columns, 128), F32),
            pltpu.VMEM((2, columns, 128), F32),
            pltpu.VMEM((orders * WINDOW, columns), F32),
            pltpu.SemaphoreType.DMA((orders,)),
            pltpu.SemaphoreType.DMA((orders,)),
            pltpu.SemaphoreType.DMA((3,)),
        ],
        compiler_params=pltpu.CompilerParams(vmem_limit_bytes=40 << 20),
        cost_estimate=pl.CostEstimate(
            flops=600_000_000, bytes_accessed=5 << 20, transcendentals=0
        ),
        name="synthesize",
    )(counts, in_hbm(trial), in_hbm(legendre))


def arrange_kernel(trial, tt, tr_v, tt_v, sem_t, sem_o):
    vectors, orders = trial.shape[:2]
    for s in range(orders):
        pltpu.make_async_copy(trial.at[:, s], tr_v.at[s], sem_t.at[s]).start()
    order = by_part(vectors)
    for s in range(orders):
        pltpu.make_async_copy(trial.at[:, s], tr_v.at[s], sem_t.at[s]).wait()
        t = dot(order, tr_v[s].reshape(4 * vectors, tr_v.shape[3])).astype(BF16)
        for c in range(4):
            tt_v[s, c] = t[c * vectors : (c + 1) * vectors]
        pltpu.make_async_copy(tt_v.at[s], tt.at[s], sem_o.at[s]).start()
    for s in range(orders):
        pltpu.make_async_copy(tt_v.at[s], tt.at[s], sem_o.at[s]).wait()


def arrange(trial):
    vectors, orders, _, degrees = trial.shape
    hbm = pl.BlockSpec(memory_space=pltpu.HBM)
    return pl.pallas_call(
        arrange_kernel,
        out_shape=pltpu.HBM((orders, 4, vectors, degrees), BF16),
        in_specs=[hbm],
        out_specs=hbm,
        scratch_shapes=[
            pltpu.VMEM((orders, vectors, 4, degrees), BF16),
            pltpu.VMEM((orders, 4, vectors, degrees), BF16),
            pltpu.SemaphoreType.DMA((orders,)),
            pltpu.SemaphoreType.DMA((orders,)),
        ],
        compiler_params=pltpu.CompilerParams(vmem_limit_bytes=40 << 20),
        cost_estimate=pl.CostEstimate(
            flops=300_000_000, bytes_accessed=4 << 20, transcendentals=0
        ),
        name="arrange",
    )(in_hbm(trial))


def quarter_sine(x):
    y = x * x
    sine = 1.0 + y * (-1 / 6 + y * (1 / 120 + y * (-1 / 5040 + y * (1 / 362880 + y * (-1 / 39916800)))))
    cosine = 1.0 + y * (
        -1 / 2 + y * (1 / 24 + y * (-1 / 720 + y * (1 / 40320 + y * (-1 / 3628800 + y * (1 / 479001600)))))
    )
    return sine * x, cosine


def turn(phase, longitudes):
    quarter = longitudes // 4
    s, c = quarter_sine((phase & (quarter - 1)).astype(F32) * (2.0 * math.pi / longitudes))
    quadrant = phase // quarter
    swapped = (quadrant & 1) == 1
    sine = jnp.where(swapped, c, s)
    cosine = jnp.where(swapped, s, c)
    sine = jnp.where(quadrant >= 2, -sine, sine)
    cosine = jnp.where((quadrant == 1) | (quadrant == 2), -cosine, cosine)
    return sine, cosine


def transform_kernel(
    where, begins, counts, weights, slots, received, returned, cosine, sines
):
    orders, longitudes = cosine.shape
    lanes = slots.shape[1]
    columns = received.shape[1]
    part = columns // 4
    scale = 1.0 / math.sqrt(orders)
    near = lax.broadcasted_iota(jnp.int32, (lanes, lanes), 1)
    for g in range(slots.shape[0]):
        m = jnp.broadcast_to(slots[g : g + 1, :].astype(F32), (lanes, lanes)).T
        m = m.astype(jnp.int32)
        span = slice(g * lanes, (g + 1) * lanes)
        step_s, step_c = turn((m * lanes) & (longitudes - 1), longitudes)
        s, c = turn((m * near) & (longitudes - 1), longitudes)
        s, c = s * scale, c * scale
        for b in range(longitudes // lanes):
            cosine[span, b * lanes : (b + 1) * lanes] = c.astype(BF16)
            sines[span, b * lanes : (b + 1) * lanes] = s.astype(BF16)
            s, c = s * step_c + c * step_s, c * step_c - s * step_s

    home = (lax.axis_index("ma_0") * 8 + lax.axis_index("ma_1")) * 2 + lax.axis_index("ma_2")
    r = where[0] + where[1] + home
    j = lax.broadcasted_iota(jnp.int32, (1, longitudes), 1)
    inside = ((j - begins[r]) & (longitudes - 1)) < counts[r]
    factor = jnp.where(inside, weights[r], 0.0)

    ft = received[...].astype(F32).T.astype(BF16)
    with_cos = jnp.concatenate([ft[:part], ft[3 * part :]], axis=0)
    with_sin = ft[part : 3 * part]
    grid = dot(with_cos, cosine[...]) + dot(with_sin, sines[...])
    weighted = (grid * factor).astype(BF16)
    colat, azimuth = weighted[:part], weighted[part:]
    none = jnp.zeros_like(colat)
    back = dot(
        cosine[...], jnp.concatenate([colat, none, none, azimuth], axis=0), NT
    ) + dot(sines[...], jnp.concatenate([none, colat, azimuth, none], axis=0), NT)
    returned[...] = back.astype(BF16)


def cycle_transform(where, begins, counts, weights, slots, received):
    vmem = pl.BlockSpec(memory_space=pltpu.VMEM)
    smem = pl.BlockSpec(memory_space=pltpu.SMEM)
    orders = slots.size
    return pl.pallas_call(
        transform_kernel,
        out_shape=jax.ShapeDtypeStruct(received.shape, BF16),
        in_specs=[smem] * 4 + [vmem] * 2,
        out_specs=vmem,
        scratch_shapes=[pltpu.VMEM((orders, 2 * orders), BF16)] * 2,
        compiler_params=pltpu.CompilerParams(vmem_limit_bytes=40 << 20),
        cost_estimate=pl.CostEstimate(
            flops=600_000_000, bytes_accessed=3 << 20, transcendentals=0
        ),
        name="transform",
    )(where, begins, counts, weights, slots, received)


def trial_gram_kernel(
    trial, block1, block2, block3, own, home1, home2, home3, mine, sem
):
    n, _, _, degrees = trial.shape
    me = lax.axis_index("vert")
    copies = [
        pltpu.make_async_copy(trial.at[:, 2 * me + i], mine.at[i], sem.at[i]) for i in range(2)
    ]
    for copy in copies:
        copy.start()
    order = by_part(n)
    total = 0.0
    for i in range(2):
        copies[i].wait()
        parts = [
            dot(order, b.reshape(4 * n, degrees)).astype(BF16)
            for b in (mine[i], block1[i], block2[i], block3[i])
        ]
        for c in range(4):
            x = jnp.concatenate([p[c * n : (c + 1) * n] for p in parts], axis=0)
            total = total + dot(x, x, NT)
    for d, out in enumerate((own, home1, home2, home3)):
        rows = total[d * n : (d + 1) * n]
        out[...] = jnp.concatenate(
            [rows[:, (d - e) % 4 * n : ((d - e) % 4 + 1) * n] for e in range(4)], axis=1
        )


def trial_gram(trial, received):
    vectors, _, parts, degrees = trial.shape
    vmem = pl.BlockSpec(memory_space=pltpu.VMEM)
    return pl.pallas_call(
        trial_gram_kernel,
        out_shape=[jax.ShapeDtypeStruct((vectors, 4 * vectors), F32)] * 4,
        in_specs=[pl.BlockSpec(memory_space=pltpu.HBM)] + [vmem] * 3,
        scratch_shapes=[
            pltpu.VMEM((2, vectors, parts, degrees), BF16),
            pltpu.SemaphoreType.DMA((2,)),
        ],
        compiler_params=pltpu.CompilerParams(vmem_limit_bytes=32 << 20),
        cost_estimate=pl.CostEstimate(
            flops=600_000_000, bytes_accessed=2 << 20, transcendentals=0
        ),
        name="trial_gram",
    )(in_hbm(trial), *received)


def analyse_kernel(
    where, got0, got1, got2, got3, rows0, rows1, rows2, rows3, legendre,
    tt, applied, gram,
    got_v, rows_v, wide, adj, leg_v, tt_v, app_v, sem_g, sem_r, sem_l, sem_t, sem_o,
):
    orders, _, vectors, _ = tt.shape
    columns = 4 * vectors
    start = pl.multiple_of(where[0], 16)
    shift = where[1]

    def trial_copy(n):
        return pltpu.make_async_copy(tt.at[n], tt_v.at[n], sem_t.at[n])

    got_copies = [
        pltpu.make_async_copy(got, got_v.at[e], sem_g.at[e])
        for e, got in enumerate((got0, got1, got2, got3))
    ]
    row_copies = [
        pltpu.make_async_copy(rows, rows_v.at[e], sem_r.at[e])
        for e, rows in enumerate((rows0, rows1, rows2, rows3))
    ]
    for copy in got_copies:
        copy.start()
    for n in range(orders):
        window_copy(legendre, leg_v, sem_l, n, n, start).start()
        trial_copy(n).start()
    for copy in row_copies:
        copy.start()
    for e, copy in enumerate(got_copies):
        copy.wait()
        wide[e] = got_v[e].astype(F32)
    adj[...] = jnp.zeros_like(adj)
    lane = lax.broadcasted_iota(jnp.int32, (1, columns), 1) // vectors
    one = jnp.ones((1, columns), F32)
    sign0 = jnp.where(lane < 2, one, -one)
    sign1 = jnp.where((lane == 0) | (lane == 3), -one, one)
    cycles = got0.shape[0] // orders
    block = {0: 0, 1: 1, 3: 2, 2: 3}
    total = 0.0
    for n in range(orders):
        for e in range(4):
            x = wide[e, pl.ds(n, cycles, stride=orders), :]
            base = e * 2 * WINDOW + shift
            adj[pl.ds(base, cycles), :] = x * sign0
            adj[pl.ds(base + WINDOW, cycles), :] = pltpu.roll(x, columns // 2, 1) * sign1
        a = jnp.concatenate(
            [adj[e * 2 * WINDOW : (e + 1) * 2 * WINDOW].T for e in range(4)], axis=0
        ).astype(BF16)
        window_copy(legendre, leg_v, sem_l, n, n, start).wait()
        rows = dot(a, leg_v[n].reshape(2 * WINDOW, leg_v.shape[3])).astype(BF16)
        trial_copy(n).wait()
        for c in range(4):
            b = block[c] * vectors
            own = [rows[e * columns + b : e * columns + b + vectors] for e in range(4)]
            every = jnp.concatenate(own, axis=0)
            app_v[n, c] = every
            total = total + dot(every, jnp.concatenate([tt_v[n, c], own[0]], axis=0), NT)
        pltpu.make_async_copy(app_v.at[n], applied.at[n], sem_o.at[n]).start()
    for copy in row_copies:
        copy.wait()
    gram[:vectors] = (rows_v[0] + rows_v[1]) + (rows_v[2] + rows_v[3])
    gram[vectors:] = total.T
    for n in range(orders):
        pltpu.make_async_copy(app_v.at[n], applied.at[n], sem_o.at[n]).wait()


def analyse(where, gots, trial_rows, legendre, tt):
    orders, _, vectors, degrees = tt.shape
    cycles_rows, columns = gots[0].shape
    vmem = pl.BlockSpec(memory_space=pltpu.VMEM)
    hbm = pl.BlockSpec(memory_space=pltpu.HBM)
    return pl.pallas_call(
        analyse_kernel,
        out_shape=(
            pltpu.HBM((orders, 4, 4 * vectors, degrees), BF16),
            jax.ShapeDtypeStruct((3 * vectors, 4 * vectors), F32),
        ),
        in_specs=[pl.BlockSpec(memory_space=pltpu.SMEM)] + [hbm] * 10,
        out_specs=(hbm, vmem),
        scratch_shapes=[
            pltpu.VMEM((4, cycles_rows, columns), BF16),
            pltpu.VMEM((4, vectors, columns), F32),
            pltpu.VMEM((4, cycles_rows, columns), F32),
            pltpu.VMEM((4 * 2 * WINDOW, columns), F32),
            pltpu.VMEM((orders, 2, WINDOW, degrees), BF16),
            pltpu.VMEM((orders, 4, vectors, degrees), BF16),
            pltpu.VMEM((orders, 4, 4 * vectors, degrees), BF16),
            pltpu.SemaphoreType.DMA((4,)),
            pltpu.SemaphoreType.DMA((4,)),
            pltpu.SemaphoreType.DMA((orders,)),
            pltpu.SemaphoreType.DMA((orders,)),
            pltpu.SemaphoreType.DMA((orders,)),
        ],
        compiler_params=pltpu.CompilerParams(vmem_limit_bytes=40 << 20),
        cost_estimate=pl.CostEstimate(
            flops=2_000_000_000, bytes_accessed=14 << 20, transcendentals=0
        ),
        name="analyse",
    )(where, *gots, *trial_rows, in_hbm(legendre), in_hbm(tt))


def eliminate(work, n):
    shape = (PANEL, n)
    sub = lax.broadcasted_iota(jnp.int32, shape, 0)
    for j in range(0, n, PANEL):
        for which in range(work.shape[0]):
            top = work[which, j : j + PANEL, :n]
            value, low, inverse = {}, {}, []
            for m in range(PANEL):
                column = jnp.broadcast_to(top[:, j + m : j + m + 1], shape)
                for i in range(m, PANEL):
                    value[i, m] = jnp.broadcast_to(column[i : i + 1], shape)
            for m in range(PANEL):
                inverse.append(lax.rsqrt(value[m, m]))
                for i in range(m + 1, PANEL):
                    low[i, m] = value[i, m] * inverse[m]
                for i in range(m + 1, PANEL):
                    for k in range(m + 1, i + 1):
                        value[i, k] = value[i, k] - low[i, m] * low[k, m]

            def solved(base):
                rows = []
                for m in range(PANEL):
                    line = jnp.broadcast_to(
                        work[which, j + m : j + m + 1, base : base + n], shape
                    )
                    for k in range(m):
                        line = line - low[m, k] * rows[k]
                    rows.append(line * inverse[m])
                return rows

            left = solved(0) if j + PANEL < n else None
            right = solved(n)
            panel = right[0]
            for m in range(1, PANEL):
                panel = jnp.where(sub == m, right[m], panel)
            work[which, j : j + PANEL, n:] = panel
            for i in range(j + PANEL, n, PANEL):
                block = work[which, i : i + PANEL, :n]
                tail = work[which, i : i + PANEL, n:]
                factor = []
                for m in range(PANEL):
                    column = jnp.broadcast_to(block[:, j + m : j + m + 1], shape)
                    for k in range(m):
                        column = column - low[m, k] * factor[k]
                    factor.append(column * inverse[m])
                for m in range(PANEL):
                    block = block - factor[m] * left[m]
                    tail = tail - factor[m] * right[m]
                work[which, i : i + PANEL, :n] = block
                work[which, i : i + PANEL, n:] = tail


def finish_kernel(
    gram0, gram1, gram2, gram3, applied, new_basis, ritz,
    gram_v, work, cross, app_v, out_v, sem_g, sem_i, sem_o,
):
    n = cross.shape[0]
    vectors = n // 4
    orders, _, _, degrees = applied.shape
    coefficients = 512 * 4 * degrees
    gram_copies = [
        pltpu.make_async_copy(gram, gram_v.at[d], sem_g.at[d])
        for d, gram in enumerate((gram0, gram1, gram2, gram3))
    ]
    for copy in gram_copies:
        copy.start()
    for s in range(orders):
        pltpu.make_async_copy(applied.at[s], app_v.at[s], sem_i.at[s]).start()
    me = lax.axis_index("vert")
    unit = (
        lax.broadcasted_iota(jnp.int32, (n, n), 0)
        == lax.broadcasted_iota(jnp.int32, (n, n), 1)
    ).astype(F32)
    work[0, :, n:] = unit
    work[1, :, n:] = unit
    for d, copy in enumerate(gram_copies):
        copy.wait()
        group = (me + d) & 3
        rows = pltpu.roll(gram_v[d] * (1.0 / coefficients), group * vectors, 1)
        span = pl.ds(pl.multiple_of(group * vectors, vectors), vectors)
        work[0, span, :n] = rows[:vectors]
        cross[span, :] = rows[vectors : 2 * vectors]
        work[1, span, :n] = rows[2 * vectors :]
    eliminate(work, n)
    inverse_trial = work[0, :, n:]
    ritz[...] = dot_high(dot_high(inverse_trial, cross[...]), inverse_trial, NT)
    mine = work[1, pl.ds(pl.multiple_of(me * vectors, vectors), vectors), n:]
    mine = pltpu.roll(mine, ((4 - me) & 3) * vectors, 1).astype(BF16)
    i = lax.broadcasted_iota(jnp.int32, (n, vectors), 0)
    repeat = (i // 4 == lax.broadcasted_iota(jnp.int32, (n, vectors), 1)).astype(BF16)
    mine = dot(repeat, mine)
    part = lax.broadcasted_iota(jnp.int32, (n, n), 0) & 3
    weights = jnp.concatenate(
        [jnp.where(part == c, mine, 0.0) for c in range(4)], axis=1
    ).astype(BF16)

    def out_copy(s):
        return pltpu.make_async_copy(
            out_v.at[s], new_basis.at[:, s], sem_o.at[s]
        )

    for s in range(orders):
        pltpu.make_async_copy(applied.at[s], app_v.at[s], sem_i.at[s]).wait()
        y = dot(weights, app_v[s].reshape(4 * n, degrees)).astype(BF16)
        out_v[s] = y.reshape(vectors, 4, degrees)
        out_copy(s).start()
    for s in range(orders):
        out_copy(s).wait()


def finish(grams, applied):
    orders, _, n, degrees = applied.shape
    vectors = n // 4
    vmem = pl.BlockSpec(memory_space=pltpu.VMEM)
    hbm = pl.BlockSpec(memory_space=pltpu.HBM)
    return pl.pallas_call(
        finish_kernel,
        out_shape=(
            jax.ShapeDtypeStruct((vectors, orders, 4, degrees), BF16),
            jax.ShapeDtypeStruct((n, n), F32),
        ),
        in_specs=[hbm] * 5,
        out_specs=(hbm, vmem),
        scratch_shapes=[
            pltpu.VMEM((4, *grams[0].shape), F32),
            pltpu.VMEM((2, n, 2 * n), F32),
            pltpu.VMEM((n, n), F32),
            pltpu.VMEM((orders, 4, n, degrees), BF16),
            pltpu.VMEM((orders, vectors, 4, degrees), BF16),
            pltpu.SemaphoreType.DMA((4,)),
            pltpu.SemaphoreType.DMA((orders,)),
            pltpu.SemaphoreType.DMA((orders,)),
        ],
        compiler_params=pltpu.CompilerParams(vmem_limit_bytes=40 << 20),
        cost_estimate=pl.CostEstimate(
            flops=1_200_000_000, bytes_accessed=11 << 20, transcendentals=0
        ),
        name="finish",
    )(*grams, in_hbm(applied))


def swap(value, axis, size, bit):
    return lax.ppermute(value, axis, [(i, i ^ bit) for i in range(size)])


def sum_of_four(value, axis, size):
    one, two, three = (swap(value, axis, size, bit) for bit in (1, 2, 3))
    return (value + one) + (two + three)


def sum_over_ma(value):
    value = value + swap(value, "ma_2", 2, 1)
    value = sum_of_four(value, "ma_1", 8)
    value = value + swap(value, "ma_1", 8, 4)
    return sum_of_four(value, "ma_0", 4)


def from_groups(value):
    return [value] + [lax.ppermute(value, "vert", ring(4, -d)) for d in (1, 2, 3)]


def shards(trial_block, legendre, order_slot, cycle_start, cycle_count, cycle_weight):
    vectors, orders, _, _ = trial_block.shape
    live = legendre.shape[2] // 4
    columns = 4 * vectors

    fields, *sent, where = synthesize(
        cycle_count.reshape(-1, 128), trial_block, legendre, live
    )
    blocks = [lax.ppermute(x, "vert", ring(4, d)) for d, x in enumerate(sent, 1)]
    received = lax.all_to_all(fields, MA, split_axis=0, concat_axis=0, tiled=True)
    tt = arrange(trial_block)
    received, tt = lax.optimization_barrier((received, tt))
    returned = cycle_transform(
        where, cycle_start, cycle_count, cycle_weight, order_slot.reshape(-1, 128),
        received.reshape(live * orders, columns),
    )
    order_fields = lax.all_to_all(
        returned.reshape(live, orders, columns), MA, split_axis=0, concat_axis=0, tiled=True
    )
    shares = trial_gram(trial_block, blocks)
    trial_rows = [shares[0]] + [
        lax.ppermute(shares[d], "vert", ring(4, -d)) for d in (1, 2, 3)
    ]
    order_fields, *trial_rows = lax.optimization_barrier((order_fields, *trial_rows))
    gots = from_groups(order_fields.reshape(live * orders, columns))
    applied, gram = analyse(where, gots, trial_rows, legendre, tt)
    return tuple(finish(from_groups(sum_over_ma(gram)), applied))


def solution(mesh):
    split = Mesh(
        mesh.devices.reshape(4, 8, 2, mesh.shape["vert"]), ("ma_0", "ma_1", "ma_2", "vert")
    )
    placed = (P("vert", MA, None, None), P(MA, None, None, None), P(), P(), P(), P())
    return jax.shard_map(
        shards,
        mesh=split,
        in_specs=placed,
        out_specs=(P("vert", MA, None, None), P()),
        check_vma=False,
    )
```

```python
import math

import jax
import jax.numpy as jnp
from jax import lax
from jax.experimental import pallas as pl
from jax.experimental.pallas import tpu as pltpu
from jax.sharding import Mesh
from jax.sharding import PartitionSpec as P

MA = ("ma_0", "ma_1", "ma_2")
F32 = jnp.float32
BF16 = jnp.bfloat16
WINDOW = 80
PANEL = 8
COEFFICIENTS = 512 * 4 * 1024
NT = (((1,), (1,)), ((), ()))
NN = (((1,), (0,)), ((), ()))


def ring(size, shift):
    return [(i, (i + shift) % size) for i in range(size)]


def dot(a, b, dims=NN):
    return lax.dot_general(a, b, dims, preferred_element_type=F32)


def in_hbm(value):
    return pltpu.with_memory_space_constraint(value, pltpu.HBM)


def dot_high(a, b, dims=NN):
    return lax.dot_general(
        a, b, dims, precision=lax.Precision.HIGHEST, preferred_element_type=F32
    )


def window_copy(legendre, leg_v, sem, s, slot, start):
    return pltpu.make_async_copy(
        legendre.at[s, :, pl.ds(start, WINDOW), :], leg_v.at[slot], sem.at[slot]
    )


def by_part(vectors):
    shape = (4 * vectors, 4 * vectors)
    i = lax.broadcasted_iota(jnp.int32, shape, 0)
    j = lax.broadcasted_iota(jnp.int32, shape, 1)
    return (j == (i % vectors) * 4 + i // vectors).astype(BF16)


def synthesize_kernel(
    counts, trial, legendre, fields, sent1, sent2, sent3, where,
    tr_v, leg_v, one, two, prod, sem_t, sem_l, sem_o,
):
    vectors, orders = trial.shape[:2]
    me = lax.axis_index("vert")
    pair = orders // 4

    def send_copies():
        for d, out in enumerate((sent1, sent2, sent3)):
            yield pltpu.make_async_copy(
                tr_v.at[pl.ds((me + d + 1) % 4 * pair, pair)], out, sem_o.at[d]
            )

    for s in range(orders):
        pltpu.make_async_copy(trial.at[:, s], tr_v.at[s], sem_t.at[s]).start()
    live = counts[...] > 0
    cycle = lax.broadcasted_iota(jnp.int32, live.shape, 0) * live.shape[1]
    cycle = cycle + lax.broadcasted_iota(jnp.int32, live.shape, 1)
    last = legendre.shape[2] - fields.shape[0]
    first = jnp.min(jnp.where(live, cycle, last).astype(F32)).astype(jnp.int32)
    start = jnp.minimum((first // 16) * 16, legendre.shape[2] - WINDOW)
    start = pl.multiple_of(start, 16)
    shift = first - start
    where[0] = start
    where[1] = shift
    for s in range(orders):
        window_copy(legendre, leg_v, sem_l, s, s, start).start()
    for s in range(orders):
        pltpu.make_async_copy(trial.at[:, s], tr_v.at[s], sem_t.at[s]).wait()
        x = tr_v[s].reshape(4 * vectors, tr_v.shape[3])
        window_copy(legendre, leg_v, sem_l, s, s, start).wait()
        slot = s % 2
        one[slot, :, :WINDOW] = dot(x, leg_v[s, 0], NT)
        two[slot, :, :WINDOW] = dot(x, leg_v[s, 1], NT)
        w, x = (
            [ref[slot, pl.ds(c, vectors, stride=4), :] for c in range(4)]
            for ref in (one, two)
        )
        f = jnp.concatenate([w[0] + x[3], w[1] - x[2], -x[0] - w[3], x[1] - w[2]], axis=0)
        prod[s * WINDOW : (s + 1) * WINDOW] = f.T[:WINDOW]
        if s == orders - 1:
            for copy in send_copies():
                copy.start()
    for r in range(fields.shape[0]):
        fields[r] = prod[pl.ds(shift + r, orders, stride=WINDOW), :].astype(BF16)
    for copy in send_copies():
        copy.wait()


def synthesize(counts, trial, legendre, cycles):
    vectors, orders, _, degrees = trial.shape
    columns = 4 * vectors
    hbm = pl.BlockSpec(memory_space=pltpu.HBM)
    vmem = pl.BlockSpec(memory_space=pltpu.VMEM)
    sent = pltpu.HBM((orders // 4, vectors, 4, degrees), BF16)
    return pl.pallas_call(
        synthesize_kernel,
        out_shape=(
            jax.ShapeDtypeStruct((cycles, orders, columns), BF16),
            sent,
            sent,
            sent,
            jax.ShapeDtypeStruct((2,), jnp.int32),
        ),
        in_specs=[vmem, hbm, hbm],
        out_specs=(vmem, hbm, hbm, hbm, pl.BlockSpec(memory_space=pltpu.SMEM)),
        scratch_shapes=[
            pltpu.VMEM((orders, vectors, 4, degrees), BF16),
            pltpu.VMEM((orders, 2, WINDOW, degrees), BF16),
            pltpu.VMEM((2, columns, 128), F32),
            pltpu.VMEM((2, columns, 128), F32),
            pltpu.VMEM((orders * WINDOW, columns), F32),
            pltpu.SemaphoreType.DMA((orders,)),
            pltpu.SemaphoreType.DMA((orders,)),
            pltpu.SemaphoreType.DMA((3,)),
        ],
        compiler_params=pltpu.CompilerParams(vmem_limit_bytes=40 << 20),
        cost_estimate=pl.CostEstimate(
            flops=600_000_000, bytes_accessed=5 << 20, transcendentals=0
        ),
        name="synthesize",
    )(counts, in_hbm(trial), in_hbm(legendre))


def arrange_kernel(trial, tt, tr_v, tt_v, sem_t, sem_o):
    vectors, orders = trial.shape[:2]
    for s in range(orders):
        pltpu.make_async_copy(trial.at[:, s], tr_v.at[s], sem_t.at[s]).start()
    order = by_part(vectors)
    for s in range(orders):
        pltpu.make_async_copy(trial.at[:, s], tr_v.at[s], sem_t.at[s]).wait()
        t = dot(order, tr_v[s].reshape(4 * vectors, tr_v.shape[3])).astype(BF16)
        for c in range(4):
            tt_v[s, c] = t[c * vectors : (c + 1) * vectors]
        pltpu.make_async_copy(tt_v.at[s], tt.at[s], sem_o.at[s]).start()
    for s in range(orders):
        pltpu.make_async_copy(tt_v.at[s], tt.at[s], sem_o.at[s]).wait()


def arrange(trial):
    vectors, orders, _, degrees = trial.shape
    hbm = pl.BlockSpec(memory_space=pltpu.HBM)
    return pl.pallas_call(
        arrange_kernel,
        out_shape=pltpu.HBM((orders, 4, vectors, degrees), BF16),
        in_specs=[hbm],
        out_specs=hbm,
        scratch_shapes=[
            pltpu.VMEM((orders, vectors, 4, degrees), BF16),
            pltpu.VMEM((orders, 4, vectors, degrees), BF16),
            pltpu.SemaphoreType.DMA((orders,)),
            pltpu.SemaphoreType.DMA((orders,)),
        ],
        compiler_params=pltpu.CompilerParams(vmem_limit_bytes=40 << 20),
        cost_estimate=pl.CostEstimate(
            flops=300_000_000, bytes_accessed=4 << 20, transcendentals=0
        ),
        name="arrange",
    )(in_hbm(trial))


def quarter_sine(x):
    y = x * x
    sine = 1.0 + y * (-1 / 6 + y * (1 / 120 + y * (-1 / 5040 + y * (1 / 362880 + y * (-1 / 39916800)))))
    cosine = 1.0 + y * (
        -1 / 2 + y * (1 / 24 + y * (-1 / 720 + y * (1 / 40320 + y * (-1 / 3628800 + y * (1 / 479001600)))))
    )
    return sine * x, cosine


def turn(phase, longitudes):
    quarter = longitudes // 4
    s, c = quarter_sine((phase & (quarter - 1)).astype(F32) * (2.0 * math.pi / longitudes))
    quadrant = phase // quarter
    swapped = (quadrant & 1) == 1
    sine = jnp.where(swapped, c, s)
    cosine = jnp.where(swapped, s, c)
    sine = jnp.where(quadrant >= 2, -sine, sine)
    cosine = jnp.where((quadrant == 1) | (quadrant == 2), -cosine, cosine)
    return sine, cosine


def transform_kernel(
    where, begins, counts, weights, slots, received, returned, cosine, sines
):
    orders, longitudes = cosine.shape
    lanes = slots.shape[1]
    columns = received.shape[1]
    part = columns // 4
    scale = 1.0 / math.sqrt(orders)
    near = lax.broadcasted_iota(jnp.int32, (lanes, lanes), 1)
    for g in range(slots.shape[0]):
        m = jnp.broadcast_to(slots[g : g + 1, :].astype(F32), (lanes, lanes)).T
        m = m.astype(jnp.int32)
        span = slice(g * lanes, (g + 1) * lanes)
        step_s, step_c = turn((m * lanes) & (longitudes - 1), longitudes)
        s, c = turn((m * near) & (longitudes - 1), longitudes)
        s, c = s * scale, c * scale
        for b in range(longitudes // lanes):
            cosine[span, b * lanes : (b + 1) * lanes] = c.astype(BF16)
            sines[span, b * lanes : (b + 1) * lanes] = s.astype(BF16)
            s, c = s * step_c + c * step_s, c * step_c - s * step_s

    home = (lax.axis_index("ma_0") * 8 + lax.axis_index("ma_1")) * 2 + lax.axis_index("ma_2")
    r = where[0] + where[1] + home
    j = lax.broadcasted_iota(jnp.int32, (1, longitudes), 1)
    inside = ((j - begins[r]) & (longitudes - 1)) < counts[r]
    factor = jnp.where(inside, weights[r], 0.0)

    ft = received[...].astype(F32).T.astype(BF16)
    with_cos = jnp.concatenate([ft[:part], ft[3 * part :]], axis=0)
    with_sin = ft[part : 3 * part]
    grid = dot(with_cos, cosine[...]) + dot(with_sin, sines[...])
    weighted = (grid * factor).astype(BF16)
    colat, azimuth = weighted[:part], weighted[part:]
    none = jnp.zeros_like(colat)
    back = dot(
        cosine[...], jnp.concatenate([colat, none, none, azimuth], axis=0), NT
    ) + dot(sines[...], jnp.concatenate([none, colat, azimuth, none], axis=0), NT)
    returned[...] = back.astype(BF16)


def cycle_transform(where, begins, counts, weights, slots, received):
    vmem = pl.BlockSpec(memory_space=pltpu.VMEM)
    smem = pl.BlockSpec(memory_space=pltpu.SMEM)
    orders = slots.size
    return pl.pallas_call(
        transform_kernel,
        out_shape=jax.ShapeDtypeStruct(received.shape, BF16),
        in_specs=[smem] * 4 + [vmem] * 2,
        out_specs=vmem,
        scratch_shapes=[pltpu.VMEM((orders, 2 * orders), BF16)] * 2,
        compiler_params=pltpu.CompilerParams(vmem_limit_bytes=40 << 20),
        cost_estimate=pl.CostEstimate(
            flops=600_000_000, bytes_accessed=3 << 20, transcendentals=0
        ),
        name="transform",
    )(where, begins, counts, weights, slots, received)


def trial_gram_kernel(
    trial, block1, block2, block3, own, home1, home2, home3, mine, sem
):
    n, _, _, degrees = trial.shape
    me = lax.axis_index("vert")
    copies = [
        pltpu.make_async_copy(trial.at[:, 2 * me + i], mine.at[i], sem.at[i]) for i in range(2)
    ]
    for copy in copies:
        copy.start()
    order = by_part(n)
    total = 0.0
    for i in range(2):
        copies[i].wait()
        parts = [
            dot(order, b.reshape(4 * n, degrees)).astype(BF16)
            for b in (mine[i], block1[i], block2[i], block3[i])
        ]
        for c in range(4):
            x = jnp.concatenate([p[c * n : (c + 1) * n] for p in parts], axis=0)
            total = total + dot(x, x, NT)
    for d, out in enumerate((own, home1, home2, home3)):
        rows = total[d * n : (d + 1) * n]
        out[...] = jnp.concatenate(
            [rows[:, (d - e) % 4 * n : ((d - e) % 4 + 1) * n] for e in range(4)], axis=1
        )


def trial_gram(trial, received):
    vectors, _, parts, degrees = trial.shape
    vmem = pl.BlockSpec(memory_space=pltpu.VMEM)
    return pl.pallas_call(
        trial_gram_kernel,
        out_shape=[jax.ShapeDtypeStruct((vectors, 4 * vectors), F32)] * 4,
        in_specs=[pl.BlockSpec(memory_space=pltpu.HBM)] + [vmem] * 3,
        scratch_shapes=[
            pltpu.VMEM((2, vectors, parts, degrees), BF16),
            pltpu.SemaphoreType.DMA((2,)),
        ],
        compiler_params=pltpu.CompilerParams(vmem_limit_bytes=32 << 20),
        cost_estimate=pl.CostEstimate(
            flops=600_000_000, bytes_accessed=2 << 20, transcendentals=0
        ),
        name="trial_gram",
    )(in_hbm(trial), *received)


def analyse_kernel(
    where, got0, got1, got2, got3, rows0, rows1, rows2, rows3, legendre,
    tt, applied, gram,
    got_v, rows_v, wide, adj, leg_v, tt_v, sem_g, sem_r, sem_l, sem_t,
):
    orders, _, vectors, _ = tt.shape
    columns = 4 * vectors
    start = pl.multiple_of(where[0], 16)
    shift = where[1]

    def trial_copy(n):
        return pltpu.make_async_copy(tt.at[n], tt_v.at[n], sem_t.at[n])

    got_copies = [
        pltpu.make_async_copy(got, got_v.at[e], sem_g.at[e])
        for e, got in enumerate((got0, got1, got2, got3))
    ]
    row_copies = [
        pltpu.make_async_copy(rows, rows_v.at[e], sem_r.at[e])
        for e, rows in enumerate((rows0, rows1, rows2, rows3))
    ]
    for copy in got_copies:
        copy.start()
    for n in range(orders):
        window_copy(legendre, leg_v, sem_l, n, n, start).start()
        trial_copy(n).start()
    for copy in row_copies:
        copy.start()
    for e, copy in enumerate(got_copies):
        copy.wait()
        wide[e] = got_v[e].astype(F32)
    adj[...] = jnp.zeros_like(adj)
    lane = lax.broadcasted_iota(jnp.int32, (1, columns), 1) // vectors
    one = jnp.ones((1, columns), F32)
    sign0 = jnp.where(lane < 2, one, -one)
    sign1 = jnp.where((lane == 0) | (lane == 3), -one, one)
    cycles = got0.shape[0] // orders
    block = {0: 0, 1: 1, 3: 2, 2: 3}
    total = 0.0
    for n in range(orders):
        for e in range(4):
            x = wide[e, pl.ds(n, cycles, stride=orders), :]
            base = e * 2 * WINDOW + shift
            adj[pl.ds(base, cycles), :] = x * sign0
            adj[pl.ds(base + WINDOW, cycles), :] = pltpu.roll(x, columns // 2, 1) * sign1
        a = jnp.concatenate(
            [adj[e * 2 * WINDOW : (e + 1) * 2 * WINDOW].T for e in range(4)], axis=0
        ).astype(BF16)
        window_copy(legendre, leg_v, sem_l, n, n, start).wait()
        rows = dot(a, leg_v[n].reshape(2 * WINDOW, leg_v.shape[3])).astype(BF16)
        trial_copy(n).wait()
        for c in range(4):
            b = block[c] * vectors
            own = [rows[e * columns + b : e * columns + b + vectors] for e in range(4)]
            every = jnp.concatenate(own, axis=0)
            applied[n, c] = every
            total = total + dot(every, jnp.concatenate([tt_v[n, c], own[0]], axis=0), NT)
    for copy in row_copies:
        copy.wait()
    gram[:vectors] = (rows_v[0] + rows_v[1]) + (rows_v[2] + rows_v[3])
    gram[vectors:] = total.T


def analyse(where, gots, trial_rows, legendre, tt):
    orders, _, vectors, degrees = tt.shape
    cycles_rows, columns = gots[0].shape
    vmem = pl.BlockSpec(memory_space=pltpu.VMEM)
    hbm = pl.BlockSpec(memory_space=pltpu.HBM)
    return pl.pallas_call(
        analyse_kernel,
        out_shape=(
            jax.ShapeDtypeStruct((orders, 4, 4 * vectors, degrees), BF16),
            jax.ShapeDtypeStruct((3 * vectors, 4 * vectors), F32),
        ),
        in_specs=[pl.BlockSpec(memory_space=pltpu.SMEM)] + [hbm] * 10,
        out_specs=(vmem, vmem),
        scratch_shapes=[
            pltpu.VMEM((4, cycles_rows, columns), BF16),
            pltpu.VMEM((4, vectors, columns), F32),
            pltpu.VMEM((4, cycles_rows, columns), F32),
            pltpu.VMEM((4 * 2 * WINDOW, columns), F32),
            pltpu.VMEM((orders, 2, WINDOW, degrees), BF16),
            pltpu.VMEM((orders, 4, vectors, degrees), BF16),
            pltpu.SemaphoreType.DMA((4,)),
            pltpu.SemaphoreType.DMA((4,)),
            pltpu.SemaphoreType.DMA((orders,)),
            pltpu.SemaphoreType.DMA((orders,)),
        ],
        compiler_params=pltpu.CompilerParams(vmem_limit_bytes=40 << 20),
        cost_estimate=pl.CostEstimate(
            flops=2_000_000_000, bytes_accessed=14 << 20, transcendentals=0
        ),
        name="analyse",
    )(where, *gots, *trial_rows, in_hbm(legendre), in_hbm(tt))


def eliminate(work, n):
    shape = (PANEL, n)
    sub = lax.broadcasted_iota(jnp.int32, shape, 0)
    for j in range(0, n, PANEL):
        for which in range(work.shape[0]):
            top = work[which, j : j + PANEL, :n]
            value, low, inverse = {}, {}, []
            for m in range(PANEL):
                column = jnp.broadcast_to(top[:, j + m : j + m + 1], shape)
                for i in range(m, PANEL):
                    value[i, m] = jnp.broadcast_to(column[i : i + 1], shape)
            for m in range(PANEL):
                inverse.append(lax.rsqrt(value[m, m]))
                for i in range(m + 1, PANEL):
                    low[i, m] = value[i, m] * inverse[m]
                for i in range(m + 1, PANEL):
                    for k in range(m + 1, i + 1):
                        value[i, k] = value[i, k] - low[i, m] * low[k, m]

            def solved(base):
                rows = []
                for m in range(PANEL):
                    line = jnp.broadcast_to(
                        work[which, j + m : j + m + 1, base : base + n], shape
                    )
                    for k in range(m):
                        line = line - low[m, k] * rows[k]
                    rows.append(line * inverse[m])
                return rows

            left = solved(0) if j + PANEL < n else None
            right = solved(n)
            panel = right[0]
            for m in range(1, PANEL):
                panel = jnp.where(sub == m, right[m], panel)
            work[which, j : j + PANEL, n:] = panel
            for i in range(j + PANEL, n, PANEL):
                block = work[which, i : i + PANEL, :n]
                tail = work[which, i : i + PANEL, n:]
                factor = []
                for m in range(PANEL):
                    column = jnp.broadcast_to(block[:, j + m : j + m + 1], shape)
                    for k in range(m):
                        column = column - low[m, k] * factor[k]
                    factor.append(column * inverse[m])
                for m in range(PANEL):
                    block = block - factor[m] * left[m]
                    tail = tail - factor[m] * right[m]
                work[which, i : i + PANEL, :n] = block
                work[which, i : i + PANEL, n:] = tail


def factors_kernel(
    gram0, gram1, gram2, gram3, weights, ritz, gram_v, work, cross, sem
):
    n = cross.shape[0]
    vectors = n // 4
    copies = [
        pltpu.make_async_copy(gram, gram_v.at[d], sem.at[d])
        for d, gram in enumerate((gram0, gram1, gram2, gram3))
    ]
    for copy in copies:
        copy.start()
    me = lax.axis_index("vert")
    unit = (
        lax.broadcasted_iota(jnp.int32, (n, n), 0)
        == lax.broadcasted_iota(jnp.int32, (n, n), 1)
    ).astype(F32)
    work[0, :, n:] = unit
    work[1, :, n:] = unit
    for d, copy in enumerate(copies):
        copy.wait()
        group = (me + d) & 3
        rows = pltpu.roll(gram_v[d] * (1.0 / COEFFICIENTS), group * vectors, 1)
        span = pl.ds(pl.multiple_of(group * vectors, vectors), vectors)
        work[0, span, :n] = rows[:vectors]
        cross[span, :] = rows[vectors : 2 * vectors]
        work[1, span, :n] = rows[2 * vectors :]
    eliminate(work, n)
    inverse_trial = work[0, :, n:]
    ritz[...] = dot_high(dot_high(inverse_trial, cross[...]), inverse_trial, NT)
    mine = work[1, pl.ds(pl.multiple_of(me * vectors, vectors), vectors), n:]
    mine = pltpu.roll(mine, ((4 - me) & 3) * vectors, 1).astype(BF16)
    i = lax.broadcasted_iota(jnp.int32, (n, vectors), 0)
    repeat = (i // 4 == lax.broadcasted_iota(jnp.int32, (n, vectors), 1)).astype(BF16)
    mine = dot(repeat, mine)
    part = lax.broadcasted_iota(jnp.int32, (n, n), 0) & 3
    weights[...] = jnp.concatenate(
        [jnp.where(part == c, mine, 0.0) for c in range(4)], axis=1
    ).astype(BF16)


def factors(grams):
    rows, n = grams[0].shape
    vmem = pl.BlockSpec(memory_space=pltpu.VMEM)
    return pl.pallas_call(
        factors_kernel,
        out_shape=(
            jax.ShapeDtypeStruct((n, 4 * n), BF16),
            jax.ShapeDtypeStruct((n, n), F32),
        ),
        in_specs=[pl.BlockSpec(memory_space=pltpu.HBM)] * 4,
        out_specs=(vmem, vmem),
        scratch_shapes=[
            pltpu.VMEM((4, rows, n), F32),
            pltpu.VMEM((2, n, 2 * n), F32),
            pltpu.VMEM((n, n), F32),
            pltpu.SemaphoreType.DMA((4,)),
        ],
        compiler_params=pltpu.CompilerParams(vmem_limit_bytes=16 << 20),
        cost_estimate=pl.CostEstimate(
            flops=100_000_000, bytes_accessed=1 << 20, transcendentals=0
        ),
        name="factors",
    )(*grams)


def mix_kernel(weights, applied, new_basis, out_v, sem):
    orders, parts, n, degrees = applied.shape
    for s in range(orders):
        y = dot(weights[...], applied[s].reshape(parts * n, degrees)).astype(BF16)
        out_v[s] = y.reshape(n // 4, 4, degrees)
        pltpu.make_async_copy(out_v.at[s], new_basis.at[:, s], sem.at[s]).start()
    for s in range(orders):
        pltpu.make_async_copy(out_v.at[s], new_basis.at[:, s], sem.at[s]).wait()


def mix(weights, applied):
    orders, _, n, degrees = applied.shape
    vmem = pl.BlockSpec(memory_space=pltpu.VMEM)
    return pl.pallas_call(
        mix_kernel,
        out_shape=pltpu.HBM((n // 4, orders, 4, degrees), BF16),
        in_specs=[vmem, vmem],
        out_specs=pl.BlockSpec(memory_space=pltpu.HBM),
        scratch_shapes=[
            pltpu.VMEM((orders, n // 4, 4, degrees), BF16),
            pltpu.SemaphoreType.DMA((orders,)),
        ],
        compiler_params=pltpu.CompilerParams(vmem_limit_bytes=32 << 20),
        cost_estimate=pl.CostEstimate(
            flops=1_100_000_000, bytes_accessed=10 << 20, transcendentals=0
        ),
        name="mix",
    )(weights, applied)


def swap(value, axis, size, bit):
    return lax.ppermute(value, axis, [(i, i ^ bit) for i in range(size)])


def sum_of_four(value, axis, size):
    one, two, three = (swap(value, axis, size, bit) for bit in (1, 2, 3))
    return (value + one) + (two + three)


def sum_over_ma(value):
    value = value + swap(value, "ma_2", 2, 1)
    value = sum_of_four(value, "ma_1", 8)
    value = value + swap(value, "ma_1", 8, 4)
    return sum_of_four(value, "ma_0", 4)


def from_groups(value):
    return [value] + [lax.ppermute(value, "vert", ring(4, -d)) for d in (1, 2, 3)]


def shards(trial_block, legendre, order_slot, cycle_start, cycle_count, cycle_weight):
    vectors, orders, _, _ = trial_block.shape
    live = legendre.shape[2] // 4
    columns = 4 * vectors

    fields, *sent, where = synthesize(
        cycle_count.reshape(-1, 128), trial_block, legendre, live
    )
    blocks = [lax.ppermute(x, "vert", ring(4, d)) for d, x in enumerate(sent, 1)]
    received = lax.all_to_all(fields, MA, split_axis=0, concat_axis=0, tiled=True)
    tt = arrange(trial_block)
    received, tt = lax.optimization_barrier((received, tt))
    returned = cycle_transform(
        where, cycle_start, cycle_count, cycle_weight, order_slot.reshape(-1, 128),
        received.reshape(live * orders, columns),
    )
    order_fields = lax.all_to_all(
        returned.reshape(live, orders, columns), MA, split_axis=0, concat_axis=0, tiled=True
    )
    shares = trial_gram(trial_block, blocks)
    trial_rows = [shares[0]] + [
        lax.ppermute(shares[d], "vert", ring(4, -d)) for d in (1, 2, 3)
    ]
    order_fields, *trial_rows = lax.optimization_barrier((order_fields, *trial_rows))
    gots = from_groups(order_fields.reshape(live * orders, columns))
    applied, gram = analyse(where, gots, trial_rows, legendre, tt)
    weights, ritz_matrix = factors(from_groups(sum_over_ma(gram)))
    return (mix(weights, applied), ritz_matrix)


def solution(mesh):
    split = Mesh(
        mesh.devices.reshape(4, 8, 2, mesh.shape["vert"]), ("ma_0", "ma_1", "ma_2", "vert")
    )
    placed = (P("vert", MA, None, None), P(MA, None, None, None), P(), P(), P(), P())
    return jax.shard_map(
        shards,
        mesh=split,
        in_specs=placed,
        out_specs=(P("vert", MA, None, None), P()),
        check_vma=False,
    )
```

```python
import math

import jax
import jax.numpy as jnp
from jax import lax
from jax.experimental import pallas as pl
from jax.experimental.pallas import tpu as pltpu
from jax.sharding import Mesh
from jax.sharding import PartitionSpec as P

MA = ("ma_0", "ma_1", "ma_2")
F32 = jnp.float32
BF16 = jnp.bfloat16
WINDOW = 80
PANEL = 8
COEFFICIENTS = 512 * 4 * 1024
NT = (((1,), (1,)), ((), ()))
NN = (((1,), (0,)), ((), ()))


def ring(size, shift):
    return [(i, (i + shift) % size) for i in range(size)]


def dot(a, b, dims=NN):
    return lax.dot_general(a, b, dims, preferred_element_type=F32)


def in_hbm(value):
    return pltpu.with_memory_space_constraint(value, pltpu.HBM)


def dot_high(a, b, dims=NN):
    return lax.dot_general(
        a, b, dims, precision=lax.Precision.HIGHEST, preferred_element_type=F32
    )


def window_copy(legendre, leg_v, sem, s, slot, start):
    return pltpu.make_async_copy(
        legendre.at[s, :, pl.ds(start, WINDOW), :], leg_v.at[slot], sem.at[slot]
    )


def by_part(vectors):
    shape = (4 * vectors, 4 * vectors)
    i = lax.broadcasted_iota(jnp.int32, shape, 0)
    j = lax.broadcasted_iota(jnp.int32, shape, 1)
    return (j == (i % vectors) * 4 + i // vectors).astype(BF16)


def synthesize_kernel(
    counts, trial, legendre, fields, sent1, sent2, sent3, where,
    tr_v, leg_v, one, two, prod, sem_t, sem_l, sem_o,
):
    vectors, orders = trial.shape[:2]
    me = lax.axis_index("vert")
    pair = orders // 4

    def send_copies():
        for d, out in enumerate((sent1, sent2, sent3)):
            yield pltpu.make_async_copy(
                tr_v.at[pl.ds((me + d + 1) % 4 * pair, pair)], out, sem_o.at[d]
            )

    for s in range(orders):
        pltpu.make_async_copy(trial.at[:, s], tr_v.at[s], sem_t.at[s]).start()
    live = counts[...] > 0
    cycle = lax.broadcasted_iota(jnp.int32, live.shape, 0) * live.shape[1]
    cycle = cycle + lax.broadcasted_iota(jnp.int32, live.shape, 1)
    last = legendre.shape[2] - fields.shape[0]
    first = jnp.min(jnp.where(live, cycle, last).astype(F32)).astype(jnp.int32)
    start = jnp.minimum((first // 16) * 16, legendre.shape[2] - WINDOW)
    start = pl.multiple_of(start, 16)
    shift = first - start
    where[0] = start
    where[1] = shift
    for s in range(orders):
        window_copy(legendre, leg_v, sem_l, s, s, start).start()
    for s in range(orders):
        pltpu.make_async_copy(trial.at[:, s], tr_v.at[s], sem_t.at[s]).wait()
        x = tr_v[s].reshape(4 * vectors, tr_v.shape[3])
        window_copy(legendre, leg_v, sem_l, s, s, start).wait()
        slot = s % 2
        one[slot, :, :WINDOW] = dot(x, leg_v[s, 0], NT)
        two[slot, :, :WINDOW] = dot(x, leg_v[s, 1], NT)
        w, x = (
            [ref[slot, pl.ds(c, vectors, stride=4), :] for c in range(4)]
            for ref in (one, two)
        )
        f = jnp.concatenate([w[0] + x[3], w[1] - x[2], -x[0] - w[3], x[1] - w[2]], axis=0)
        prod[s * WINDOW : (s + 1) * WINDOW] = f.T[:WINDOW]
        if s == orders - 1:
            for copy in send_copies():
                copy.start()
    for r in range(fields.shape[0]):
        fields[r] = prod[pl.ds(shift + r, orders, stride=WINDOW), :].astype(BF16)
    for copy in send_copies():
        copy.wait()


def synthesize(counts, trial, legendre, cycles):
    vectors, orders, _, degrees = trial.shape
    columns = 4 * vectors
    hbm = pl.BlockSpec(memory_space=pltpu.HBM)
    vmem = pl.BlockSpec(memory_space=pltpu.VMEM)
    sent = pltpu.HBM((orders // 4, vectors, 4, degrees), BF16)
    return pl.pallas_call(
        synthesize_kernel,
        out_shape=(
            jax.ShapeDtypeStruct((cycles, orders, columns), BF16),
            sent,
            sent,
            sent,
            jax.ShapeDtypeStruct((2,), jnp.int32),
        ),
        in_specs=[vmem, hbm, hbm],
        out_specs=(vmem, hbm, hbm, hbm, pl.BlockSpec(memory_space=pltpu.SMEM)),
        scratch_shapes=[
            pltpu.VMEM((orders, vectors, 4, degrees), BF16),
            pltpu.VMEM((orders, 2, WINDOW, degrees), BF16),
            pltpu.VMEM((2, columns, 128), F32),
            pltpu.VMEM((2, columns, 128), F32),
            pltpu.VMEM((orders * WINDOW, columns), F32),
            pltpu.SemaphoreType.DMA((orders,)),
            pltpu.SemaphoreType.DMA((orders,)),
            pltpu.SemaphoreType.DMA((3,)),
        ],
        compiler_params=pltpu.CompilerParams(vmem_limit_bytes=40 << 20),
        cost_estimate=pl.CostEstimate(
            flops=600_000_000, bytes_accessed=5 << 20, transcendentals=0
        ),
        name="synthesize",
    )(counts, in_hbm(trial), in_hbm(legendre))


def arrange_kernel(trial, tt, tr_v, tt_v, sem_t, sem_o):
    vectors, orders = trial.shape[:2]
    for s in range(orders):
        pltpu.make_async_copy(trial.at[:, s], tr_v.at[s], sem_t.at[s]).start()
    order = by_part(vectors)
    for s in range(orders):
        pltpu.make_async_copy(trial.at[:, s], tr_v.at[s], sem_t.at[s]).wait()
        t = dot(order, tr_v[s].reshape(4 * vectors, tr_v.shape[3])).astype(BF16)
        for c in range(4):
            tt_v[s, c] = t[c * vectors : (c + 1) * vectors]
        pltpu.make_async_copy(tt_v.at[s], tt.at[s], sem_o.at[s]).start()
    for s in range(orders):
        pltpu.make_async_copy(tt_v.at[s], tt.at[s], sem_o.at[s]).wait()


def arrange(trial):
    vectors, orders, _, degrees = trial.shape
    hbm = pl.BlockSpec(memory_space=pltpu.HBM)
    return pl.pallas_call(
        arrange_kernel,
        out_shape=pltpu.HBM((orders, 4, vectors, degrees), BF16),
        in_specs=[hbm],
        out_specs=hbm,
        scratch_shapes=[
            pltpu.VMEM((orders, vectors, 4, degrees), BF16),
            pltpu.VMEM((orders, 4, vectors, degrees), BF16),
            pltpu.SemaphoreType.DMA((orders,)),
            pltpu.SemaphoreType.DMA((orders,)),
        ],
        compiler_params=pltpu.CompilerParams(vmem_limit_bytes=40 << 20),
        cost_estimate=pl.CostEstimate(
            flops=300_000_000, bytes_accessed=4 << 20, transcendentals=0
        ),
        name="arrange",
    )(in_hbm(trial))


def quarter_sine(x):
    y = x * x
    sine = 1.0 + y * (-1 / 6 + y * (1 / 120 + y * (-1 / 5040 + y * (1 / 362880 + y * (-1 / 39916800)))))
    cosine = 1.0 + y * (
        -1 / 2 + y * (1 / 24 + y * (-1 / 720 + y * (1 / 40320 + y * (-1 / 3628800 + y * (1 / 479001600)))))
    )
    return sine * x, cosine


def turn(phase, longitudes):
    quarter = longitudes // 4
    s, c = quarter_sine((phase & (quarter - 1)).astype(F32) * (2.0 * math.pi / longitudes))
    quadrant = phase // quarter
    swapped = (quadrant & 1) == 1
    sine = jnp.where(swapped, c, s)
    cosine = jnp.where(swapped, s, c)
    sine = jnp.where(quadrant >= 2, -sine, sine)
    cosine = jnp.where((quadrant == 1) | (quadrant == 2), -cosine, cosine)
    return sine, cosine


def transform_kernel(
    where, begins, counts, weights, slots, received, returned, cosine, sines
):
    orders, longitudes = cosine.shape
    lanes = slots.shape[1]
    columns = received.shape[1]
    part = columns // 4
    scale = 1.0 / math.sqrt(orders)
    near = lax.broadcasted_iota(jnp.int32, (lanes, lanes), 1)
    for g in range(slots.shape[0]):
        m = jnp.broadcast_to(slots[g : g + 1, :].astype(F32), (lanes, lanes)).T
        m = m.astype(jnp.int32)
        span = slice(g * lanes, (g + 1) * lanes)
        step_s, step_c = turn((m * lanes) & (longitudes - 1), longitudes)
        s, c = turn((m * near) & (longitudes - 1), longitudes)
        s, c = s * scale, c * scale
        for b in range(longitudes // lanes):
            cosine[span, b * lanes : (b + 1) * lanes] = c.astype(BF16)
            sines[span, b * lanes : (b + 1) * lanes] = s.astype(BF16)
            s, c = s * step_c + c * step_s, c * step_c - s * step_s

    home = (lax.axis_index("ma_0") * 8 + lax.axis_index("ma_1")) * 2 + lax.axis_index("ma_2")
    r = where[0] + where[1] + home
    j = lax.broadcasted_iota(jnp.int32, (1, longitudes), 1)
    inside = ((j - begins[r]) & (longitudes - 1)) < counts[r]
    factor = jnp.where(inside, weights[r], 0.0)

    ft = received[...].astype(F32).T.astype(BF16)
    with_cos = jnp.concatenate([ft[:part], ft[3 * part :]], axis=0)
    with_sin = ft[part : 3 * part]
    grid = dot(with_cos, cosine[...]) + dot(with_sin, sines[...])
    weighted = (grid * factor).astype(BF16)
    colat, azimuth = weighted[:part], weighted[part:]
    none = jnp.zeros_like(colat)
    back = dot(
        cosine[...], jnp.concatenate([colat, none, none, azimuth], axis=0), NT
    ) + dot(sines[...], jnp.concatenate([none, colat, azimuth, none], axis=0), NT)
    returned[...] = back.astype(BF16)


def cycle_transform(where, begins, counts, weights, slots, received):
    vmem = pl.BlockSpec(memory_space=pltpu.VMEM)
    smem = pl.BlockSpec(memory_space=pltpu.SMEM)
    orders = slots.size
    return pl.pallas_call(
        transform_kernel,
        out_shape=jax.ShapeDtypeStruct(received.shape, BF16),
        in_specs=[smem] * 4 + [vmem] * 2,
        out_specs=vmem,
        scratch_shapes=[pltpu.VMEM((orders, 2 * orders), BF16)] * 2,
        compiler_params=pltpu.CompilerParams(vmem_limit_bytes=40 << 20),
        cost_estimate=pl.CostEstimate(
            flops=600_000_000, bytes_accessed=3 << 20, transcendentals=0
        ),
        name="transform",
    )(where, begins, counts, weights, slots, received)


def trial_gram_kernel(
    trial, block1, block2, block3, own, home1, home2, home3, mine, sem
):
    n, _, _, degrees = trial.shape
    me = lax.axis_index("vert")
    copies = [
        pltpu.make_async_copy(trial.at[:, 2 * me + i], mine.at[i], sem.at[i]) for i in range(2)
    ]
    for copy in copies:
        copy.start()
    order = by_part(n)
    total = 0.0
    for i in range(2):
        copies[i].wait()
        parts = [
            dot(order, b.reshape(4 * n, degrees)).astype(BF16)
            for b in (mine[i], block1[i], block2[i], block3[i])
        ]
        for c in range(4):
            x = jnp.concatenate([p[c * n : (c + 1) * n] for p in parts], axis=0)
            total = total + dot(x, x, NT)
    for d, out in enumerate((own, home1, home2, home3)):
        rows = total[d * n : (d + 1) * n]
        out[...] = jnp.concatenate(
            [rows[:, (d - e) % 4 * n : ((d - e) % 4 + 1) * n] for e in range(4)], axis=1
        )


def trial_gram(trial, received):
    vectors, _, parts, degrees = trial.shape
    vmem = pl.BlockSpec(memory_space=pltpu.VMEM)
    return pl.pallas_call(
        trial_gram_kernel,
        out_shape=[jax.ShapeDtypeStruct((vectors, 4 * vectors), F32)] * 4,
        in_specs=[pl.BlockSpec(memory_space=pltpu.HBM)] + [vmem] * 3,
        scratch_shapes=[
            pltpu.VMEM((2, vectors, parts, degrees), BF16),
            pltpu.SemaphoreType.DMA((2,)),
        ],
        compiler_params=pltpu.CompilerParams(vmem_limit_bytes=32 << 20),
        cost_estimate=pl.CostEstimate(
            flops=600_000_000, bytes_accessed=2 << 20, transcendentals=0
        ),
        name="trial_gram",
    )(in_hbm(trial), *received)


def analyse_kernel(
    where, got0, got1, got2, got3, rows0, rows1, rows2, rows3, legendre,
    tt, applied, gram,
    got_v, rows_v, wide, adj, leg_v, tt_v, sem_g, sem_r, sem_l, sem_t,
):
    orders, _, vectors, _ = tt.shape
    columns = 4 * vectors
    start = pl.multiple_of(where[0], 16)
    shift = where[1]

    def trial_copy(n):
        return pltpu.make_async_copy(tt.at[n], tt_v.at[n], sem_t.at[n])

    got_copies = [
        pltpu.make_async_copy(got, got_v.at[e], sem_g.at[e])
        for e, got in enumerate((got0, got1, got2, got3))
    ]
    row_copies = [
        pltpu.make_async_copy(rows, rows_v.at[e], sem_r.at[e])
        for e, rows in enumerate((rows0, rows1, rows2, rows3))
    ]
    for copy in got_copies:
        copy.start()
    for n in range(orders):
        window_copy(legendre, leg_v, sem_l, n, n, start).start()
        trial_copy(n).start()
    for copy in row_copies:
        copy.start()
    for e, copy in enumerate(got_copies):
        copy.wait()
        wide[e] = got_v[e].astype(F32)
    adj[...] = jnp.zeros_like(adj)
    lane = lax.broadcasted_iota(jnp.int32, (1, columns), 1) // vectors
    one = jnp.ones((1, columns), F32)
    sign0 = jnp.where(lane < 2, one, -one)
    sign1 = jnp.where((lane == 0) | (lane == 3), -one, one)
    cycles = got0.shape[0] // orders
    block = {0: 0, 1: 1, 3: 2, 2: 3}
    total = 0.0
    for n in range(orders):
        for e in range(4):
            x = wide[e, pl.ds(n, cycles, stride=orders), :]
            base = e * 2 * WINDOW + shift
            adj[pl.ds(base, cycles), :] = x * sign0
            adj[pl.ds(base + WINDOW, cycles), :] = pltpu.roll(x, columns // 2, 1) * sign1
        a = jnp.concatenate(
            [adj[e * 2 * WINDOW : (e + 1) * 2 * WINDOW].T for e in range(4)], axis=0
        ).astype(BF16)
        window_copy(legendre, leg_v, sem_l, n, n, start).wait()
        rows = dot(a, leg_v[n].reshape(2 * WINDOW, leg_v.shape[3])).astype(BF16)
        trial_copy(n).wait()
        for c in range(4):
            b = block[c] * vectors
            own = [rows[e * columns + b : e * columns + b + vectors] for e in range(4)]
            every = jnp.concatenate(own, axis=0)
            applied[n, c] = every
            total = total + dot(every, jnp.concatenate([tt_v[n, c], own[0]], axis=0), NT)
    for copy in row_copies:
        copy.wait()
    gram[:vectors] = (rows_v[0] + rows_v[1]) + (rows_v[2] + rows_v[3])
    gram[vectors:] = total.T


def analyse(where, gots, trial_rows, legendre, tt):
    orders, _, vectors, degrees = tt.shape
    cycles_rows, columns = gots[0].shape
    vmem = pl.BlockSpec(memory_space=pltpu.VMEM)
    hbm = pl.BlockSpec(memory_space=pltpu.HBM)
    return pl.pallas_call(
        analyse_kernel,
        out_shape=(
            jax.ShapeDtypeStruct((orders, 4, 4 * vectors, degrees), BF16),
            jax.ShapeDtypeStruct((3 * vectors, 4 * vectors), F32),
        ),
        in_specs=[pl.BlockSpec(memory_space=pltpu.SMEM)] + [hbm] * 10,
        out_specs=(vmem, vmem),
        scratch_shapes=[
            pltpu.VMEM((4, cycles_rows, columns), BF16),
            pltpu.VMEM((4, vectors, columns), F32),
            pltpu.VMEM((4, cycles_rows, columns), F32),
            pltpu.VMEM((4 * 2 * WINDOW, columns), F32),
            pltpu.VMEM((orders, 2, WINDOW, degrees), BF16),
            pltpu.VMEM((orders, 4, vectors, degrees), BF16),
            pltpu.SemaphoreType.DMA((4,)),
            pltpu.SemaphoreType.DMA((4,)),
            pltpu.SemaphoreType.DMA((orders,)),
            pltpu.SemaphoreType.DMA((orders,)),
        ],
        compiler_params=pltpu.CompilerParams(vmem_limit_bytes=40 << 20),
        cost_estimate=pl.CostEstimate(
            flops=2_000_000_000, bytes_accessed=14 << 20, transcendentals=0
        ),
        name="analyse",
    )(where, *gots, *trial_rows, in_hbm(legendre), in_hbm(tt))


def eliminate(work, n):
    shape = (PANEL, n)
    sub = lax.broadcasted_iota(jnp.int32, shape, 0)
    for j in range(0, n, PANEL):
        for which in range(work.shape[0]):
            top = work[which, j : j + PANEL, :n]
            value, low, inverse = {}, {}, []
            for m in range(PANEL):
                column = jnp.broadcast_to(top[:, j + m : j + m + 1], shape)
                for i in range(m, PANEL):
                    value[i, m] = jnp.broadcast_to(column[i : i + 1], shape)
            for m in range(PANEL):
                inverse.append(lax.rsqrt(value[m, m]))
                for i in range(m + 1, PANEL):
                    low[i, m] = value[i, m] * inverse[m]
                for i in range(m + 1, PANEL):
                    for k in range(m + 1, i + 1):
                        value[i, k] = value[i, k] - low[i, m] * low[k, m]

            def solved(base):
                rows = []
                for m in range(PANEL):
                    line = jnp.broadcast_to(
                        work[which, j + m : j + m + 1, base : base + n], shape
                    )
                    for k in range(m):
                        line = line - low[m, k] * rows[k]
                    rows.append(line * inverse[m])
                return rows

            left = solved(0) if j + PANEL < n else None
            right = solved(n)
            panel = right[0]
            for m in range(1, PANEL):
                panel = jnp.where(sub == m, right[m], panel)
            work[which, j : j + PANEL, n:] = panel
            for i in range(j + PANEL, n, PANEL):
                block = work[which, i : i + PANEL, :n]
                tail = work[which, i : i + PANEL, n:]
                factor = []
                for m in range(PANEL):
                    column = jnp.broadcast_to(block[:, j + m : j + m + 1], shape)
                    for k in range(m):
                        column = column - low[m, k] * factor[k]
                    factor.append(column * inverse[m])
                for m in range(PANEL):
                    block = block - factor[m] * left[m]
                    tail = tail - factor[m] * right[m]
                work[which, i : i + PANEL, :n] = block
                work[which, i : i + PANEL, n:] = tail


def factors_kernel(
    grams, weights, ritz, gram_v, work, cross, sem
):
    n = cross.shape[0]
    vectors = n // 4
    copies = [
        pltpu.make_async_copy(grams.at[group], gram_v.at[group], sem.at[group])
        for group in range(grams.shape[0])
    ]
    for copy in copies:
        copy.start()
    me = lax.axis_index("vert")
    unit = (
        lax.broadcasted_iota(jnp.int32, (n, n), 0)
        == lax.broadcasted_iota(jnp.int32, (n, n), 1)
    ).astype(F32)
    work[0, :, n:] = unit
    work[1, :, n:] = unit
    for group, copy in enumerate(copies):
        copy.wait()
        rows = gram_v[group] * (1.0 / COEFFICIENTS)
        if group:
            rows = pltpu.roll(rows, group * vectors, 1)
        span = pl.ds(group * vectors, vectors)
        work[0, span, :n] = rows[:vectors]
        cross[span, :] = rows[vectors : 2 * vectors]
        work[1, span, :n] = rows[2 * vectors :]
    eliminate(work, n)
    inverse_trial = work[0, :, n:]
    ritz[...] = dot_high(dot_high(inverse_trial, cross[...]), inverse_trial, NT)
    mine = work[1, pl.ds(pl.multiple_of(me * vectors, vectors), vectors), n:]
    mine = pltpu.roll(mine, ((4 - me) & 3) * vectors, 1).astype(BF16)
    i = lax.broadcasted_iota(jnp.int32, (n, vectors), 0)
    repeat = (i // 4 == lax.broadcasted_iota(jnp.int32, (n, vectors), 1)).astype(BF16)
    mine = dot(repeat, mine)
    part = lax.broadcasted_iota(jnp.int32, (n, n), 0) & 3
    weights[...] = jnp.concatenate(
        [jnp.where(part == c, mine, 0.0) for c in range(4)], axis=1
    ).astype(BF16)


def factors(grams):
    _, rows, n = grams.shape
    vmem = pl.BlockSpec(memory_space=pltpu.VMEM)
    return pl.pallas_call(
        factors_kernel,
        out_shape=(
            jax.ShapeDtypeStruct((n, 4 * n), BF16),
            jax.ShapeDtypeStruct((n, n), F32),
        ),
        in_specs=[pl.BlockSpec(memory_space=pltpu.HBM)],
        out_specs=(vmem, vmem),
        scratch_shapes=[
            pltpu.VMEM((4, rows, n), F32),
            pltpu.VMEM((2, n, 2 * n), F32),
            pltpu.VMEM((n, n), F32),
            pltpu.SemaphoreType.DMA((4,)),
        ],
        compiler_params=pltpu.CompilerParams(vmem_limit_bytes=16 << 20),
        cost_estimate=pl.CostEstimate(
            flops=100_000_000, bytes_accessed=1 << 20, transcendentals=0
        ),
        name="factors",
    )(grams)


def mix_kernel(weights, applied, new_basis, out_v, sem):
    orders, parts, n, degrees = applied.shape
    for s in range(orders):
        y = dot(weights[...], applied[s].reshape(parts * n, degrees)).astype(BF16)
        out_v[s] = y.reshape(n // 4, 4, degrees)
        pltpu.make_async_copy(out_v.at[s], new_basis.at[:, s], sem.at[s]).start()
    for s in range(orders):
        pltpu.make_async_copy(out_v.at[s], new_basis.at[:, s], sem.at[s]).wait()


def mix(weights, applied):
    orders, _, n, degrees = applied.shape
    vmem = pl.BlockSpec(memory_space=pltpu.VMEM)
    return pl.pallas_call(
        mix_kernel,
        out_shape=pltpu.HBM((n // 4, orders, 4, degrees), BF16),
        in_specs=[vmem, vmem],
        out_specs=pl.BlockSpec(memory_space=pltpu.HBM),
        scratch_shapes=[
            pltpu.VMEM((orders, n // 4, 4, degrees), BF16),
            pltpu.SemaphoreType.DMA((orders,)),
        ],
        compiler_params=pltpu.CompilerParams(vmem_limit_bytes=32 << 20),
        cost_estimate=pl.CostEstimate(
            flops=1_100_000_000, bytes_accessed=10 << 20, transcendentals=0
        ),
        name="mix",
    )(weights, applied)


def swap(value, axis, size, bit):
    return lax.ppermute(value, axis, [(i, i ^ bit) for i in range(size)])


def sum_of_four(value, axis, size):
    one, two, three = (swap(value, axis, size, bit) for bit in (1, 2, 3))
    return (value + one) + (two + three)


def sum_over_ma(value):
    value = value + swap(value, "ma_2", 2, 1)
    value = sum_of_four(value, "ma_1", 8)
    value = value + swap(value, "ma_1", 8, 4)
    return sum_of_four(value, "ma_0", 4)


def from_groups(value):
    return [value] + [lax.ppermute(value, "vert", ring(4, -d)) for d in (1, 2, 3)]


def shards(trial_block, legendre, order_slot, cycle_start, cycle_count, cycle_weight):
    vectors, orders, _, _ = trial_block.shape
    live = legendre.shape[2] // 4
    columns = 4 * vectors

    fields, *sent, where = synthesize(
        cycle_count.reshape(-1, 128), trial_block, legendre, live
    )
    blocks = [lax.ppermute(x, "vert", ring(4, d)) for d, x in enumerate(sent, 1)]
    received = lax.all_to_all(fields, MA, split_axis=0, concat_axis=0, tiled=True)
    tt = arrange(trial_block)
    received, tt = lax.optimization_barrier((received, tt))
    returned = cycle_transform(
        where, cycle_start, cycle_count, cycle_weight, order_slot.reshape(-1, 128),
        received.reshape(live * orders, columns),
    )
    order_fields = lax.all_to_all(
        returned.reshape(live, orders, columns), MA, split_axis=0, concat_axis=0, tiled=True
    )
    shares = trial_gram(trial_block, blocks)
    trial_rows = [shares[0]] + [
        lax.ppermute(shares[d], "vert", ring(4, -d)) for d in (1, 2, 3)
    ]
    order_fields, *trial_rows = lax.optimization_barrier((order_fields, *trial_rows))
    gots = from_groups(order_fields.reshape(live * orders, columns))
    applied, gram = analyse(where, gots, trial_rows, legendre, tt)
    summed = jnp.broadcast_to(sum_over_ma(gram)[None], (4, *gram.shape))
    grams = lax.all_to_all(summed, "vert", split_axis=0, concat_axis=0, tiled=True)
    weights, ritz_matrix = factors(grams)
    return (mix(weights, applied), ritz_matrix)


def solution(mesh):
    split = Mesh(
        mesh.devices.reshape(4, 8, 2, mesh.shape["vert"]), ("ma_0", "ma_1", "ma_2", "vert")
    )
    placed = (P("vert", MA, None, None), P(MA, None, None, None), P(), P(), P(), P())
    return jax.shard_map(
        shards,
        mesh=split,
        in_specs=placed,
        out_specs=(P("vert", MA, None, None), P()),
        check_vma=False,
    )
```

```python
import math

import jax
import jax.numpy as jnp
from jax import lax
from jax.experimental import pallas as pl
from jax.experimental.pallas import tpu as pltpu
from jax.sharding import Mesh
from jax.sharding import PartitionSpec as P

MA = ("ma_0", "ma_1", "ma_2")
F32 = jnp.float32
BF16 = jnp.bfloat16
WINDOW = 80
PANEL = 8
COEFFICIENTS = 512 * 4 * 1024
NT = (((1,), (1,)), ((), ()))
NN = (((1,), (0,)), ((), ()))


def ring(size, shift):
    return [(i, (i + shift) % size) for i in range(size)]


def dot(a, b, dims=NN):
    return lax.dot_general(a, b, dims, preferred_element_type=F32)


def in_hbm(value):
    return pltpu.with_memory_space_constraint(value, pltpu.HBM)


def dot_high(a, b, dims=NN):
    return lax.dot_general(
        a, b, dims, precision=lax.Precision.HIGHEST, preferred_element_type=F32
    )


def window_copy(legendre, leg_v, sem, s, slot, start):
    return pltpu.make_async_copy(
        legendre.at[s, :, pl.ds(start, WINDOW), :], leg_v.at[slot], sem.at[slot]
    )


def by_part(vectors):
    shape = (4 * vectors, 4 * vectors)
    i = lax.broadcasted_iota(jnp.int32, shape, 0)
    j = lax.broadcasted_iota(jnp.int32, shape, 1)
    return (j == (i % vectors) * 4 + i // vectors).astype(BF16)


def synthesize_kernel(
    counts, trial, legendre, fields, sent1, sent2, sent3, where,
    tr_v, leg_v, one, two, prod, sem_t, sem_l, sem_o,
):
    vectors, orders = trial.shape[:2]
    me = lax.axis_index("vert")
    pair = orders // 4

    def send_copies():
        for d, out in enumerate((sent1, sent2, sent3)):
            yield pltpu.make_async_copy(
                tr_v.at[pl.ds((me + d + 1) % 4 * pair, pair)], out, sem_o.at[d]
            )

    for s in range(orders):
        pltpu.make_async_copy(trial.at[:, s], tr_v.at[s], sem_t.at[s]).start()
    live = counts[...] > 0
    cycle = lax.broadcasted_iota(jnp.int32, live.shape, 0) * live.shape[1]
    cycle = cycle + lax.broadcasted_iota(jnp.int32, live.shape, 1)
    last = legendre.shape[2] - fields.shape[0]
    first = jnp.min(jnp.where(live, cycle, last).astype(F32)).astype(jnp.int32)
    start = jnp.minimum((first // 16) * 16, legendre.shape[2] - WINDOW)
    start = pl.multiple_of(start, 16)
    shift = first - start
    where[0] = start
    where[1] = shift
    for s in range(orders):
        window_copy(legendre, leg_v, sem_l, s, s, start).start()
    for s in range(orders):
        pltpu.make_async_copy(trial.at[:, s], tr_v.at[s], sem_t.at[s]).wait()
        x = tr_v[s].reshape(4 * vectors, tr_v.shape[3])
        window_copy(legendre, leg_v, sem_l, s, s, start).wait()
        slot = s % 2
        one[slot, :, :WINDOW] = dot(x, leg_v[s, 0], NT)
        two[slot, :, :WINDOW] = dot(x, leg_v[s, 1], NT)
        w, x = (
            [ref[slot, pl.ds(c, vectors, stride=4), :] for c in range(4)]
            for ref in (one, two)
        )
        f = jnp.concatenate([w[0] + x[3], w[1] - x[2], -x[0] - w[3], x[1] - w[2]], axis=0)
        prod[s * WINDOW : (s + 1) * WINDOW] = f.T[:WINDOW]
        if s == orders - 1:
            for copy in send_copies():
                copy.start()
    for r in range(fields.shape[0]):
        fields[r] = prod[pl.ds(shift + r, orders, stride=WINDOW), :].astype(BF16)
    for copy in send_copies():
        copy.wait()


def synthesize(counts, trial, legendre, cycles):
    vectors, orders, _, degrees = trial.shape
    columns = 4 * vectors
    hbm = pl.BlockSpec(memory_space=pltpu.HBM)
    vmem = pl.BlockSpec(memory_space=pltpu.VMEM)
    sent = pltpu.HBM((orders // 4, vectors, 4, degrees), BF16)
    return pl.pallas_call(
        synthesize_kernel,
        out_shape=(
            jax.ShapeDtypeStruct((cycles, orders, columns), BF16),
            sent,
            sent,
            sent,
            jax.ShapeDtypeStruct((2,), jnp.int32),
        ),
        in_specs=[vmem, hbm, hbm],
        out_specs=(vmem, hbm, hbm, hbm, pl.BlockSpec(memory_space=pltpu.SMEM)),
        scratch_shapes=[
            pltpu.VMEM((orders, vectors, 4, degrees), BF16),
            pltpu.VMEM((orders, 2, WINDOW, degrees), BF16),
            pltpu.VMEM((2, columns, 128), F32),
            pltpu.VMEM((2, columns, 128), F32),
            pltpu.VMEM((orders * WINDOW, columns), F32),
            pltpu.SemaphoreType.DMA((orders,)),
            pltpu.SemaphoreType.DMA((orders,)),
            pltpu.SemaphoreType.DMA((3,)),
        ],
        compiler_params=pltpu.CompilerParams(vmem_limit_bytes=40 << 20),
        cost_estimate=pl.CostEstimate(
            flops=600_000_000, bytes_accessed=5 << 20, transcendentals=0
        ),
        name="synthesize",
    )(counts, in_hbm(trial), in_hbm(legendre))


def arrange_kernel(trial, tt, tr_v, tt_v, sem_t, sem_o):
    vectors, orders = trial.shape[:2]
    for s in range(orders):
        pltpu.make_async_copy(trial.at[:, s], tr_v.at[s], sem_t.at[s]).start()
    order = by_part(vectors)
    for s in range(orders):
        pltpu.make_async_copy(trial.at[:, s], tr_v.at[s], sem_t.at[s]).wait()
        t = dot(order, tr_v[s].reshape(4 * vectors, tr_v.shape[3])).astype(BF16)
        for c in range(4):
            tt_v[s, c] = t[c * vectors : (c + 1) * vectors]
        pltpu.make_async_copy(tt_v.at[s], tt.at[s], sem_o.at[s]).start()
    for s in range(orders):
        pltpu.make_async_copy(tt_v.at[s], tt.at[s], sem_o.at[s]).wait()


def arrange(trial):
    vectors, orders, _, degrees = trial.shape
    hbm = pl.BlockSpec(memory_space=pltpu.HBM)
    return pl.pallas_call(
        arrange_kernel,
        out_shape=pltpu.HBM((orders, 4, vectors, degrees), BF16),
        in_specs=[hbm],
        out_specs=hbm,
        scratch_shapes=[
            pltpu.VMEM((orders, vectors, 4, degrees), BF16),
            pltpu.VMEM((orders, 4, vectors, degrees), BF16),
            pltpu.SemaphoreType.DMA((orders,)),
            pltpu.SemaphoreType.DMA((orders,)),
        ],
        compiler_params=pltpu.CompilerParams(vmem_limit_bytes=40 << 20),
        cost_estimate=pl.CostEstimate(
            flops=300_000_000, bytes_accessed=4 << 20, transcendentals=0
        ),
        name="arrange",
    )(in_hbm(trial))


def quarter_sine(x):
    y = x * x
    sine = 1.0 + y * (-1 / 6 + y * (1 / 120 + y * (-1 / 5040 + y * (1 / 362880 + y * (-1 / 39916800)))))
    cosine = 1.0 + y * (
        -1 / 2 + y * (1 / 24 + y * (-1 / 720 + y * (1 / 40320 + y * (-1 / 3628800 + y * (1 / 479001600)))))
    )
    return sine * x, cosine


def turn(phase, longitudes):
    quarter = longitudes // 4
    s, c = quarter_sine((phase & (quarter - 1)).astype(F32) * (2.0 * math.pi / longitudes))
    quadrant = phase // quarter
    swapped = (quadrant & 1) == 1
    sine = jnp.where(swapped, c, s)
    cosine = jnp.where(swapped, s, c)
    sine = jnp.where(quadrant >= 2, -sine, sine)
    cosine = jnp.where((quadrant == 1) | (quadrant == 2), -cosine, cosine)
    return sine, cosine


def tables_kernel(slots, cosine, sines):
    orders, longitudes = cosine.shape
    lanes = slots.shape[1]
    scale = 1.0 / math.sqrt(orders)
    near = lax.broadcasted_iota(jnp.int32, (lanes, lanes), 1)
    for g in range(slots.shape[0]):
        m = jnp.broadcast_to(slots[g : g + 1, :].astype(F32), (lanes, lanes)).T
        m = m.astype(jnp.int32)
        span = slice(g * lanes, (g + 1) * lanes)
        step_s, step_c = turn((m * lanes) & (longitudes - 1), longitudes)
        s, c = turn((m * near) & (longitudes - 1), longitudes)
        s, c = s * scale, c * scale
        for b in range(longitudes // lanes):
            cosine[span, b * lanes : (b + 1) * lanes] = c.astype(BF16)
            sines[span, b * lanes : (b + 1) * lanes] = s.astype(BF16)
            s, c = s * step_c + c * step_s, c * step_c - s * step_s


def fourier_tables(slots):
    table = jax.ShapeDtypeStruct((slots.size, 2 * slots.size), BF16)
    return pl.pallas_call(
        tables_kernel,
        out_shape=(table, table),
        compiler_params=pltpu.CompilerParams(vmem_limit_bytes=16 << 20),
        cost_estimate=pl.CostEstimate(
            flops=10_000_000, bytes_accessed=2 << 20, transcendentals=0
        ),
        name="tables",
    )(slots)


def transform_kernel(where, begins, counts, weights, cosine, sines, received, returned):
    longitudes = cosine.shape[1]
    columns = received.shape[1]
    part = columns // 4
    home = (lax.axis_index("ma_0") * 8 + lax.axis_index("ma_1")) * 2 + lax.axis_index("ma_2")
    r = where[0] + where[1] + home
    j = lax.broadcasted_iota(jnp.int32, (1, longitudes), 1)
    inside = ((j - begins[r]) & (longitudes - 1)) < counts[r]
    factor = jnp.where(inside, weights[r], 0.0)

    ft = received[...].astype(F32).T.astype(BF16)
    with_cos = jnp.concatenate([ft[:part], ft[3 * part :]], axis=0)
    with_sin = ft[part : 3 * part]
    grid = dot(with_cos, cosine[...]) + dot(with_sin, sines[...])
    weighted = (grid * factor).astype(BF16)
    colat, azimuth = weighted[:part], weighted[part:]
    none = jnp.zeros_like(colat)
    back = dot(
        cosine[...], jnp.concatenate([colat, none, none, azimuth], axis=0), NT
    ) + dot(sines[...], jnp.concatenate([none, colat, azimuth, none], axis=0), NT)
    returned[...] = back.astype(BF16)


def cycle_transform(where, begins, counts, weights, cosine, sines, received):
    vmem = pl.BlockSpec(memory_space=pltpu.VMEM)
    smem = pl.BlockSpec(memory_space=pltpu.SMEM)
    return pl.pallas_call(
        transform_kernel,
        out_shape=jax.ShapeDtypeStruct(received.shape, BF16),
        in_specs=[smem] * 4 + [vmem] * 3,
        out_specs=vmem,
        compiler_params=pltpu.CompilerParams(vmem_limit_bytes=40 << 20),
        cost_estimate=pl.CostEstimate(
            flops=600_000_000, bytes_accessed=3 << 20, transcendentals=0
        ),
        name="transform",
    )(where, begins, counts, weights, cosine, sines, received)


def trial_gram_kernel(
    trial, block1, block2, block3, own, home1, home2, home3, mine, sem
):
    n, _, _, degrees = trial.shape
    me = lax.axis_index("vert")
    copies = [
        pltpu.make_async_copy(trial.at[:, 2 * me + i], mine.at[i], sem.at[i]) for i in range(2)
    ]
    for copy in copies:
        copy.start()
    order = by_part(n)
    total = 0.0
    for i in range(2):
        copies[i].wait()
        parts = [
            dot(order, b.reshape(4 * n, degrees)).astype(BF16)
            for b in (mine[i], block1[i], block2[i], block3[i])
        ]
        for c in range(4):
            x = jnp.concatenate([p[c * n : (c + 1) * n] for p in parts], axis=0)
            total = total + dot(x, x, NT)
    for d, out in enumerate((own, home1, home2, home3)):
        rows = total[d * n : (d + 1) * n]
        out[...] = jnp.concatenate(
            [rows[:, (d - e) % 4 * n : ((d - e) % 4 + 1) * n] for e in range(4)], axis=1
        )


def trial_gram(trial, received):
    vectors, _, parts, degrees = trial.shape
    vmem = pl.BlockSpec(memory_space=pltpu.VMEM)
    return pl.pallas_call(
        trial_gram_kernel,
        out_shape=[jax.ShapeDtypeStruct((vectors, 4 * vectors), F32)] * 4,
        in_specs=[pl.BlockSpec(memory_space=pltpu.HBM)] + [vmem] * 3,
        scratch_shapes=[
            pltpu.VMEM((2, vectors, parts, degrees), BF16),
            pltpu.SemaphoreType.DMA((2,)),
        ],
        compiler_params=pltpu.CompilerParams(vmem_limit_bytes=32 << 20),
        cost_estimate=pl.CostEstimate(
            flops=600_000_000, bytes_accessed=2 << 20, transcendentals=0
        ),
        name="trial_gram",
    )(in_hbm(trial), *received)


def placed_pair(adj, x, base, shift, sign0, sign1):
    cycles, columns = x.shape
    adj[pl.ds(base + shift, cycles), :] = x * sign0
    adj[pl.ds(base + WINDOW + shift, cycles), :] = pltpu.roll(x, columns // 2, 1) * sign1


def adjoint_signs(columns, vectors):
    lane = lax.broadcasted_iota(jnp.int32, (1, columns), 1) // vectors
    one = jnp.ones((1, columns), F32)
    return jnp.where(lane < 2, one, -one), jnp.where((lane == 0) | (lane == 3), -one, one)


ROWS_OF = {0: 0, 1: 1, 3: 2, 2: 3}


def analyse_own_kernel(
    where, got, legendre, tt, own, gram, leg_v, tt_v, wide, adj, sem_l, sem_t
):
    orders, _, vectors, degrees = tt.shape
    columns = 4 * vectors
    start = pl.multiple_of(where[0], 16)
    shift = where[1]
    for n in range(orders):
        window_copy(legendre, leg_v, sem_l, n, n, start).start()
        pltpu.make_async_copy(tt.at[n], tt_v.at[n], sem_t.at[n]).start()
    wide[...] = got[...].astype(F32)
    adj[...] = jnp.zeros_like(adj)
    sign0, sign1 = adjoint_signs(columns, vectors)
    cycles = got.shape[0] // orders
    total = 0.0
    for n in range(orders):
        x = wide[pl.ds(n, cycles, stride=orders), :]
        base = n % 2 * 2 * WINDOW
        placed_pair(adj, x, base, shift, sign0, sign1)
        a = adj[base : base + 2 * WINDOW].T.astype(BF16)
        window_copy(legendre, leg_v, sem_l, n, n, start).wait()
        rows = dot(a, leg_v[n].reshape(2 * WINDOW, degrees)).astype(BF16)
        pltpu.make_async_copy(tt.at[n], tt_v.at[n], sem_t.at[n]).wait()
        for c in range(4):
            mine = rows[ROWS_OF[c] * vectors : (ROWS_OF[c] + 1) * vectors]
            own[n, c] = mine
            total = total + dot(mine, jnp.concatenate([tt_v[n, c], mine], axis=0), NT)
    gram[...] = total


def analyse_own(where, got, legendre, tt):
    orders, _, vectors, degrees = tt.shape
    rows, columns = got.shape
    vmem = pl.BlockSpec(memory_space=pltpu.VMEM)
    hbm = pl.BlockSpec(memory_space=pltpu.HBM)
    block = jax.ShapeDtypeStruct(tt.shape, BF16)
    return pl.pallas_call(
        analyse_own_kernel,
        out_shape=(
            block,
            jax.ShapeDtypeStruct((vectors, 2 * vectors), F32),
            jax.ShapeDtypeStruct((orders, 2, WINDOW, degrees), BF16),
            block,
        ),
        in_specs=[pl.BlockSpec(memory_space=pltpu.SMEM), vmem, hbm, hbm],
        out_specs=(vmem,) * 4,
        scratch_shapes=[
            pltpu.VMEM((rows, columns), F32),
            pltpu.VMEM((2 * 2 * WINDOW, columns), F32),
            pltpu.SemaphoreType.DMA((orders,)),
            pltpu.SemaphoreType.DMA((orders,)),
        ],
        compiler_params=pltpu.CompilerParams(vmem_limit_bytes=24 << 20),
        cost_estimate=pl.CostEstimate(
            flops=500_000_000, bytes_accessed=5 << 20, transcendentals=0
        ),
        name="analyse_own",
    )(where, got, in_hbm(legendre), in_hbm(tt))


def analyse_kernel(
    where, got1, got2, got3, rows0, rows1, rows2, rows3, own, own_gram, leg_v, tt_v,
    rest, kept, sent, gram, got_v, rows_v, wide, adj, sem_g, sem_r,
):
    orders, _, vectors, degrees = own.shape
    columns = 4 * vectors
    shift = where[1]
    got_copies = [
        pltpu.make_async_copy(got, got_v.at[e], sem_g.at[e])
        for e, got in enumerate((got1, got2, got3))
    ]
    row_copies = [
        pltpu.make_async_copy(rows, rows_v.at[e], sem_r.at[e])
        for e, rows in enumerate((rows0, rows1, rows2, rows3))
    ]
    for copy in got_copies + row_copies:
        copy.start()
    adj[...] = jnp.zeros_like(adj)
    for e, copy in enumerate(got_copies):
        copy.wait()
        wide[e] = got_v[e].astype(F32)
    sign0, sign1 = adjoint_signs(columns, vectors)
    cycles = got1.shape[0] // orders
    total = 0.0
    for n in range(orders):
        for e in range(3):
            x = wide[e, pl.ds(n, cycles, stride=orders), :]
            placed_pair(adj, x, e * 2 * WINDOW, shift, sign0, sign1)
        a = jnp.concatenate(
            [adj[e * 2 * WINDOW : (e + 1) * 2 * WINDOW].T for e in range(3)], axis=0
        ).astype(BF16)
        rows = dot(a, leg_v[n].reshape(2 * WINDOW, degrees)).astype(BF16)
        for c in range(4):
            b = ROWS_OF[c] * vectors
            others = jnp.concatenate(
                [rows[e * columns + b : e * columns + b + vectors] for e in range(3)], axis=0
            )
            rest[n, c] = others
            total = total + dot(
                others, jnp.concatenate([tt_v[n, c], own[n, c]], axis=0), NT
            )
    for copy in row_copies:
        copy.wait()
    gram[:vectors] = (rows_v[0] + rows_v[1]) + (rows_v[2] + rows_v[3])
    gram[vectors:] = jnp.concatenate([own_gram[...], total], axis=0).T
    half = kept.shape[0]
    core = lax.axis_index("ma_2")
    kept[...] = gram[pl.ds(pl.multiple_of(core * half, half), half), :]
    sent[...] = gram[pl.ds(pl.multiple_of((1 - core) * half, half), half), :]


def analyse(where, gots, trial_rows, own, own_gram, leg_v, tt_v):
    orders, _, vectors, degrees = own.shape
    cycles_rows, columns = gots[0].shape
    vmem = pl.BlockSpec(memory_space=pltpu.VMEM)
    hbm = pl.BlockSpec(memory_space=pltpu.HBM)
    return pl.pallas_call(
        analyse_kernel,
        out_shape=(
            jax.ShapeDtypeStruct((orders, 4, 3 * vectors, degrees), BF16),
            *([jax.ShapeDtypeStruct((3 * vectors // 2, columns), F32)] * 2),
        ),
        in_specs=[pl.BlockSpec(memory_space=pltpu.SMEM)] + [hbm] * 7 + [vmem] * 4,
        out_specs=(vmem, vmem, vmem),
        scratch_shapes=[
            pltpu.VMEM((3 * vectors, columns), F32),
            pltpu.VMEM((3, cycles_rows, columns), BF16),
            pltpu.VMEM((4, vectors, columns), F32),
            pltpu.VMEM((3, cycles_rows, columns), F32),
            pltpu.VMEM((3 * 2 * WINDOW, columns), F32),
            pltpu.SemaphoreType.DMA((3,)),
            pltpu.SemaphoreType.DMA((4,)),
        ],
        compiler_params=pltpu.CompilerParams(vmem_limit_bytes=32 << 20),
        cost_estimate=pl.CostEstimate(
            flops=1_500_000_000, bytes_accessed=12 << 20, transcendentals=0
        ),
        name="analyse",
    )(where, *gots, *trial_rows, own, own_gram, leg_v, tt_v)


def eliminate(work, n):
    shape = (PANEL, n)
    sub = lax.broadcasted_iota(jnp.int32, shape, 0)
    for j in range(0, n, PANEL):
        for which in range(work.shape[0]):
            top = work[which, j : j + PANEL, :n]
            value, low, inverse = {}, {}, []
            for m in range(PANEL):
                column = jnp.broadcast_to(top[:, j + m : j + m + 1], shape)
                for i in range(m, PANEL):
                    value[i, m] = jnp.broadcast_to(column[i : i + 1], shape)
            for m in range(PANEL):
                inverse.append(lax.rsqrt(value[m, m]))
                for i in range(m + 1, PANEL):
                    low[i, m] = value[i, m] * inverse[m]
                for i in range(m + 1, PANEL):
                    for k in range(m + 1, i + 1):
                        value[i, k] = value[i, k] - low[i, m] * low[k, m]

            def solved(base):
                rows = []
                for m in range(PANEL):
                    line = jnp.broadcast_to(
                        work[which, j + m : j + m + 1, base : base + n], shape
                    )
                    for k in range(m):
                        line = line - low[m, k] * rows[k]
                    rows.append(line * inverse[m])
                return rows

            left = solved(0) if j + PANEL < n else None
            right = solved(n)
            panel = right[0]
            for m in range(1, PANEL):
                panel = jnp.where(sub == m, right[m], panel)
            work[which, j : j + PANEL, n:] = panel
            for i in range(j + PANEL, n, PANEL):
                block = work[which, i : i + PANEL, :n]
                tail = work[which, i : i + PANEL, n:]
                factor = []
                for m in range(PANEL):
                    column = jnp.broadcast_to(block[:, j + m : j + m + 1], shape)
                    for k in range(m):
                        column = column - low[m, k] * factor[k]
                    factor.append(column * inverse[m])
                for m in range(PANEL):
                    block = block - factor[m] * left[m]
                    tail = tail - factor[m] * right[m]
                work[which, i : i + PANEL, :n] = block
                work[which, i : i + PANEL, n:] = tail


def factors_kernel(
    grams, weights, ritz, gram_v, work, cross, sem
):
    n = cross.shape[0]
    vectors = n // 4
    copies = [
        pltpu.make_async_copy(grams.at[half, group], gram_v.at[half, group], sem.at[half, group])
        for group in range(4)
        for half in range(2)
    ]
    for copy in copies:
        copy.start()
    me = lax.axis_index("vert")
    unit = (
        lax.broadcasted_iota(jnp.int32, (n, n), 0)
        == lax.broadcasted_iota(jnp.int32, (n, n), 1)
    ).astype(F32)
    work[0, :, n:] = unit
    work[1, :, n:] = unit
    for group in range(4):
        copies[2 * group].wait()
        copies[2 * group + 1].wait()
        rows = jnp.concatenate([gram_v[0, group], gram_v[1, group]], axis=0)
        rows = rows * (1.0 / COEFFICIENTS)
        if group:
            rows = pltpu.roll(rows, group * vectors, 1)
        span = pl.ds(group * vectors, vectors)
        work[0, span, :n] = rows[:vectors]
        cross[span, :] = rows[vectors : 2 * vectors]
        work[1, span, :n] = rows[2 * vectors :]
    eliminate(work, n)
    inverse_trial = work[0, :, n:]
    ritz[...] = dot_high(dot_high(inverse_trial, cross[...]), inverse_trial, NT)
    mine = work[1, pl.ds(pl.multiple_of(me * vectors, vectors), vectors), n:]
    mine = pltpu.roll(mine, ((4 - me) & 3) * vectors, 1).astype(BF16)
    i = lax.broadcasted_iota(jnp.int32, (n, vectors), 0)
    repeat = (i // 4 == lax.broadcasted_iota(jnp.int32, (n, vectors), 1)).astype(BF16)
    mine = dot(repeat, mine)
    part = lax.broadcasted_iota(jnp.int32, (n, n), 0) & 3
    weights[...] = jnp.concatenate(
        [jnp.where(part == c, mine, 0.0) for c in range(4)], axis=1
    ).astype(BF16)


def factors(grams):
    _, _, rows, n = grams.shape
    vmem = pl.BlockSpec(memory_space=pltpu.VMEM)
    return pl.pallas_call(
        factors_kernel,
        out_shape=(
            jax.ShapeDtypeStruct((n, 4 * n), BF16),
            jax.ShapeDtypeStruct((n, n), F32),
        ),
        in_specs=[pl.BlockSpec(memory_space=pltpu.HBM)],
        out_specs=(vmem, vmem),
        scratch_shapes=[
            pltpu.VMEM((2, 4, rows, n), F32),
            pltpu.VMEM((2, n, 2 * n), F32),
            pltpu.VMEM((n, n), F32),
            pltpu.SemaphoreType.DMA((2, 4)),
        ],
        compiler_params=pltpu.CompilerParams(vmem_limit_bytes=16 << 20),
        cost_estimate=pl.CostEstimate(
            flops=100_000_000, bytes_accessed=1 << 20, transcendentals=0
        ),
        name="factors",
    )(grams)


def mix_kernel(weights, own, rest, new_basis, out_v, sem):
    orders, parts, vectors, degrees = own.shape
    for s in range(orders):
        every = [piece for c in range(parts) for piece in (own[s, c], rest[s, c])]
        y = dot(weights[...], jnp.concatenate(every, axis=0)).astype(BF16)
        out_v[s] = y.reshape(vectors, 4, degrees)
        pltpu.make_async_copy(out_v.at[s], new_basis.at[:, s], sem.at[s]).start()
    for s in range(orders):
        pltpu.make_async_copy(out_v.at[s], new_basis.at[:, s], sem.at[s]).wait()


def mix(weights, own, rest):
    orders, _, vectors, degrees = own.shape
    vmem = pl.BlockSpec(memory_space=pltpu.VMEM)
    return pl.pallas_call(
        mix_kernel,
        out_shape=pltpu.HBM((vectors, orders, 4, degrees), BF16),
        in_specs=[vmem, vmem, vmem],
        out_specs=pl.BlockSpec(memory_space=pltpu.HBM),
        scratch_shapes=[
            pltpu.VMEM((orders, vectors, 4, degrees), BF16),
            pltpu.SemaphoreType.DMA((orders,)),
        ],
        compiler_params=pltpu.CompilerParams(vmem_limit_bytes=32 << 20),
        cost_estimate=pl.CostEstimate(
            flops=1_100_000_000, bytes_accessed=10 << 20, transcendentals=0
        ),
        name="mix",
    )(weights, own, rest)


def swap(value, axis, size, bit):
    return lax.ppermute(value, axis, [(i, i ^ bit) for i in range(size)])


def sum_of_four(value, axis, size):
    one, two, three = (swap(value, axis, size, bit) for bit in (1, 2, 3))
    return (value + one) + (two + three)


def sum_over_ma(kept, sent):
    value = kept + swap(sent, "ma_2", 2, 1)
    value = sum_of_four(value, "ma_1", 8)
    value = value + swap(value, "ma_1", 8, 4)
    return sum_of_four(value, "ma_0", 4)


def from_groups(value):
    return [value] + [lax.ppermute(value, "vert", ring(4, -d)) for d in (1, 2, 3)]


def shards(trial_block, legendre, order_slot, cycle_start, cycle_count, cycle_weight):
    vectors, orders, _, _ = trial_block.shape
    live = legendre.shape[2] // 4
    columns = 4 * vectors

    fields, *sent, where = synthesize(
        cycle_count.reshape(-1, 128), trial_block, legendre, live
    )
    blocks = [lax.ppermute(x, "vert", ring(4, d)) for d, x in enumerate(sent, 1)]
    received = lax.all_to_all(fields, MA, split_axis=0, concat_axis=0, tiled=True)
    tt = arrange(trial_block)
    cosine, sines = fourier_tables(order_slot.reshape(-1, 128))
    received, tt, cosine, sines = lax.optimization_barrier((received, tt, cosine, sines))
    returned = cycle_transform(
        where, cycle_start, cycle_count, cycle_weight, cosine, sines,
        received.reshape(live * orders, columns),
    )
    order_fields = lax.all_to_all(
        returned.reshape(live, orders, columns), MA, split_axis=0, concat_axis=0, tiled=True
    )
    shares = trial_gram(trial_block, blocks)
    trial_rows = [shares[0]] + [
        lax.ppermute(shares[d], "vert", ring(4, -d)) for d in (1, 2, 3)
    ]
    order_fields, *trial_rows = lax.optimization_barrier((order_fields, *trial_rows))
    gots = from_groups(order_fields.reshape(live * orders, columns))
    own, *of_own = analyse_own(where, gots[0], legendre, tt)
    rest, kept, sent = analyse(where, gots[1:], trial_rows, own, *of_own)
    summed = jnp.broadcast_to(sum_over_ma(kept, sent)[None], (8, *kept.shape))
    grams = lax.all_to_all(summed, ("ma_2", "vert"), split_axis=0, concat_axis=0, tiled=True)
    weights, ritz_matrix = factors(grams.reshape(2, 4, *kept.shape))
    return (mix(weights, own, rest), ritz_matrix)


def solution(mesh):
    split = Mesh(
        mesh.devices.reshape(4, 8, 2, mesh.shape["vert"]), ("ma_0", "ma_1", "ma_2", "vert")
    )
    placed = (P("vert", MA, None, None), P(MA, None, None, None), P(), P(), P(), P())
    return jax.shard_map(
        shards,
        mesh=split,
        in_specs=placed,
        out_specs=(P("vert", MA, None, None), P()),
        check_vma=False,
    )
```

```python
import math

import jax
import jax.numpy as jnp
from jax import lax
from jax.experimental import pallas as pl
from jax.experimental.pallas import tpu as pltpu
from jax.sharding import Mesh
from jax.sharding import PartitionSpec as P

MA = ("ma_0", "ma_1", "ma_2")
F32 = jnp.float32
BF16 = jnp.bfloat16
WINDOW = 80
PANEL = 8
COEFFICIENTS = 512 * 4 * 1024
NT = (((1,), (1,)), ((), ()))
NN = (((1,), (0,)), ((), ()))


def ring(size, shift):
    return [(i, (i + shift) % size) for i in range(size)]


def dot(a, b, dims=NN):
    return lax.dot_general(a, b, dims, preferred_element_type=F32)


def in_hbm(value):
    return pltpu.with_memory_space_constraint(value, pltpu.HBM)


def dot_high(a, b, dims=NN):
    return lax.dot_general(
        a, b, dims, precision=lax.Precision.HIGHEST, preferred_element_type=F32
    )


def window_copy(legendre, leg_v, sem, s, slot, start):
    return pltpu.make_async_copy(
        legendre.at[s, :, pl.ds(start, WINDOW), :], leg_v.at[slot], sem.at[slot]
    )


def by_part(vectors):
    shape = (4 * vectors, 4 * vectors)
    i = lax.broadcasted_iota(jnp.int32, shape, 0)
    j = lax.broadcasted_iota(jnp.int32, shape, 1)
    return (j == (i % vectors) * 4 + i // vectors).astype(BF16)


def synthesize_kernel(
    counts, trial, legendre, fields, sent1, sent2, sent3, where,
    counts_v, tr_v, leg_v, one, two, prod, sem_c, sem_t, sem_l, sem_o,
):
    count_copy = pltpu.make_async_copy(counts, counts_v, sem_c.at[0])
    count_copy.start()
    vectors, orders = trial.shape[:2]
    me = lax.axis_index("vert")
    pair = orders // 4

    def send_copies():
        for d, out in enumerate((sent1, sent2, sent3)):
            yield pltpu.make_async_copy(
                tr_v.at[pl.ds((me + d + 1) % 4 * pair, pair)], out, sem_o.at[d]
            )

    for s in range(orders):
        pltpu.make_async_copy(trial.at[:, s], tr_v.at[s], sem_t.at[s]).start()
    count_copy.wait()
    live = counts_v[...] > 0
    cycle = lax.broadcasted_iota(jnp.int32, live.shape, 0) * live.shape[1]
    cycle = cycle + lax.broadcasted_iota(jnp.int32, live.shape, 1)
    last = legendre.shape[2] - fields.shape[0]
    first = jnp.min(jnp.where(live, cycle, last).astype(F32)).astype(jnp.int32)
    start = jnp.minimum((first // 16) * 16, legendre.shape[2] - WINDOW)
    start = pl.multiple_of(start, 16)
    shift = first - start
    where[0] = start
    where[1] = shift
    for s in range(orders):
        window_copy(legendre, leg_v, sem_l, s, s, start).start()
    for s in range(orders):
        pltpu.make_async_copy(trial.at[:, s], tr_v.at[s], sem_t.at[s]).wait()
        x = tr_v[s].reshape(4 * vectors, tr_v.shape[3])
        window_copy(legendre, leg_v, sem_l, s, s, start).wait()
        slot = s % 2
        one[slot, :, :WINDOW] = dot(x, leg_v[s, 0], NT)
        two[slot, :, :WINDOW] = dot(x, leg_v[s, 1], NT)
        w, x = (
            [ref[slot, pl.ds(c, vectors, stride=4), :] for c in range(4)]
            for ref in (one, two)
        )
        f = jnp.concatenate([w[0] + x[3], w[1] - x[2], -x[0] - w[3], x[1] - w[2]], axis=0)
        prod[s * WINDOW : (s + 1) * WINDOW] = f.T[:WINDOW]
        if s == orders - 1:
            for copy in send_copies():
                copy.start()
    for r in range(fields.shape[0]):
        fields[r] = prod[pl.ds(shift + r, orders, stride=WINDOW), :].astype(BF16)
    for copy in send_copies():
        copy.wait()


def synthesize(counts, trial, legendre, cycles):
    vectors, orders, _, degrees = trial.shape
    columns = 4 * vectors
    hbm = pl.BlockSpec(memory_space=pltpu.HBM)
    vmem = pl.BlockSpec(memory_space=pltpu.VMEM)
    sent = pltpu.HBM((orders // 4, vectors, 4, degrees), BF16)
    return pl.pallas_call(
        synthesize_kernel,
        out_shape=(
            jax.ShapeDtypeStruct((cycles, orders, columns), BF16),
            sent,
            sent,
            sent,
            jax.ShapeDtypeStruct((2,), jnp.int32),
        ),
        in_specs=[hbm, hbm, hbm],
        out_specs=(vmem, hbm, hbm, hbm, pl.BlockSpec(memory_space=pltpu.SMEM)),
        scratch_shapes=[
            pltpu.VMEM(counts.shape, jnp.int32),
            pltpu.VMEM((orders, vectors, 4, degrees), BF16),
            pltpu.VMEM((orders, 2, WINDOW, degrees), BF16),
            pltpu.VMEM((2, columns, 128), F32),
            pltpu.VMEM((2, columns, 128), F32),
            pltpu.VMEM((orders * WINDOW, columns), F32),
            pltpu.SemaphoreType.DMA((1,)),
            pltpu.SemaphoreType.DMA((orders,)),
            pltpu.SemaphoreType.DMA((orders,)),
            pltpu.SemaphoreType.DMA((3,)),
        ],
        compiler_params=pltpu.CompilerParams(vmem_limit_bytes=40 << 20),
        cost_estimate=pl.CostEstimate(
            flops=600_000_000, bytes_accessed=5 << 20, transcendentals=0
        ),
        name="synthesize",
    )(in_hbm(counts), in_hbm(trial), in_hbm(legendre))


def arrange_kernel(trial, tt, tr_v, tt_v, sem_t, sem_o):
    vectors, orders = trial.shape[:2]
    for s in range(orders):
        pltpu.make_async_copy(trial.at[:, s], tr_v.at[s], sem_t.at[s]).start()
    order = by_part(vectors)
    for s in range(orders):
        pltpu.make_async_copy(trial.at[:, s], tr_v.at[s], sem_t.at[s]).wait()
        t = dot(order, tr_v[s].reshape(4 * vectors, tr_v.shape[3])).astype(BF16)
        for c in range(4):
            tt_v[s, c] = t[c * vectors : (c + 1) * vectors]
        pltpu.make_async_copy(tt_v.at[s], tt.at[s], sem_o.at[s]).start()
    for s in range(orders):
        pltpu.make_async_copy(tt_v.at[s], tt.at[s], sem_o.at[s]).wait()


def arrange(trial):
    vectors, orders, _, degrees = trial.shape
    hbm = pl.BlockSpec(memory_space=pltpu.HBM)
    return pl.pallas_call(
        arrange_kernel,
        out_shape=pltpu.HBM((orders, 4, vectors, degrees), BF16),
        in_specs=[hbm],
        out_specs=hbm,
        scratch_shapes=[
            pltpu.VMEM((orders, vectors, 4, degrees), BF16),
            pltpu.VMEM((orders, 4, vectors, degrees), BF16),
            pltpu.SemaphoreType.DMA((orders,)),
            pltpu.SemaphoreType.DMA((orders,)),
        ],
        compiler_params=pltpu.CompilerParams(vmem_limit_bytes=40 << 20),
        cost_estimate=pl.CostEstimate(
            flops=300_000_000, bytes_accessed=4 << 20, transcendentals=0
        ),
        name="arrange",
    )(in_hbm(trial))


def quarter_sine(x):
    y = x * x
    sine = 1.0 + y * (-1 / 6 + y * (1 / 120 + y * (-1 / 5040 + y * (1 / 362880 + y * (-1 / 39916800)))))
    cosine = 1.0 + y * (
        -1 / 2 + y * (1 / 24 + y * (-1 / 720 + y * (1 / 40320 + y * (-1 / 3628800 + y * (1 / 479001600)))))
    )
    return sine * x, cosine


def turn(phase, longitudes):
    quarter = longitudes // 4
    s, c = quarter_sine((phase & (quarter - 1)).astype(F32) * (2.0 * math.pi / longitudes))
    quadrant = phase // quarter
    swapped = (quadrant & 1) == 1
    sine = jnp.where(swapped, c, s)
    cosine = jnp.where(swapped, s, c)
    sine = jnp.where(quadrant >= 2, -sine, sine)
    cosine = jnp.where((quadrant == 1) | (quadrant == 2), -cosine, cosine)
    return sine, cosine


def tables_kernel(slots, cosine, sines):
    orders, longitudes = cosine.shape
    lanes = slots.shape[1]
    scale = 1.0 / math.sqrt(orders)
    near = lax.broadcasted_iota(jnp.int32, (lanes, lanes), 1)
    for g in range(slots.shape[0]):
        m = jnp.broadcast_to(slots[g : g + 1, :].astype(F32), (lanes, lanes)).T
        m = m.astype(jnp.int32)
        span = slice(g * lanes, (g + 1) * lanes)
        step_s, step_c = turn((m * lanes) & (longitudes - 1), longitudes)
        s, c = turn((m * near) & (longitudes - 1), longitudes)
        s, c = s * scale, c * scale
        for b in range(longitudes // lanes):
            cosine[span, b * lanes : (b + 1) * lanes] = c.astype(BF16)
            sines[span, b * lanes : (b + 1) * lanes] = s.astype(BF16)
            s, c = s * step_c + c * step_s, c * step_c - s * step_s


def fourier_tables(slots):
    table = jax.ShapeDtypeStruct((slots.size, 2 * slots.size), BF16)
    return pl.pallas_call(
        tables_kernel,
        out_shape=(table, table),
        compiler_params=pltpu.CompilerParams(vmem_limit_bytes=16 << 20),
        cost_estimate=pl.CostEstimate(
            flops=10_000_000, bytes_accessed=2 << 20, transcendentals=0
        ),
        name="tables",
    )(slots)


def transform_kernel(where, begins, counts, weights, cosine, sines, received, returned):
    longitudes = cosine.shape[1]
    columns = received.shape[1]
    part = columns // 4
    home = (lax.axis_index("ma_0") * 8 + lax.axis_index("ma_1")) * 2 + lax.axis_index("ma_2")
    r = where[0] + where[1] + home
    j = lax.broadcasted_iota(jnp.int32, (1, longitudes), 1)
    inside = ((j - begins[r]) & (longitudes - 1)) < counts[r]
    factor = jnp.where(inside, weights[r], 0.0)

    ft = received[...].astype(F32).T.astype(BF16)
    with_cos = jnp.concatenate([ft[:part], ft[3 * part :]], axis=0)
    with_sin = ft[part : 3 * part]
    grid = dot(with_cos, cosine[...]) + dot(with_sin, sines[...])
    weighted = (grid * factor).astype(BF16)
    colat, azimuth = weighted[:part], weighted[part:]
    none = jnp.zeros_like(colat)
    back = dot(
        cosine[...], jnp.concatenate([colat, none, none, azimuth], axis=0), NT
    ) + dot(sines[...], jnp.concatenate([none, colat, azimuth, none], axis=0), NT)
    returned[...] = back.astype(BF16)


def cycle_transform(where, begins, counts, weights, cosine, sines, received):
    vmem = pl.BlockSpec(memory_space=pltpu.VMEM)
    smem = pl.BlockSpec(memory_space=pltpu.SMEM)
    return pl.pallas_call(
        transform_kernel,
        out_shape=jax.ShapeDtypeStruct(received.shape, BF16),
        in_specs=[smem] * 4 + [vmem] * 3,
        out_specs=vmem,
        compiler_params=pltpu.CompilerParams(vmem_limit_bytes=40 << 20),
        cost_estimate=pl.CostEstimate(
            flops=600_000_000, bytes_accessed=3 << 20, transcendentals=0
        ),
        name="transform",
    )(where, begins, counts, weights, cosine, sines, received)


def trial_gram_kernel(
    trial, block1, block2, block3, own, home1, home2, home3, mine, sem
):
    n, _, _, degrees = trial.shape
    me = lax.axis_index("vert")
    copies = [
        pltpu.make_async_copy(trial.at[:, 2 * me + i], mine.at[i], sem.at[i]) for i in range(2)
    ]
    for copy in copies:
        copy.start()
    order = by_part(n)
    total = 0.0
    for i in range(2):
        copies[i].wait()
        parts = [
            dot(order, b.reshape(4 * n, degrees)).astype(BF16)
            for b in (mine[i], block1[i], block2[i], block3[i])
        ]
        for c in range(4):
            x = jnp.concatenate([p[c * n : (c + 1) * n] for p in parts], axis=0)
            total = total + dot(x, x, NT)
    for d, out in enumerate((own, home1, home2, home3)):
        rows = total[d * n : (d + 1) * n]
        out[...] = jnp.concatenate(
            [rows[:, (d - e) % 4 * n : ((d - e) % 4 + 1) * n] for e in range(4)], axis=1
        )


def trial_gram(trial, received):
    vectors, _, parts, degrees = trial.shape
    vmem = pl.BlockSpec(memory_space=pltpu.VMEM)
    return pl.pallas_call(
        trial_gram_kernel,
        out_shape=[jax.ShapeDtypeStruct((vectors, 4 * vectors), F32)] * 4,
        in_specs=[pl.BlockSpec(memory_space=pltpu.HBM)] + [vmem] * 3,
        scratch_shapes=[
            pltpu.VMEM((2, vectors, parts, degrees), BF16),
            pltpu.SemaphoreType.DMA((2,)),
        ],
        compiler_params=pltpu.CompilerParams(vmem_limit_bytes=32 << 20),
        cost_estimate=pl.CostEstimate(
            flops=600_000_000, bytes_accessed=2 << 20, transcendentals=0
        ),
        name="trial_gram",
    )(in_hbm(trial), *received)


def placed_pair(adj, x, base, shift, sign0, sign1):
    cycles, columns = x.shape
    adj[pl.ds(base + shift, cycles), :] = x * sign0
    adj[pl.ds(base + WINDOW + shift, cycles), :] = pltpu.roll(x, columns // 2, 1) * sign1


def adjoint_signs(columns, vectors):
    lane = lax.broadcasted_iota(jnp.int32, (1, columns), 1) // vectors
    one = jnp.ones((1, columns), F32)
    return jnp.where(lane < 2, one, -one), jnp.where((lane == 0) | (lane == 3), -one, one)


ROWS_OF = {0: 0, 1: 1, 3: 2, 2: 3}


def analyse_own_kernel(
    where, got, legendre, tt, own, gram, leg_v, tt_v, wide, adj, sem_l, sem_t
):
    orders, _, vectors, degrees = tt.shape
    columns = 4 * vectors
    start = pl.multiple_of(where[0], 16)
    shift = where[1]
    for n in range(orders):
        window_copy(legendre, leg_v, sem_l, n, n, start).start()
        pltpu.make_async_copy(tt.at[n], tt_v.at[n], sem_t.at[n]).start()
    wide[...] = got[...].astype(F32)
    adj[...] = jnp.zeros_like(adj)
    sign0, sign1 = adjoint_signs(columns, vectors)
    cycles = got.shape[0] // orders
    total = 0.0
    for n in range(orders):
        x = wide[pl.ds(n, cycles, stride=orders), :]
        base = n % 2 * 2 * WINDOW
        placed_pair(adj, x, base, shift, sign0, sign1)
        a = adj[base : base + 2 * WINDOW].T.astype(BF16)
        window_copy(legendre, leg_v, sem_l, n, n, start).wait()
        rows = dot(a, leg_v[n].reshape(2 * WINDOW, degrees)).astype(BF16)
        pltpu.make_async_copy(tt.at[n], tt_v.at[n], sem_t.at[n]).wait()
        for c in range(4):
            mine = rows[ROWS_OF[c] * vectors : (ROWS_OF[c] + 1) * vectors]
            own[n, c] = mine
            total = total + dot(mine, jnp.concatenate([tt_v[n, c], mine], axis=0), NT)
    gram[...] = total


def analyse_own(where, got, legendre, tt):
    orders, _, vectors, degrees = tt.shape
    rows, columns = got.shape
    vmem = pl.BlockSpec(memory_space=pltpu.VMEM)
    hbm = pl.BlockSpec(memory_space=pltpu.HBM)
    block = jax.ShapeDtypeStruct(tt.shape, BF16)
    return pl.pallas_call(
        analyse_own_kernel,
        out_shape=(
            block,
            jax.ShapeDtypeStruct((vectors, 2 * vectors), F32),
            jax.ShapeDtypeStruct((orders, 2, WINDOW, degrees), BF16),
            block,
        ),
        in_specs=[pl.BlockSpec(memory_space=pltpu.SMEM), vmem, hbm, hbm],
        out_specs=(vmem,) * 4,
        scratch_shapes=[
            pltpu.VMEM((rows, columns), F32),
            pltpu.VMEM((2 * 2 * WINDOW, columns), F32),
            pltpu.SemaphoreType.DMA((orders,)),
            pltpu.SemaphoreType.DMA((orders,)),
        ],
        compiler_params=pltpu.CompilerParams(vmem_limit_bytes=24 << 20),
        cost_estimate=pl.CostEstimate(
            flops=500_000_000, bytes_accessed=5 << 20, transcendentals=0
        ),
        name="analyse_own",
    )(where, got, in_hbm(legendre), in_hbm(tt))


def analyse_kernel(
    where, got1, got2, got3, rows0, rows1, rows2, rows3, own, own_gram, leg_v, tt_v,
    rest, kept, sent, gram, got_v, rows_v, wide, adj, sem_g, sem_r,
):
    orders, _, vectors, degrees = own.shape
    columns = 4 * vectors
    shift = where[1]
    got_copies = [
        pltpu.make_async_copy(got, got_v.at[e], sem_g.at[e])
        for e, got in enumerate((got1, got2, got3))
    ]
    row_copies = [
        pltpu.make_async_copy(rows, rows_v.at[e], sem_r.at[e])
        for e, rows in enumerate((rows0, rows1, rows2, rows3))
    ]
    for copy in got_copies + row_copies:
        copy.start()
    adj[...] = jnp.zeros_like(adj)
    for e, copy in enumerate(got_copies):
        copy.wait()
        wide[e] = got_v[e].astype(F32)
    sign0, sign1 = adjoint_signs(columns, vectors)
    cycles = got1.shape[0] // orders
    total = 0.0
    for n in range(orders):
        for e in range(3):
            x = wide[e, pl.ds(n, cycles, stride=orders), :]
            placed_pair(adj, x, e * 2 * WINDOW, shift, sign0, sign1)
        a = jnp.concatenate(
            [adj[e * 2 * WINDOW : (e + 1) * 2 * WINDOW].T for e in range(3)], axis=0
        ).astype(BF16)
        rows = dot(a, leg_v[n].reshape(2 * WINDOW, degrees)).astype(BF16)
        for c in range(4):
            b = ROWS_OF[c] * vectors
            others = jnp.concatenate(
                [rows[e * columns + b : e * columns + b + vectors] for e in range(3)], axis=0
            )
            rest[n, c] = others
            total = total + dot(
                others, jnp.concatenate([tt_v[n, c], own[n, c]], axis=0), NT
            )
    for copy in row_copies:
        copy.wait()
    gram[:vectors] = (rows_v[0] + rows_v[1]) + (rows_v[2] + rows_v[3])
    gram[vectors:] = jnp.concatenate([own_gram[...], total], axis=0).T
    half = kept.shape[0]
    core = lax.axis_index("ma_2")
    kept[...] = gram[pl.ds(pl.multiple_of(core * half, half), half), :]
    sent[...] = gram[pl.ds(pl.multiple_of((1 - core) * half, half), half), :]


def analyse(where, gots, trial_rows, own, own_gram, leg_v, tt_v):
    orders, _, vectors, degrees = own.shape
    cycles_rows, columns = gots[0].shape
    vmem = pl.BlockSpec(memory_space=pltpu.VMEM)
    hbm = pl.BlockSpec(memory_space=pltpu.HBM)
    return pl.pallas_call(
        analyse_kernel,
        out_shape=(
            jax.ShapeDtypeStruct((orders, 4, 3 * vectors, degrees), BF16),
            *([jax.ShapeDtypeStruct((3 * vectors // 2, columns), F32)] * 2),
        ),
        in_specs=[pl.BlockSpec(memory_space=pltpu.SMEM)] + [hbm] * 7 + [vmem] * 4,
        out_specs=(vmem, vmem, vmem),
        scratch_shapes=[
            pltpu.VMEM((3 * vectors, columns), F32),
            pltpu.VMEM((3, cycles_rows, columns), BF16),
            pltpu.VMEM((4, vectors, columns), F32),
            pltpu.VMEM((3, cycles_rows, columns), F32),
            pltpu.VMEM((3 * 2 * WINDOW, columns), F32),
            pltpu.SemaphoreType.DMA((3,)),
            pltpu.SemaphoreType.DMA((4,)),
        ],
        compiler_params=pltpu.CompilerParams(vmem_limit_bytes=32 << 20),
        cost_estimate=pl.CostEstimate(
            flops=1_500_000_000, bytes_accessed=12 << 20, transcendentals=0
        ),
        name="analyse",
    )(where, *gots, *trial_rows, own, own_gram, leg_v, tt_v)


def eliminate(work, n):
    shape = (PANEL, n)
    sub = lax.broadcasted_iota(jnp.int32, shape, 0)
    for j in range(0, n, PANEL):
        for which in range(work.shape[0]):
            top = work[which, j : j + PANEL, :n]
            value, low, inverse = {}, {}, []
            for m in range(PANEL):
                column = jnp.broadcast_to(top[:, j + m : j + m + 1], shape)
                for i in range(m, PANEL):
                    value[i, m] = jnp.broadcast_to(column[i : i + 1], shape)
            for m in range(PANEL):
                inverse.append(lax.rsqrt(value[m, m]))
                for i in range(m + 1, PANEL):
                    low[i, m] = value[i, m] * inverse[m]
                for i in range(m + 1, PANEL):
                    for k in range(m + 1, i + 1):
                        value[i, k] = value[i, k] - low[i, m] * low[k, m]

            def solved(base):
                rows = []
                for m in range(PANEL):
                    line = jnp.broadcast_to(
                        work[which, j + m : j + m + 1, base : base + n], shape
                    )
                    for k in range(m):
                        line = line - low[m, k] * rows[k]
                    rows.append(line * inverse[m])
                return rows

            left = solved(0) if j + PANEL < n else None
            right = solved(n)
            panel = right[0]
            for m in range(1, PANEL):
                panel = jnp.where(sub == m, right[m], panel)
            work[which, j : j + PANEL, n:] = panel
            for i in range(j + PANEL, n, PANEL):
                block = work[which, i : i + PANEL, :n]
                tail = work[which, i : i + PANEL, n:]
                factor = []
                for m in range(PANEL):
                    column = jnp.broadcast_to(block[:, j + m : j + m + 1], shape)
                    for k in range(m):
                        column = column - low[m, k] * factor[k]
                    factor.append(column * inverse[m])
                for m in range(PANEL):
                    block = block - factor[m] * left[m]
                    tail = tail - factor[m] * right[m]
                work[which, i : i + PANEL, :n] = block
                work[which, i : i + PANEL, n:] = tail


def factors_kernel(
    grams, weights, ritz, gram_v, work, cross, sem
):
    n = cross.shape[0]
    vectors = n // 4
    copies = [
        pltpu.make_async_copy(grams.at[half, group], gram_v.at[half, group], sem.at[half, group])
        for group in range(4)
        for half in range(2)
    ]
    for copy in copies:
        copy.start()
    me = lax.axis_index("vert")
    unit = (
        lax.broadcasted_iota(jnp.int32, (n, n), 0)
        == lax.broadcasted_iota(jnp.int32, (n, n), 1)
    ).astype(F32)
    work[0, :, n:] = unit
    work[1, :, n:] = unit
    for group in range(4):
        copies[2 * group].wait()
        copies[2 * group + 1].wait()
        rows = jnp.concatenate([gram_v[0, group], gram_v[1, group]], axis=0)
        rows = rows * (1.0 / COEFFICIENTS)
        if group:
            rows = pltpu.roll(rows, group * vectors, 1)
        span = pl.ds(group * vectors, vectors)
        work[0, span, :n] = rows[:vectors]
        cross[span, :] = rows[vectors : 2 * vectors]
        work[1, span, :n] = rows[2 * vectors :]
    eliminate(work, n)
    inverse_trial = work[0, :, n:]
    ritz[...] = dot_high(dot_high(inverse_trial, cross[...]), inverse_trial, NT)
    mine = work[1, pl.ds(pl.multiple_of(me * vectors, vectors), vectors), n:]
    mine = pltpu.roll(mine, ((4 - me) & 3) * vectors, 1).astype(BF16)
    i = lax.broadcasted_iota(jnp.int32, (n, vectors), 0)
    repeat = (i // 4 == lax.broadcasted_iota(jnp.int32, (n, vectors), 1)).astype(BF16)
    mine = dot(repeat, mine)
    part = lax.broadcasted_iota(jnp.int32, (n, n), 0) & 3
    weights[...] = jnp.concatenate(
        [jnp.where(part == c, mine, 0.0) for c in range(4)], axis=1
    ).astype(BF16)


def factors(grams):
    _, _, rows, n = grams.shape
    vmem = pl.BlockSpec(memory_space=pltpu.VMEM)
    return pl.pallas_call(
        factors_kernel,
        out_shape=(
            jax.ShapeDtypeStruct((n, 4 * n), BF16),
            jax.ShapeDtypeStruct((n, n), F32),
        ),
        in_specs=[pl.BlockSpec(memory_space=pltpu.HBM)],
        out_specs=(vmem, vmem),
        scratch_shapes=[
            pltpu.VMEM((2, 4, rows, n), F32),
            pltpu.VMEM((2, n, 2 * n), F32),
            pltpu.VMEM((n, n), F32),
            pltpu.SemaphoreType.DMA((2, 4)),
        ],
        compiler_params=pltpu.CompilerParams(vmem_limit_bytes=16 << 20),
        cost_estimate=pl.CostEstimate(
            flops=100_000_000, bytes_accessed=1 << 20, transcendentals=0
        ),
        name="factors",
    )(grams)


def mix_kernel(weights, own, rest, new_basis, out_v, sem):
    orders, parts, vectors, degrees = own.shape
    for s in range(orders):
        every = [piece for c in range(parts) for piece in (own[s, c], rest[s, c])]
        y = dot(weights[...], jnp.concatenate(every, axis=0)).astype(BF16)
        out_v[s] = y.reshape(vectors, 4, degrees)
        pltpu.make_async_copy(out_v.at[s], new_basis.at[:, s], sem.at[s]).start()
    for s in range(orders):
        pltpu.make_async_copy(out_v.at[s], new_basis.at[:, s], sem.at[s]).wait()


def mix(weights, own, rest):
    orders, _, vectors, degrees = own.shape
    vmem = pl.BlockSpec(memory_space=pltpu.VMEM)
    return pl.pallas_call(
        mix_kernel,
        out_shape=pltpu.HBM((vectors, orders, 4, degrees), BF16),
        in_specs=[vmem, vmem, vmem],
        out_specs=pl.BlockSpec(memory_space=pltpu.HBM),
        scratch_shapes=[
            pltpu.VMEM((orders, vectors, 4, degrees), BF16),
            pltpu.SemaphoreType.DMA((orders,)),
        ],
        compiler_params=pltpu.CompilerParams(vmem_limit_bytes=32 << 20),
        cost_estimate=pl.CostEstimate(
            flops=1_100_000_000, bytes_accessed=10 << 20, transcendentals=0
        ),
        name="mix",
    )(weights, own, rest)


def swap(value, axis, size, bit):
    return lax.ppermute(value, axis, [(i, i ^ bit) for i in range(size)])


def sum_of_four(value, axis, size):
    one, two, three = (swap(value, axis, size, bit) for bit in (1, 2, 3))
    return (value + one) + (two + three)


def sum_over_ma(kept, sent):
    value = kept + swap(sent, "ma_2", 2, 1)
    value = sum_of_four(value, "ma_1", 8)
    value = value + swap(value, "ma_1", 8, 4)
    return sum_of_four(value, "ma_0", 4)


def from_groups(value):
    return [value] + [lax.ppermute(value, "vert", ring(4, -d)) for d in (1, 2, 3)]


def shards(trial_block, legendre, order_slot, cycle_start, cycle_count, cycle_weight):
    vectors, orders, _, _ = trial_block.shape
    live = legendre.shape[2] // 4
    columns = 4 * vectors

    fields, *sent, where = synthesize(
        cycle_count.reshape(-1, 128), trial_block, legendre, live
    )
    blocks = [lax.ppermute(x, "vert", ring(4, d)) for d, x in enumerate(sent, 1)]
    received = lax.all_to_all(fields, MA, split_axis=0, concat_axis=0, tiled=True)
    tt = arrange(trial_block)
    cosine, sines = fourier_tables(order_slot.reshape(-1, 128))
    received, tt, cosine, sines = lax.optimization_barrier((received, tt, cosine, sines))
    returned = cycle_transform(
        where, cycle_start, cycle_count, cycle_weight, cosine, sines,
        received.reshape(live * orders, columns),
    )
    order_fields = lax.all_to_all(
        returned.reshape(live, orders, columns), MA, split_axis=0, concat_axis=0, tiled=True
    )
    shares = trial_gram(trial_block, blocks)
    trial_rows = [shares[0]] + [
        lax.ppermute(shares[d], "vert", ring(4, -d)) for d in (1, 2, 3)
    ]
    order_fields, *trial_rows = lax.optimization_barrier((order_fields, *trial_rows))
    gots = from_groups(order_fields.reshape(live * orders, columns))
    own, *of_own = analyse_own(where, gots[0], legendre, tt)
    rest, kept, sent = analyse(where, gots[1:], trial_rows, own, *of_own)
    summed = jnp.broadcast_to(sum_over_ma(kept, sent)[None], (8, *kept.shape))
    grams = lax.all_to_all(summed, ("ma_2", "vert"), split_axis=0, concat_axis=0, tiled=True)
    weights, ritz_matrix = factors(grams.reshape(2, 4, *kept.shape))
    return (mix(weights, own, rest), ritz_matrix)


def solution(mesh):
    split = Mesh(
        mesh.devices.reshape(4, 8, 2, mesh.shape["vert"]), ("ma_0", "ma_1", "ma_2", "vert")
    )
    placed = (P("vert", MA, None, None), P(MA, None, None, None), P(), P(), P(), P())
    return jax.shard_map(
        shards,
        mesh=split,
        in_specs=placed,
        out_specs=(P("vert", MA, None, None), P()),
        check_vma=False,
    )
```
